32 devices in a mesh: gx: 8 (over z, x), gy: 2 (over y), lvl: 2 (over core).
Axes of the slice: x: 2, y: 2, z: 4, core: 2. Of those that a mesh axis runs over, the one named last changes fastest.
Arguments:
- right_side: float32 [4, 64, 32, 512], P(None, 'gx', 'gy', 'lvl'), may hold values from -6 to 6
- start_field: float32 [4, 64, 32, 512], P(None, 'gx', 'gy', 'lvl'), may hold values from -4 to 4
- mask_blocks: float32 [3072, 1024], P(('gx', 'gy', 'lvl')), may hold values from 0.5 to 20
- block_tile: int32 [3072, 1], replicated, may hold values from 0 to 15; in each aligned block of 96 rows (0 to 95, 96 to 191, ...) at most 12 rows name the same one
- block_slot: int32 [3072], replicated, may hold values from 0 to 31
Outputs:
- solution: float32 [4, 64, 32, 512], P(None, 'gx', 'gy', 'lvl')
The draws below stay inside these ranges and needn't reach their ends.
Inputs may be any that keep to these rules, and one draw needn't show every extreme that they name: `block_tile`: rows s * 96 to (s + 1) * 96 - 1 are the blocks of the device at position s of the joined gx, gy, lvl order; in each such block of rows no tile is named by more than 12 rows, a bound that some block reaches. `block_slot`: several blocks may name the same slot of a tile; their coefficients add.
All inputs are finite; a program needn't handle non-finite values.
Results may differ from the reference program's by a relative error of at most 0.00002.
Values sent between devices are 32-bit elements; how exact they have to be, the bound alone decides.
No kernel may reach another device: no remote copies, remote signals or barrier semaphores. Data moves between devices by JAX's collectives and lax.ppermute only.
A program may use at most 128 MiB of HBM per device.

```python
import math
import jax
import jax.numpy as jnp
import numpy as np

CX = 8
CY = 16
CZ = 256
NB = 96
SMOOTH_SWEEPS = 2
COARSE_SWEEPS = 4
TILES = 16
CAP = 12
SLOTS = 32
BLK = 1024
NX = 64
NY = 32
NZ = 512
N_GX = 8
N_GY = 2
N_LVL = 2
DEVICES = 32


def touch_ends(result, own_key, low, high):
    spot = [jax.random.randint(jax.random.fold_in(own_key, axis), (), 0, length) for axis, length in enumerate(result.shape)]
    widest = result.shape.index(max(result.shape))
    beside = spot[:widest] + [(spot[widest] + 1) % result.shape[widest]] + spot[widest + 1:]
    return result.at[tuple(spot)].set(low).at[tuple(beside)].set(high)


def levels(own_key, dims, cuts, least, high):
    gain = 1.0
    for dim, parts in cuts:
        steps = jax.random.uniform(jax.random.fold_in(jax.random.fold_in(own_key, 6), dim), (parts,), jnp.float32, least / len(cuts), high / len(cuts))
        gain = gain * jnp.repeat(jnp.exp(steps), dims[dim] // parts).reshape((-1,) + (1,) * (len(dims) - 1 - dim))
    return gain


def shared_out(key, own, number, rows, count, top, most, skew):
    ranking = jax.random.permutation(key, count)
    crowded, usual = portions_of(count, rows * top, most, skew, True), portions_of(count, rows * top, most, skew, False)
    places = jnp.arange(count)

    def named(lengths, offset_by):
        used = int((lengths > 0).sum())
        fixed = max(1, used // 4)
        passed = fixed + (places - fixed + offset_by * (used - fixed)) % max(1, count - fixed)
        return jnp.zeros((count,), jnp.int32).at[ranking[jnp.where(places < fixed, places, passed)]].set(jnp.asarray(lengths, jnp.int32))

    lengths = jnp.where(number % 4 == 0, named(crowded, number // 4), named(usual, number - number // 4 - 1))
    mixed = jax.random.permutation(jax.random.fold_in(own, 3), count)
    giver, sink = mixed[0:count // 2 * 2:2], mixed[1:count // 2 * 2:2]
    margin = jnp.minimum(lengths[giver] - 1, most - lengths[sink]) // 2
    margin = jnp.where((giver == ranking[0]) | (sink == ranking[0]) | (lengths[sink] == 0), 0, jnp.maximum(margin, 0))
    passed = jax.random.randint(jax.random.fold_in(own, 4), (count // 2,), 0, 1 << 20) % (margin + 1)
    lengths = lengths.at[giver].add(-passed).at[sink].add(passed)
    labels = jnp.searchsorted(jnp.cumsum(lengths), jnp.arange(rows * top), side="right").astype(jnp.int32)
    grid = labels.reshape(top, rows).T
    grid = grid[jax.random.permutation(jax.random.fold_in(own, 1), rows)]
    offset_by = jax.random.randint(jax.random.fold_in(own, 2), (rows, 1), 0, top)
    return jnp.take_along_axis(grid, (jnp.arange(top)[None, :] + offset_by) % top, axis=1)


def portions_of(amount, total, limit, slope, full):
    loads = [(1 << 20) // math.isqrt(rank ** slope) + 1 for rank in range(1, amount + 1)]
    largest = limit if full else min(limit, max(-(-total // amount), total * loads[0] // sum(loads)))
    least = 1 if total - largest >= amount - 1 else 0
    given, surplus = [largest] + [least] * (amount - 1), total - largest - least * (amount - 1)
    while surplus > 0:
        free = [i for i in range(1, amount) if given[i] < largest] or [i for i in range(1, amount) if given[i] < limit]
        whole, remaining = sum([loads[i] for i in free]), surplus
        for i in free:
            more = min(limit - given[i], max(1, remaining * loads[i] // whole), surplus)
            given[i] = given[i] + more
            surplus = surplus - more
    return np.array(given)


def scatter_about(stream_key, dims, scale, bound, shards=(), held_as=jnp.bfloat16):
    level = levels(stream_key, dims, shards, -0.22, 0.18) if shards else 1.0
    values = jax.random.normal(stream_key, dims, jnp.float32) * scale * level
    return jnp.minimum(jnp.maximum(values, -bound), bound).astype(held_as)


def setup_inputs(seed: int = 0) -> dict:
    key_list = jax.random.split(jax.random.key(seed), 6)
    right_side = scatter_about(key_list[0], (4, NX, NY, NZ), 1.0, 6.0, ((1, 8), (2, 2), (3, 2)), jnp.float32)
    start_field = scatter_about(key_list[1], (4, NX, NY, NZ), 0.5, 4.0, ((1, 8), (2, 2), (3, 2)), jnp.float32)
    mask_blocks = jnp.clip(jnp.exp(math.log(20.0) - 3.6888795 * jax.random.uniform(key_list[2], (DEVICES * NB, BLK), jnp.float32) ** levels(key_list[2], (DEVICES * NB, BLK), ((0, 32),), -0.2, 0.2)), 0.5, 20.0)
    block_tile_keys = jax.random.split(jax.random.fold_in(key_list[3], 1), (DEVICES * NB) // NB)
    block_tile_turns = jax.random.permutation(jax.random.fold_in(key_list[3], 3), (DEVICES * NB) // NB)
    block_tile = jax.vmap(lambda own, number: shared_out(jax.random.fold_in(key_list[3], 2), own, number, NB, TILES, 1, CAP, 2))(block_tile_keys, block_tile_turns).reshape((DEVICES * NB, 1))
    block_slot = touch_ends(jax.random.randint(key_list[4], (DEVICES * NB,), 0, SLOTS), jax.random.fold_in(key_list[4], 1), 0, SLOTS - 1).astype(jnp.int32)
    return dict(right_side=right_side, start_field=start_field, mask_blocks=mask_blocks, block_tile=block_tile, block_slot=block_slot)


VEL_SHIFT = 0.05
PRES_SHIFT = 0.05
RELAX = 0.6


def apply_operator(padded, chi, lap_coef, grad_coef):
    center = padded[:, 1:-1, 1:-1, 1:-1]
    x_next = padded[:, 2:, 1:-1, 1:-1]
    x_prev = padded[:, :-2, 1:-1, 1:-1]
    y_next = padded[:, 1:-1, 2:, 1:-1]
    y_prev = padded[:, 1:-1, :-2, 1:-1]
    z_next = padded[:, 1:-1, 1:-1, 2:]
    z_prev = padded[:, 1:-1, 1:-1, :-2]
    laplace = 6.0 * center - (x_next + x_prev + y_next + y_prev + z_next + z_prev)
    gradients = [x_next[3] - x_prev[3], y_next[3] - y_prev[3], z_next[3] - z_prev[3]]
    rows = [(VEL_SHIFT + chi) * center[k] + lap_coef * laplace[k] + grad_coef * gradients[k] for k in range(3)]
    spread = (x_next[0] - x_prev[0]) + (y_next[1] - y_prev[1]) + (z_next[2] - z_prev[2])
    rows.append(PRES_SHIFT * center[3] + lap_coef * laplace[3] + grad_coef * spread)
    return jnp.stack(rows)


def diagonal_of(chi, lap_coef):
    velocity = VEL_SHIFT + chi + 6.0 * lap_coef
    pressure = jnp.zeros_like(chi) + (PRES_SHIFT + 6.0 * lap_coef)
    return jnp.stack([velocity, velocity, velocity, pressure])


def restrict(values):
    lead, size_x, size_y, size_z = values.shape
    shaped = values.reshape(lead, size_x // 2, 2, size_y // 2, 2, size_z // 2, 2)
    return jnp.mean(shaped, axis=(2, 4, 6))


def prolong(values):
    return jnp.repeat(jnp.repeat(jnp.repeat(values, 2, axis=1), 2, axis=2), 2, axis=3)


def zero_pad(values):
    return jnp.pad(values, ((0, 0), (1, 1), (1, 1), (1, 1)))


def reference(right_side, start_field, mask_blocks, block_tile, block_slot):
    rows = mask_blocks.shape[0]
    source = jnp.arange(rows, dtype=jnp.int32) // NB
    half = source % N_LVL
    key = (half * TILES + block_tile[:, 0].astype(jnp.int32)) * SLOTS + block_slot.astype(jnp.int32)
    summed = jax.ops.segment_sum(mask_blocks, key, num_segments=N_LVL * TILES * SLOTS)
    shaped = summed.reshape(N_LVL, N_GX, N_GY, CX // 2, CY // 2, 2, 2, CZ)
    chi = shaped.transpose(1, 3, 5, 2, 4, 6, 0, 7).reshape(NX, NY, NZ)
    diag = diagonal_of(chi, 1.0)
    state = start_field
    for sweep in range(SMOOTH_SWEEPS):
        state = state + RELAX * (right_side - apply_operator(zero_pad(state), chi, 1.0, 0.5)) / diag
    residual = right_side - apply_operator(zero_pad(state), chi, 1.0, 0.5)
    coarse_source = restrict(residual)
    coarse_chi = restrict(chi[None])[0]
    coarse_diag = diagonal_of(coarse_chi, 0.25)
    correction = RELAX * coarse_source / coarse_diag
    for sweep in range(COARSE_SWEEPS - 1):
        update = coarse_source - apply_operator(zero_pad(correction), coarse_chi, 0.25, 0.25)
        correction = correction + RELAX * update / coarse_diag
    state = state + prolong(correction)
    for sweep in range(SMOOTH_SWEEPS):
        state = state + RELAX * (right_side - apply_operator(zero_pad(state), chi, 1.0, 0.5)) / diag
    return state
```

```python
import functools

import jax
import jax.numpy as jnp
from jax import lax
from jax.experimental import pallas as pl
from jax.experimental.pallas import tpu as pltpu
from jax.sharding import PartitionSpec as P

COARSE_SWEEPS = 4
SHIFT = 0.05
RELAX = 0.6
KEEP = 1.0 - RELAX
LANES = 128
FIRST_W = 2
FINE_W = 3
COARSE_W = 4
HIGHEST = lax.Precision.HIGHEST
VMEM = pl.BlockSpec(memory_space=pltpu.VMEM)
SMEM = pl.BlockSpec(memory_space=pltpu.SMEM)
PARAMS = pltpu.CompilerParams(vmem_limit_bytes=48 << 20)


def pairs(count, first):
    return [p for i in range(first, count - 1, 2) for p in ((i, i + 1), (i + 1, i))]


def cut(values, dim, width, to_next):
    size = values.shape[dim]
    if size == width:
        return values
    start = jnp.where(to_next, size - width, 0)
    return lax.dynamic_slice_in_dim(values, start, width, axis=dim)


def swap(axis, values, dim, width):
    count = lax.axis_size(axis)
    even = lax.axis_index(axis) % 2 == 0
    got = [lax.ppermute(cut(values, dim, width, even), axis, pairs(count, 0))]
    if count > 2:
        got.append(lax.ppermute(cut(values, dim, width, ~even), axis, pairs(count, 1)))
    return got


def halo(values, width):
    xs = swap("gx", values, 1, width)
    values = jnp.concatenate([values, *xs], axis=1)
    ys = swap("gy", values, 2, width)
    values = jnp.concatenate([values, *ys], axis=2)
    zs = swap("lvl", values, 3, LANES)
    return xs, ys, zs


def place_halo(dst, margin, own, xs, ys, zs, flags, width):
    fields, planes, rows, lanes = own.shape
    total = dst.shape[2]
    even_x, even_y, even_z = flags[0] == 1, flags[1] == 1, flags[2] == 1
    near = (lax.broadcasted_iota(jnp.int32, (1, LANES), 1) < LANES // 2) == even_z
    gap = total - rows - 2 * width

    def field(f, _):
        for k in range(planes + len(xs) * width):
            if k < planes:
                at, source, j = margin + k, own, k
            else:
                which, j = divmod(k - planes, width)
                up, down = margin + planes + j, margin - width + j
                at = jnp.where(even_x, up, down) if which == 0 else jnp.where(even_x, down, up)
                source = xs[which]
            dst[f, at, 0:rows, 0:lanes] = source[f, j]
            zv = jnp.where(near, zs[0][f, k], 0.0 if len(zs) == 1 else zs[1][f, k])
            dst[f, at, 0:rows, lanes:] = zv[0:rows]
            for src, z_at, to in ((0, 0, slice(0, lanes)), (1, 0, slice(lanes, lanes + LANES))):
                if src == 0:
                    first = ys[0][f, k]
                    second = ys[1][f, k] if len(ys) > 1 else jnp.zeros_like(first)
                else:
                    first = zv[rows:rows + width]
                    second = zv[rows + width:rows + 2 * width] if len(ys) > 1 else jnp.zeros_like(first)
                dst[f, at, rows:rows + width, to] = jnp.where(even_y, first, second)
                dst[f, at, total - width:total, to] = jnp.where(even_y, second, first)
            if gap:
                dst[f, at, rows + width:total - width, :] = jnp.zeros((gap, dst.shape[3]), jnp.float32)
        return 0

    lax.fori_loop(0, fields, field, 0)


def inside(flags, rows, lanes, total, depth):
    row = lax.broadcasted_iota(jnp.int32, (total, lanes + LANES), 0)
    lane = lax.broadcasted_iota(jnp.int32, (total, lanes + LANES), 1)
    end = lanes + LANES
    row_ok = (row < rows) | ((row < rows + depth) & (flags[5] == 1)) | ((row >= total - depth) & (flags[6] == 1))
    lane_ok = (lane < lanes) | ((lane < lanes + depth) & (flags[7] == 1)) | ((lane >= end - depth) & (flags[8] == 1))
    return jnp.where(row_ok & lane_ok, 1.0, 0.0)


def plane_inside(flags, p, margin, planes):
    return jnp.where(p < margin, flags[4], jnp.where(p >= margin + planes, flags[3], 1)).astype(jnp.float32)


def neighbours(ref, p):
    rows, lanes = ref.shape[2], ref.shape[3]
    sums, grads, spread = [], [], 0.0
    for f in range(4):
        c, xn, xp = ref[f, p], ref[f, p + 1], ref[f, p - 1]
        yn, yp = pltpu.roll(c, rows - 1, 0), pltpu.roll(c, 1, 0)
        zn, zp = pltpu.roll(c, lanes - 1, 1), pltpu.roll(c, 1, 1)
        sums.append((xn + xp) + (yn + yp) + (zn + zp))
        if f == 3:
            grads = [xn - xp, yn - yp, zn - zp]
        else:
            spread = spread + (xn - xp, yn - yp, zn - zp)[f]
    return sums, grads + [spread]


def pack_kernel(tile_ref, mask_ref, out_ref, used_ref, *, capacity):
    tiles = out_ref.shape[0]
    count = mask_ref.shape[0]
    out_ref[...] = jnp.zeros(out_ref.shape, jnp.float32)

    def clear(t, _):
        used_ref[t] = 0
        return 0

    lax.fori_loop(0, tiles, clear, 0)

    def row(r, _):
        t = tile_ref[r]
        n = used_ref[t]
        used_ref[t] = n + 1
        out_ref[t, jnp.minimum(n, capacity - 1)] = mask_ref[r]
        return 0

    lax.fori_loop(0, count, row, 0)


def first_kernel(flags, rhs, start, *refs, nxs, nys, nzs):
    halos, (rhs_out, part_out, both) = refs[:nxs + nys + nzs], refs[nxs + nys + nzs:]
    xs, ys, zs = halos[:nxs], halos[nxs:nxs + nys], halos[nxs + nys:]
    half = lambda refs_, lo: [r.at[lo:lo + 4] for r in refs_]
    planes, rows, lanes = rhs.shape[1:]
    place_halo(rhs_out, FIRST_W, rhs, half(xs, 0), half(ys, 0), half(zs, 0), flags, FIRST_W)
    place_halo(both, FIRST_W, start, half(xs, 4), half(ys, 4), half(zs, 4), flags, FIRST_W)

    def plane(k, _):
        p = k + FIRST_W
        sums, grads = neighbours(both, p)
        for f in range(4):
            part = rhs_out[f, p] + sums[f] - 0.5 * grads[f]
            part_out[f, k] = part[0:rows, 0:lanes]
        return 0

    lax.fori_loop(0, planes, plane, 0)


def chi_kernel(slot_ref, rows_ref, start, part, out, coarse_out, acc, pooled):
    planes, rows, lanes = start.shape[1:]
    acc[...] = jnp.zeros(acc.shape, jnp.float32)
    per = rows_ref.shape[1]

    def add(s, _):
        for c in range(per):
            at = pl.ds(pl.multiple_of(slot_ref[s * per + c] * 8, 8), 8)
            acc[at, :] = acc[at, :] + rows_ref[s, c]
        return 0

    lax.fori_loop(0, rows_ref.shape[0], add, 0)
    z_tiles = lanes // LANES
    across = rows // 2
    for qx in range(planes // 2):
        for zt in range(z_tiles):
            total = None
            for i in range(2):
                for j in range(2):
                    v = acc[pl.ds(qx * across * 8 + (2 * i + j) * z_tiles + zt, across, stride=8), :]
                    pooled[zt, pl.ds(j, across, stride=2), :] = v
                    total = v if total is None else total + v
                out[4, 2 * qx + i, :, zt * LANES:(zt + 1) * LANES] = pooled[zt]
            coarse_out[qx, :, zt * LANES:(zt + 1) * LANES] = total
    for f in range(4):
        for p in range(planes):
            weight = RELAX / (SHIFT + 6.0 + out[4, p]) if f < 3 else RELAX / (SHIFT + 6.0)
            out[f, p] = KEEP * start[f, p] + weight * part[f, p]


def second_kernel(flags, own, pooled_chi, rhs, *refs, nxs, nys, nzs):
    halos, (state_out, weight_out, coarse_out, ext, tmp, pooled) = refs[:nxs + nys + nzs], refs[nxs + nys + nzs:]
    xs, ys, zs = halos[:nxs], halos[nxs:nxs + nys], halos[nxs + nys:]
    planes, rows, lanes = own.shape[1:]
    total = ext.shape[2]
    place_halo(ext, FINE_W, own, xs, ys, zs, flags, FINE_W)
    mask = inside(flags, rows, lanes, total, 2)
    w_p = (RELAX / (SHIFT + 6.0)) * mask

    def sweep(k, _):
        p = k + FINE_W - 2
        here = plane_inside(flags, k, 2, planes)
        sums, grads = neighbours(ext, p)
        w_u = (RELAX / (SHIFT + 6.0 + ext[4, p])) * (mask * here)
        weight_out[k] = w_u
        for f in range(4):
            w = w_u if f < 3 else w_p * here
            state_out[f, k] = KEEP * ext[f, p] + w * (rhs[f, k] + sums[f] - 0.5 * grads[f])
        return 0

    lax.fori_loop(0, planes + 4, sweep, 0)

    def pool(cx, _):
        both = [None] * 4
        for i in range(2):
            k = 2 + 2 * cx + i
            sums, grads = neighbours(state_out, k)
            for f in range(4):
                diag = SHIFT + 6.0 + (ext[4, k + FINE_W - 2] if f < 3 else 0.0)
                r = rhs[f, k] + sums[f] - 0.5 * grads[f] - diag * state_out[f, k]
                both[f] = r if i == 0 else both[f] + r
        for f in range(4):
            for zt in range(lanes // LANES):
                tmp[f, zt] = both[f][0:rows, zt * LANES:(zt + 1) * LANES]
                v = tmp[f, zt, pl.ds(0, rows // 2, stride=2), :] + tmp[f, zt, pl.ds(1, rows // 2, stride=2), :]
                pooled[f, cx, :, zt * LANES:(zt + 1) * LANES] = v
        return 0

    lax.fori_loop(0, planes // 2, pool, 0)
    pooled[4] = pooled_chi[...]
    lane = lax.broadcasted_iota(jnp.int32, (lanes, lanes // 2), 0)
    cell = lax.broadcasted_iota(jnp.int32, (lanes, lanes // 2), 1)
    gather = jnp.where(lane // 2 == cell, 0.125, 0.0)
    flat = pooled[...].reshape(5 * planes // 2 * rows // 2, lanes)
    coarse = jnp.dot(flat, gather, precision=HIGHEST, preferred_element_type=jnp.float32)
    coarse_out[...] = coarse.reshape(coarse_out.shape)


def last_kernel(flags, own, state, weight, rhs, *refs, nxs, nys, nzs):
    halos = refs[:nxs + nys + nzs]
    out, ext, one, two, fine, mid, tmp = refs[nxs + nys + nzs:]
    xs, ys, zs = halos[:nxs], halos[nxs:nxs + nys], halos[nxs + nys:]
    planes, rows, lanes = own.shape[1:]
    total, wide = ext.shape[2], ext.shape[3]
    place_halo(ext, COARSE_W, own, xs, ys, zs, flags, COARSE_W)
    mask = inside(flags, rows, lanes, total, COARSE_W)
    w_p = (RELAX / (SHIFT + 1.5)) * mask

    def begin(p, _):
        here = plane_inside(flags, p, COARSE_W, planes)
        w_u = (RELAX / (SHIFT + 1.5 + ext[4, p])) * (mask * here)
        ext[4, p] = w_u
        for f in range(4):
            one[f, p] = (w_u if f < 3 else w_p * here) * ext[f, p]
        return 0

    lax.fori_loop(0, planes + 2 * COARSE_W, begin, 0)
    now, then = one, two
    for s in range(1, COARSE_SWEEPS):
        def sweep(k, _, now=now, then=then, s=s):
            p = k + s
            here = plane_inside(flags, p, COARSE_W, planes)
            sums, grads = neighbours(now, p)
            for f in range(4):
                w = ext[4, p] if f < 3 else w_p * here
                then[f, p] = KEEP * now[f, p] + w * (ext[f, p] + 0.25 * (sums[f] - grads[f]))
            return 0

        lax.fori_loop(0, planes + 2 * COARSE_W - 2 * s, sweep, 0)
        now, then = then, now

    f_total, f_wide = fine.shape[2], fine.shape[3]
    f_rows, f_lanes = 2 * rows, 2 * lanes
    cell = lax.broadcasted_iota(jnp.int32, (wide, f_wide), 0)
    lane = lax.broadcasted_iota(jnp.int32, (wide, f_wide), 1)
    from_cell = jnp.where(lane < f_lanes + LANES // 2, lane // 2, wide - 1 - (f_wide - 1 - lane) // 2)
    spread = jnp.where(cell == from_cell, 1.0, 0.0)
    c_planes = planes + 2
    flat = now[:, COARSE_W - 1:COARSE_W - 1 + c_planes].reshape(4 * c_planes * total, wide)
    grown = jnp.dot(flat, spread, precision=HIGHEST, preferred_element_type=jnp.float32)
    for f in range(4):
        for cp in range(c_planes):
            lo = (f * c_planes + cp) * total
            for zt in range(f_wide // LANES):
                v = grown[lo:lo + total, zt * LANES:(zt + 1) * LANES]
                at = f * c_planes + cp
                for j in range(2):
                    tmp[zt, pl.ds(j, rows, stride=2), :] = v[0:rows]
                    tmp[zt, pl.ds(f_rows + j, 2, stride=2), :] = v[rows:rows + 2]
                    tmp[zt, pl.ds(f_total - 4 + j, 2, stride=2), :] = v[total - 2:total]
                for i in range(2):
                    to = slice(zt * LANES, (zt + 1) * LANES)
                    fine[f, 2 * cp + i, :, to] = state[f, 2 * cp + i, :, to] + tmp[zt]
    f_planes = 2 * planes
    f_mask = inside(flags, f_rows, f_lanes, f_total, 2)
    w_q = (RELAX / (SHIFT + 6.0)) * f_mask

    def post(k, _):
        p = k + 1
        here = plane_inside(flags, p, 2, f_planes)
        sums, grads = neighbours(fine, p)
        for f in range(4):
            w = weight[p] if f < 3 else w_q * here
            mid[f, p] = KEEP * fine[f, p] + w * (rhs[f, p] + sums[f] - 0.5 * grads[f])
        return 0

    lax.fori_loop(0, f_planes + 2, post, 0)

    def final(k, _):
        p = k + 2
        sums, grads = neighbours(mid, p)
        for f in range(4):
            w = weight[p] if f < 3 else w_q
            v = KEEP * mid[f, p] + w * (rhs[f, p] + sums[f] - 0.5 * grads[f])
            out[f, k] = v[0:f_rows, 0:f_lanes]
        return 0

    lax.fori_loop(0, f_planes, final, 0)


def call(kernel, shapes, scratch, *args, smem=1):
    outs = [jax.ShapeDtypeStruct(s, jnp.float32) for s in shapes]
    return pl.pallas_call(
        kernel,
        out_shape=outs,
        in_specs=[SMEM] * smem + [VMEM] * (len(args) - smem),
        out_specs=[VMEM] * len(outs),
        scratch_shapes=scratch,
        compiler_params=PARAMS,
    )(*args)


def routes(block_tile, block_slot, tiles, count_l, per_device, capacity, slots):
    my_tile = lax.axis_index("gx") * lax.axis_size("gy") + lax.axis_index("gy")
    index_l = lax.axis_index("lvl")
    their_tiles = lax.dynamic_index_in_dim(block_tile.reshape(tiles, count_l, per_device), index_l, 1, keepdims=False)
    their_slots = lax.dynamic_index_in_dim(block_slot.reshape(tiles, count_l, per_device), index_l, 1, keepdims=False)
    arriving = their_tiles == my_tile
    counter = jnp.arange(per_device, dtype=jnp.int32)
    earlier = counter[None, :, None] < counter[None, None, :]
    order = jnp.sum(jnp.where(arriving[:, :, None] & earlier, 1, 0), axis=1)
    places = jnp.arange(capacity, dtype=jnp.int32)
    hit = arriving[:, None, :] & (order[:, None, :] == places[None, :, None])
    slot = jnp.sum(jnp.where(hit, their_slots[:, None, :] - slots, 0), axis=2) + slots
    return slot.reshape(-1)


def body(right_side, start_field, mask_blocks, block_tile, block_slot):
    axes = ("gx", "gy", "lvl")
    counts = [lax.axis_size(a) for a in axes]
    index = [lax.axis_index(a) for a in axes]
    tiles = counts[0] * counts[1]
    per_device, width = mask_blocks.shape
    capacity = max(2, 2 * per_device // tiles)
    _, planes, rows, lanes = right_side.shape
    slots = planes // 2 * (rows // 2)
    c_planes, c_rows, c_lanes = planes // 2, rows // 2, lanes // 2
    flags = [i % 2 == 0 for i in index]
    for i, n in zip(index, counts):
        flags += [i < n - 1, i > 0]
    flags = jnp.stack(flags).astype(jnp.int32)

    my_flat = (index[0] * counts[1] + index[1]) * counts[2] + index[2]
    tile_ids = block_tile[:, 0]
    my_tiles = lax.dynamic_slice_in_dim(tile_ids, my_flat * per_device, per_device)
    (outgoing,) = call(
        functools.partial(pack_kernel, capacity=capacity),
        [(tiles, capacity, width // LANES, LANES)],
        [pltpu.SMEM((tiles,), jnp.int32)],
        my_tiles, mask_blocks.reshape(per_device, width // LANES, LANES),
    )
    arrived = lax.all_to_all(outgoing, ("gx", "gy"), split_axis=0, concat_axis=0, tiled=True)
    slot_of = routes(tile_ids, block_slot, tiles, counts[2], per_device, capacity, slots)

    fields = jnp.concatenate([right_side, start_field], axis=0)
    xs, ys, zs = halo(fields, FIRST_W)
    num = dict(nxs=len(xs), nys=len(ys), nzs=len(zs))
    total, wide = rows + 8, lanes + LANES
    near = planes + 4
    rhs, part = call(
        functools.partial(first_kernel, **num),
        [(4, near, total, wide), (4, planes, rows, lanes)],
        [pltpu.VMEM((4, near, total, wide), jnp.float32)],
        flags, right_side, start_field, *xs, *ys, *zs,
    )
    state, pooled_chi = call(
        chi_kernel,
        [(5, planes, rows, lanes), (c_planes, c_rows, lanes)],
        [pltpu.VMEM(((slots + 1) * 8, LANES), jnp.float32), pltpu.VMEM((lanes // LANES, rows, LANES), jnp.float32)],
        slot_of, arrived, start_field, part,
    )
    xs, ys, zs = halo(state, FINE_W)
    state, weight, coarse = call(
        functools.partial(second_kernel, **num),
        [(4, near, total, wide), (near, total, wide), (5, c_planes, c_rows, c_lanes)],
        [
            pltpu.VMEM((5, planes + 2 * FINE_W, total, wide), jnp.float32),
            pltpu.VMEM((4, lanes // LANES, rows, LANES), jnp.float32),
            pltpu.VMEM((5, c_planes, c_rows, lanes), jnp.float32),
        ],
        flags, state, pooled_chi, rhs, *xs, *ys, *zs,
    )
    xs, ys, zs = halo(coarse, COARSE_W)
    c_ext = (c_planes + 2 * COARSE_W, c_rows + 8, c_lanes + LANES)
    (out,) = call(
        functools.partial(last_kernel, **num),
        [right_side.shape],
        [
            pltpu.VMEM((5, *c_ext), jnp.float32),
            pltpu.VMEM((4, *c_ext), jnp.float32),
            pltpu.VMEM((4, *c_ext), jnp.float32),
            pltpu.VMEM((4, near, total, wide), jnp.float32),
            pltpu.VMEM((4, near, total, wide), jnp.float32),
            pltpu.VMEM((wide // LANES, total, LANES), jnp.float32),
        ],
        flags, coarse, state, weight, rhs, *xs, *ys, *zs,
    )
    return out


def solution(mesh):
    in_specs = (
        P(None, "gx", "gy", "lvl"),
        P(None, "gx", "gy", "lvl"),
        P(("gx", "gy", "lvl"), None),
        P(),
        P(),
    )
    out_specs = P(None, "gx", "gy", "lvl")
    return jax.shard_map(body, mesh=mesh, in_specs=in_specs, out_specs=out_specs, check_vma=False)
```

```python
import functools

import jax
import jax.numpy as jnp
from jax import lax
from jax.experimental import pallas as pl
from jax.experimental.pallas import tpu as pltpu
from jax.sharding import PartitionSpec as P

COARSE_SWEEPS = 4
SHIFT = 0.05
RELAX = 0.6
KEEP = 1.0 - RELAX
LANES = 128
START_W = 4
FINE_W = 3
STATE_W = 2
COARSE_W = 4
PAD = 4
HIGHEST = lax.Precision.HIGHEST
VMEM = pl.BlockSpec(memory_space=pltpu.VMEM)
SMEM = pl.BlockSpec(memory_space=pltpu.SMEM)
PARAMS = pltpu.CompilerParams(vmem_limit_bytes=48 << 20)


def pairs(count, first):
    return [p for i in range(first, count - 1, 2) for p in ((i, i + 1), (i + 1, i))]


def cut(values, dim, width, to_next):
    size = values.shape[dim]
    if size == width:
        return values
    start = jnp.where(to_next, size - width, 0)
    return lax.dynamic_slice_in_dim(values, start, width, axis=dim)


def flat(parts):
    return jnp.concatenate([p.reshape(-1, *p.shape[-2:]) for p in parts], axis=0)


def swap(axis, message):
    count = lax.axis_size(axis)
    even = lax.axis_index(axis) % 2 == 0
    got = [lax.ppermute(message(even), axis, pairs(count, 0))]
    if count > 2:
        got.append(lax.ppermute(message(~even), axis, pairs(count, 1)))
    return got


def halo(groups, depth):
    xs = swap("gx", lambda up: flat([cut(v, 1, w, up) for v, w in groups]))
    whole, at = [], 0
    for v, w in groups:
        got = [x[at:at + v.shape[0] * w].reshape(v.shape[0], w, *v.shape[2:]) for x in xs]
        whole.append((v, *got))
        at += v.shape[0] * w

    def slabs(dim, width, up):
        return flat([jnp.concatenate([cut(p, dim, width, up) for p in parts], axis=1) for parts in whole])

    ys = swap("gy", lambda up: slabs(2, depth, up))
    rows = groups[0][0].shape[2]

    def last(up):
        sent = [slabs(3, LANES, up)]
        for y in ys:
            edge = cut(y, 2, LANES, up)
            short = -edge.shape[0] % (rows // PAD)
            edge = jnp.pad(edge, ((0, short), (0, PAD - depth), (0, 0)))
            sent.append(edge.reshape(-1, rows, LANES))
        return jnp.concatenate(sent, axis=0)

    return xs, ys, swap("lvl", last)


def place_halo(dst, margin, own, got, flags, width, depth, before=(0, 0), slab_count=None):
    xs, ys, zs = got
    fields, planes, rows, lanes = own.shape
    total = dst.shape[2]
    count = planes + len(xs) * width
    slab_count = slab_count or fields * count
    per = rows // PAD
    even_x, even_y, even_z = flags[0] == 1, flags[1] == 1, flags[2] == 1
    near = (lax.broadcasted_iota(jnp.int32, (1, LANES), 1) < LANES // 2) == even_z
    gap = total - rows - 2 * depth

    def edge(at, row, size):
        part = slice(row, row + size)
        return jnp.where(near, zs[0][at, part], 0.0 if len(zs) == 1 else zs[1][at, part])

    for f in range(fields):
        for k in range(count):
            if k < planes:
                at, plane = margin + k, own[f, k]
            else:
                which, j = divmod(k - planes, width)
                up, down = margin + planes + j, margin - width + j
                at = jnp.where(even_x, up, down) if which == 0 else jnp.where(even_x, down, up)
                plane = xs[which][before[0] + f * width + j]
            slab = before[1] + f * count + k
            dst[f, at, 0:rows, 0:lanes] = plane
            dst[f, at, 0:rows, lanes:] = edge(slab, 0, rows)
            sides = []
            for n, y in enumerate(ys):
                at_z = slab_count + n * (-(-slab_count // per)) + slab // per
                sides.append((y[slab], edge(at_z, slab % per * PAD, depth)))
            if len(sides) == 1:
                sides.append([jnp.zeros_like(v) for v in sides[0]])
            for to, first, second in zip((slice(0, lanes), slice(lanes, lanes + LANES)), *sides):
                dst[f, at, rows:rows + depth, to] = jnp.where(even_y, first, second)
                dst[f, at, total - depth:total, to] = jnp.where(even_y, second, first)
            if gap:
                dst[f, at, rows + depth:total - depth, :] = jnp.zeros((gap, dst.shape[3]), jnp.float32)


def inside(flags, rows, lanes, total, depth):
    row = lax.broadcasted_iota(jnp.int32, (total, lanes + LANES), 0)
    lane = lax.broadcasted_iota(jnp.int32, (total, lanes + LANES), 1)
    end = lanes + LANES
    row_ok = (row < rows) | ((row < rows + depth) & (flags[5] == 1)) | ((row >= total - depth) & (flags[6] == 1))
    lane_ok = (lane < lanes) | ((lane < lanes + depth) & (flags[7] == 1)) | ((lane >= end - depth) & (flags[8] == 1))
    return jnp.where(row_ok & lane_ok, 1.0, 0.0)


def plane_inside(flags, p, margin, planes):
    return jnp.where(p < margin, flags[4], jnp.where(p >= margin + planes, flags[3], 1)).astype(jnp.float32)


def neighbours(ref, p):
    rows, lanes = ref.shape[2], ref.shape[3]
    sums, grads, spread = [], [], 0.0
    for f in range(4):
        c, xn, xp = ref[f, p], ref[f, p + 1], ref[f, p - 1]
        yn, yp = pltpu.roll(c, rows - 1, 0), pltpu.roll(c, 1, 0)
        zn, zp = pltpu.roll(c, lanes - 1, 1), pltpu.roll(c, 1, 1)
        sums.append((xn + xp) + (yn + yp) + (zn + zp))
        if f == 3:
            grads = [xn - xp, yn - yp, zn - zp]
        else:
            spread = spread + (xn - xp, yn - yp, zn - zp)[f]
    return sums, grads + [spread]


def pack_kernel(tile_ref, mask_ref, out_ref, used_ref, *, capacity):
    tiles = out_ref.shape[0]
    count = mask_ref.shape[0]
    out_ref[...] = jnp.zeros(out_ref.shape, jnp.float32)

    def clear(t, _):
        used_ref[t] = 0
        return 0

    lax.fori_loop(0, tiles, clear, 0)

    def row(r, _):
        t = tile_ref[r]
        n = used_ref[t]
        used_ref[t] = n + 1
        out_ref[t, jnp.minimum(n, capacity - 1)] = mask_ref[r]
        return 0

    lax.fori_loop(0, count, row, 0)


def split(refs, nums):
    at, got = 0, []
    for n in nums:
        got.append(refs[at:at + n])
        at += n
    return got, refs[at:]


def first_kernel(flags, rhs, start, *refs, nums):
    got, (rhs_out, start_out, part_out) = split(refs, nums)
    planes = rhs.shape[1]
    many = [4 * (planes + len(got[0]) * w) for w in (START_W, FINE_W)]
    place_halo(start_out, START_W, start, got, flags, START_W, START_W, slab_count=sum(many))
    place_halo(rhs_out, FINE_W, rhs, got, flags, FINE_W, START_W, (4 * START_W, many[0]), sum(many))

    def plane(k, _):
        sums, grads = neighbours(start_out, k + START_W - FINE_W)
        for f in range(4):
            part_out[f, k] = rhs_out[f, k] + sums[f] - 0.5 * grads[f]
        return 0

    lax.fori_loop(0, planes + 2 * FINE_W, plane, 0)


def chi_kernel(slot_ref, rows_ref, out, coarse_out, acc, pooled):
    _, planes, rows, lanes = out.shape
    acc[...] = jnp.zeros(acc.shape, jnp.float32)
    per = rows_ref.shape[1]

    def add(s, _):
        for c in range(per):
            at = pl.ds(pl.multiple_of(slot_ref[s * per + c] * 8, 8), 8)
            acc[at, :] = acc[at, :] + rows_ref[s, c]
        return 0

    lax.fori_loop(0, rows_ref.shape[0], add, 0)
    z_tiles = lanes // LANES
    across = rows // 2
    for qx in range(planes // 2):
        for zt in range(z_tiles):
            total = None
            for i in range(2):
                for j in range(2):
                    v = acc[pl.ds(qx * across * 8 + (2 * i + j) * z_tiles + zt, across, stride=8), :]
                    pooled[zt, pl.ds(j, across, stride=2), :] = v
                    total = v if total is None else total + v
                out[0, 2 * qx + i, :, zt * LANES:(zt + 1) * LANES] = pooled[zt]
            coarse_out[qx, :, zt * LANES:(zt + 1) * LANES] = total


def second_kernel(flags, own, pooled_chi, rhs, start, part, *refs, nums):
    got, (state_out, weight_out, coarse_out, chi, ext, tmp, pooled) = split(refs, nums)
    _, planes, rows, lanes = own.shape
    total = ext.shape[2]
    place_halo(chi, FINE_W, own, got, flags, FINE_W, FINE_W)
    mask = inside(flags, rows, lanes, total, FINE_W)
    w_p = (RELAX / (SHIFT + 6.0)) * mask

    def begin(k, _):
        here = plane_inside(flags, k, FINE_W, planes)
        w_u = (RELAX / (SHIFT + 6.0 + chi[0, k])) * (mask * here)
        weight_out[k] = w_u
        for f in range(4):
            w = w_u if f < 3 else w_p * here
            ext[f, k] = KEEP * start[f, k + START_W - FINE_W] + w * part[f, k]
        return 0

    lax.fori_loop(0, planes + 2 * FINE_W, begin, 0)

    def sweep(k, _):
        p = k + FINE_W - STATE_W
        here = plane_inside(flags, k, STATE_W, planes)
        sums, grads = neighbours(ext, p)
        w_u = weight_out[p]
        for f in range(4):
            w = w_u if f < 3 else w_p * here
            state_out[f, k] = KEEP * ext[f, p] + w * (rhs[f, p] + sums[f] - 0.5 * grads[f])
        return 0

    lax.fori_loop(0, planes + 2 * STATE_W, sweep, 0)

    def pool(cx, _):
        both = [None] * 4
        for i in range(2):
            k = STATE_W + 2 * cx + i
            p = FINE_W + 2 * cx + i
            sums, grads = neighbours(state_out, k)
            for f in range(4):
                diag = SHIFT + 6.0 + (chi[0, p] if f < 3 else 0.0)
                r = rhs[f, p] + sums[f] - 0.5 * grads[f] - diag * state_out[f, k]
                both[f] = r if i == 0 else both[f] + r
        for f in range(4):
            for zt in range(lanes // LANES):
                tmp[f, zt] = both[f][0:rows, zt * LANES:(zt + 1) * LANES]
                v = tmp[f, zt, pl.ds(0, rows // 2, stride=2), :] + tmp[f, zt, pl.ds(1, rows // 2, stride=2), :]
                pooled[f, cx, :, zt * LANES:(zt + 1) * LANES] = v
        return 0

    lax.fori_loop(0, planes // 2, pool, 0)
    pooled[4] = pooled_chi[...]
    lane = lax.broadcasted_iota(jnp.int32, (lanes, lanes // 2), 0)
    cell = lax.broadcasted_iota(jnp.int32, (lanes, lanes // 2), 1)
    gather = jnp.where(lane // 2 == cell, 0.125, 0.0)
    flat_rows = pooled[...].reshape(5 * planes // 2 * rows // 2, lanes)
    coarse = jnp.dot(flat_rows, gather, precision=HIGHEST, preferred_element_type=jnp.float32)
    coarse_out[...] = coarse.reshape(coarse_out.shape)


def last_kernel(flags, own, state, weight, rhs, *refs, nums):
    got, (out, ext, one, two, fine, mid, tmp) = split(refs, nums)
    planes, rows, lanes = own.shape[1:]
    total, wide = ext.shape[2], ext.shape[3]
    place_halo(ext, COARSE_W, own, got, flags, COARSE_W, COARSE_W)
    mask = inside(flags, rows, lanes, total, COARSE_W)
    w_p = (RELAX / (SHIFT + 1.5)) * mask

    def begin(p, _):
        here = plane_inside(flags, p, COARSE_W, planes)
        w_u = (RELAX / (SHIFT + 1.5 + ext[4, p])) * (mask * here)
        ext[4, p] = w_u
        for f in range(4):
            one[f, p] = (w_u if f < 3 else w_p * here) * ext[f, p]
        return 0

    lax.fori_loop(0, planes + 2 * COARSE_W, begin, 0)
    now, then = one, two
    for s in range(1, COARSE_SWEEPS):
        def sweep(k, _, now=now, then=then, s=s):
            p = k + s
            here = plane_inside(flags, p, COARSE_W, planes)
            sums, grads = neighbours(now, p)
            for f in range(4):
                w = ext[4, p] if f < 3 else w_p * here
                then[f, p] = KEEP * now[f, p] + w * (ext[f, p] + 0.25 * (sums[f] - grads[f]))
            return 0

        lax.fori_loop(0, planes + 2 * COARSE_W - 2 * s, sweep, 0)
        now, then = then, now

    f_total, f_wide = fine.shape[2], fine.shape[3]
    f_rows, f_lanes = 2 * rows, 2 * lanes
    cell = lax.broadcasted_iota(jnp.int32, (wide, f_wide), 0)
    lane = lax.broadcasted_iota(jnp.int32, (wide, f_wide), 1)
    from_cell = jnp.where(lane < f_lanes + LANES // 2, lane // 2, wide - 1 - (f_wide - 1 - lane) // 2)
    spread = jnp.where(cell == from_cell, 1.0, 0.0)
    c_planes = planes + 2
    flat = now[:, COARSE_W - 1:COARSE_W - 1 + c_planes].reshape(4 * c_planes * total, wide)
    grown = jnp.dot(flat, spread, precision=HIGHEST, preferred_element_type=jnp.float32)
    for f in range(4):
        for cp in range(c_planes):
            lo = (f * c_planes + cp) * total
            for zt in range(f_wide // LANES):
                v = grown[lo:lo + total, zt * LANES:(zt + 1) * LANES]
                at = f * c_planes + cp
                for j in range(2):
                    tmp[zt, pl.ds(j, rows, stride=2), :] = v[0:rows]
                    tmp[zt, pl.ds(f_rows + j, 2, stride=2), :] = v[rows:rows + 2]
                    tmp[zt, pl.ds(f_total - 4 + j, 2, stride=2), :] = v[total - 2:total]
                for i in range(2):
                    to = slice(zt * LANES, (zt + 1) * LANES)
                    fine[f, 2 * cp + i, :, to] = state[f, 2 * cp + i, :, to] + tmp[zt]
    f_planes = 2 * planes
    f_mask = inside(flags, f_rows, f_lanes, f_total, STATE_W)
    off = FINE_W - STATE_W
    w_q = (RELAX / (SHIFT + 6.0)) * f_mask

    def post(k, _):
        p = k + 1
        here = plane_inside(flags, p, STATE_W, f_planes)
        sums, grads = neighbours(fine, p)
        for f in range(4):
            w = weight[p + off] if f < 3 else w_q * here
            mid[f, p] = KEEP * fine[f, p] + w * (rhs[f, p + off] + sums[f] - 0.5 * grads[f])
        return 0

    lax.fori_loop(0, f_planes + 2, post, 0)

    def final(k, _):
        p = k + 2
        sums, grads = neighbours(mid, p)
        for f in range(4):
            w = weight[p + off] if f < 3 else w_q
            v = KEEP * mid[f, p] + w * (rhs[f, p + off] + sums[f] - 0.5 * grads[f])
            out[f, k] = v[0:f_rows, 0:f_lanes]
        return 0

    lax.fori_loop(0, f_planes, final, 0)


def call(kernel, shapes, scratch, *args, smem=1):
    outs = [jax.ShapeDtypeStruct(s, jnp.float32) for s in shapes]
    return pl.pallas_call(
        kernel,
        out_shape=outs,
        in_specs=[SMEM] * smem + [VMEM] * (len(args) - smem),
        out_specs=[VMEM] * len(outs),
        scratch_shapes=scratch,
        compiler_params=PARAMS,
    )(*args)


def routes(block_tile, block_slot, tiles, count_l, per_device, capacity, slots):
    my_tile = lax.axis_index("gx") * lax.axis_size("gy") + lax.axis_index("gy")
    index_l = lax.axis_index("lvl")
    their_tiles = lax.dynamic_index_in_dim(block_tile.reshape(tiles, count_l, per_device), index_l, 1, keepdims=False)
    their_slots = lax.dynamic_index_in_dim(block_slot.reshape(tiles, count_l, per_device), index_l, 1, keepdims=False)
    arriving = their_tiles == my_tile
    counter = jnp.arange(per_device, dtype=jnp.int32)
    earlier = counter[None, :, None] < counter[None, None, :]
    order = jnp.sum(jnp.where(arriving[:, :, None] & earlier, 1, 0), axis=1)
    places = jnp.arange(capacity, dtype=jnp.int32)
    hit = arriving[:, None, :] & (order[:, None, :] == places[None, :, None])
    slot = jnp.sum(jnp.where(hit, their_slots[:, None, :] - slots, 0), axis=2) + slots
    return slot.reshape(-1)


def body(right_side, start_field, mask_blocks, block_tile, block_slot):
    axes = ("gx", "gy", "lvl")
    counts = [lax.axis_size(a) for a in axes]
    index = [lax.axis_index(a) for a in axes]
    tiles = counts[0] * counts[1]
    per_device, width = mask_blocks.shape
    capacity = max(2, 2 * per_device // tiles)
    _, planes, rows, lanes = right_side.shape
    slots = planes // 2 * (rows // 2)
    c_planes, c_rows, c_lanes = planes // 2, rows // 2, lanes // 2
    flags = [i % 2 == 0 for i in index]
    for i, n in zip(index, counts):
        flags += [i < n - 1, i > 0]
    flags = jnp.stack(flags).astype(jnp.int32)

    my_flat = (index[0] * counts[1] + index[1]) * counts[2] + index[2]
    tile_ids = block_tile[:, 0]
    my_tiles = lax.dynamic_slice_in_dim(tile_ids, my_flat * per_device, per_device)
    (outgoing,) = call(
        functools.partial(pack_kernel, capacity=capacity),
        [(tiles, capacity, width // LANES, LANES)],
        [pltpu.SMEM((tiles,), jnp.int32)],
        my_tiles, mask_blocks.reshape(per_device, width // LANES, LANES),
    )
    outgoing, right_side, start_field = lax.optimization_barrier((outgoing, right_side, start_field))
    arrived = lax.all_to_all(outgoing, ("gx", "gy"), split_axis=0, concat_axis=0, tiled=True)
    slot_of = routes(tile_ids, block_slot, tiles, counts[2], per_device, capacity, slots)

    total, wide = rows + 8, lanes + LANES
    near, far = planes + 2 * STATE_W, planes + 2 * FINE_W
    got = halo([(start_field, START_W), (right_side, FINE_W)], START_W)
    nums = [len(g) for g in got]
    rhs, start, part = call(
        functools.partial(first_kernel, nums=nums),
        [(4, far, total, wide), (4, planes + 2 * START_W, total, wide), (4, far, total, wide)],
        [],
        flags, right_side, start_field, *sum(got, []),
    )
    chi, pooled_chi = call(
        chi_kernel,
        [(1, planes, rows, lanes), (c_planes, c_rows, lanes)],
        [pltpu.VMEM(((slots + 1) * 8, LANES), jnp.float32), pltpu.VMEM((lanes // LANES, rows, LANES), jnp.float32)],
        slot_of, arrived,
    )
    got = halo([(chi, FINE_W)], FINE_W)
    state, weight, coarse = call(
        functools.partial(second_kernel, nums=nums),
        [(4, near, total, wide), (far, total, wide), (5, c_planes, c_rows, c_lanes)],
        [
            pltpu.VMEM((1, far, total, wide), jnp.float32),
            pltpu.VMEM((4, far, total, wide), jnp.float32),
            pltpu.VMEM((4, lanes // LANES, rows, LANES), jnp.float32),
            pltpu.VMEM((5, c_planes, c_rows, lanes), jnp.float32),
        ],
        flags, chi, pooled_chi, rhs, start, part, *sum(got, []),
    )
    got = halo([(coarse, COARSE_W)], COARSE_W)
    c_ext = (c_planes + 2 * COARSE_W, c_rows + 8, c_lanes + LANES)
    (out,) = call(
        functools.partial(last_kernel, nums=nums),
        [right_side.shape],
        [
            pltpu.VMEM((5, *c_ext), jnp.float32),
            pltpu.VMEM((4, *c_ext), jnp.float32),
            pltpu.VMEM((4, *c_ext), jnp.float32),
            pltpu.VMEM((4, near, total, wide), jnp.float32),
            pltpu.VMEM((4, near, total, wide), jnp.float32),
            pltpu.VMEM((wide // LANES, total, LANES), jnp.float32),
        ],
        flags, coarse, state, weight, rhs, *sum(got, []),
    )
    return out


def solution(mesh):
    in_specs = (
        P(None, "gx", "gy", "lvl"),
        P(None, "gx", "gy", "lvl"),
        P(("gx", "gy", "lvl"), None),
        P(),
        P(),
    )
    out_specs = P(None, "gx", "gy", "lvl")
    return jax.shard_map(body, mesh=mesh, in_specs=in_specs, out_specs=out_specs, check_vma=False)
```

```python
import functools

import jax
import jax.numpy as jnp
from jax import lax
from jax.experimental import pallas as pl
from jax.experimental.pallas import tpu as pltpu
from jax.sharding import PartitionSpec as P

COARSE_SWEEPS = 4
SHIFT = 0.05
RELAX = 0.6
KEEP = 1.0 - RELAX
LANES = 128
START_W = 3
FINE_W = 2
CORNER = 2
STATE_W = 2
COARSE_W = 4
PAD = 4
HIGHEST = lax.Precision.HIGHEST
VMEM = pl.BlockSpec(memory_space=pltpu.VMEM)
SMEM = pl.BlockSpec(memory_space=pltpu.SMEM)
PARAMS = pltpu.CompilerParams(vmem_limit_bytes=48 << 20)


def pairs(count, first):
    return [p for i in range(first, count - 1, 2) for p in ((i, i + 1), (i + 1, i))]


def cut(values, dim, width, to_next):
    size = values.shape[dim]
    if size == width:
        return values
    start = jnp.where(to_next, size - width, 0)
    return lax.dynamic_slice_in_dim(values, start, width, axis=dim)


def flat(parts):
    return jnp.concatenate([p.reshape(-1, *p.shape[-2:]) for p in parts], axis=0)


def swap(axis, message):
    count = lax.axis_size(axis)
    even = lax.axis_index(axis) % 2 == 0
    got = [lax.ppermute(message(even), axis, pairs(count, 0))]
    if count > 2:
        got.append(lax.ppermute(message(~even), axis, pairs(count, 1)))
    return got


def halo(groups, depth, corner=0):
    xs = swap("gx", lambda up: flat([cut(v, 1, w, up) for v, w in groups]))
    own_y = lambda up: flat([cut(v, 2, depth, up) for v, _ in groups])
    far_y = lambda up: jnp.concatenate([cut(x, 1, corner or depth, up) for x in xs], axis=0)
    if corner:
        ys = swap("gy", own_y) + swap("gy", far_y)
        pad = lambda v: jnp.pad(v, ((0, 0), (0, PAD - v.shape[1]), (0, 0)))
        half = len(ys) // 2
        joined = [jnp.concatenate([pad(o), pad(c)], axis=0) for o, c in zip(ys[:half], ys[half:])]
    else:
        ys = swap("gy", lambda up: jnp.concatenate([own_y(up), far_y(up)], axis=0))
        joined = ys
    rows = groups[0][0].shape[2]

    def last(up):
        sent = [flat([cut(v, 3, LANES, up) for v, _ in groups]), *[cut(x, 2, LANES, up) for x in xs]]
        for y in joined:
            edge = cut(y, 2, LANES, up)
            short = -edge.shape[0] % (rows // PAD)
            edge = jnp.pad(edge, ((0, short), (0, PAD - edge.shape[1]), (0, 0)))
            sent.append(edge.reshape(-1, rows, LANES))
        return jnp.concatenate(sent, axis=0)

    return xs, ys, swap("lvl", last)


def place_halo(dst, margin, own, got, flags, width, depth, group=(0, 0), corner=0):
    xs, ys, zs = got
    fields, planes, rows, lanes = own.shape
    total = dst.shape[2]
    x_slabs = xs[0].shape[0]
    pairs_y = len(ys) // 2 if corner else len(ys)
    if corner:
        own_slabs = ys[0].shape[0]
    else:
        own_slabs = ys[0].shape[0] - len(xs) * x_slabs
    slab_count = own_slabs + len(xs) * x_slabs
    per = rows // PAD
    even_x, even_y, even_z = flags[0] == 1, flags[1] == 1, flags[2] == 1
    near = (lax.broadcasted_iota(jnp.int32, (1, LANES), 1) < LANES // 2) == even_z

    def edge(at, row, size):
        part = slice(row, row + size)
        return jnp.where(near, zs[0][at, part], 0.0 if len(zs) == 1 else zs[1][at, part])

    for f in range(fields):
        for k in range(planes + len(xs) * width):
            deep = depth
            if k < planes:
                at, plane, slab = margin + k, own[f, k], group[0] + f * planes + k
            else:
                which, j = divmod(k - planes, width)
                up, down = margin + planes + j, margin - width + j
                at = jnp.where(even_x, up, down) if which == 0 else jnp.where(even_x, down, up)
                plane = xs[which][group[1] + f * width + j]
                slab = own_slabs + which * x_slabs + group[1] + f * width + j
                deep = corner or depth
            dst[f, at, 0:rows, 0:lanes] = plane
            dst[f, at, 0:rows, lanes:] = edge(slab, 0, rows)
            sides = []
            for n in range(pairs_y):
                at_z = slab_count + n * (-(-slab_count // per)) + slab // per
                if corner and k >= planes:
                    y = ys[pairs_y + n][slab - own_slabs]
                else:
                    y = ys[n][slab]
                sides.append((y, edge(at_z, slab % per * PAD, deep)))
            if len(sides) == 1:
                sides.append([jnp.zeros_like(v) for v in sides[0]])
            for to, first, second in zip((slice(0, lanes), slice(lanes, lanes + LANES)), *sides):
                dst[f, at, rows:rows + deep, to] = jnp.where(even_y, first, second)
                dst[f, at, total - deep:total, to] = jnp.where(even_y, second, first)
            gap = total - rows - 2 * deep
            if gap:
                dst[f, at, rows + deep:total - deep, :] = jnp.zeros((gap, dst.shape[3]), jnp.float32)


def state_halo(state):
    first, rows, lanes = STATE_W, state.shape[2] - 8, state.shape[3] - LANES
    planes = state.shape[1] - 2 * STATE_W
    own = state[:, first:first + planes, :rows, :lanes]
    xs = swap("gx", lambda up: lax.dynamic_index_in_dim(own, jnp.where(up, planes - 2, 1), 1, keepdims=False))
    near = state[:, first - 1:first + planes + 1]
    ys = swap("gy", lambda up: cut(near[:, :, :rows, :lanes], 2, STATE_W, up).reshape(-1, STATE_W, lanes))
    zs = swap("lvl", lambda up: cut(near[..., :lanes], 3, LANES, up).reshape(-1, rows + 8, LANES))
    return xs, ys, zs


def outer_kernel(flags, state, *refs, nums):
    got, (out,) = split(refs, nums)
    xs, ys, zs = got
    fields, near, total, wide = state.shape
    planes, rows, lanes = near - 2 * STATE_W, total - 8, wide - LANES
    even_x, even_y, even_z = flags[0] == 1, flags[1] == 1, flags[2] == 1
    side = (lax.broadcasted_iota(jnp.int32, (1, LANES), 1) < LANES // 2) == even_z
    for f in range(fields):
        for k in range(planes + 2):
            p, slab = STATE_W - 1 + k, f * (planes + 2) + k
            out[f, p, :, 0:lanes] = state[f, p, :, 0:lanes]
            out[f, p, :, lanes:] = jnp.where(side, zs[0][slab], 0.0 if len(zs) == 1 else zs[1][slab])
            first = ys[0][slab]
            second = ys[1][slab] if len(ys) > 1 else jnp.zeros_like(first)
            out[f, p, rows:rows + STATE_W, 0:lanes] = jnp.where(even_y, first, second)
            out[f, p, total - STATE_W:total, 0:lanes] = jnp.where(even_y, second, first)
        first = xs[0][f]
        second = xs[1][f] if len(xs) > 1 else jnp.zeros_like(first)
        for p in (0, near - 1):
            out[f, p] = jnp.zeros((total, wide), jnp.float32)
            is_first = even_x if p else ~even_x
            out[f, p, 0:rows, 0:lanes] = jnp.where(is_first, first, second)


def inside(flags, rows, lanes, total, depth):
    row = lax.broadcasted_iota(jnp.int32, (total, lanes + LANES), 0)
    lane = lax.broadcasted_iota(jnp.int32, (total, lanes + LANES), 1)
    end = lanes + LANES
    row_ok = (row < rows) | ((row < rows + depth) & (flags[5] == 1)) | ((row >= total - depth) & (flags[6] == 1))
    lane_ok = (lane < lanes) | ((lane < lanes + depth) & (flags[7] == 1)) | ((lane >= end - depth) & (flags[8] == 1))
    return jnp.where(row_ok & lane_ok, 1.0, 0.0)


def plane_inside(flags, p, margin, planes):
    return jnp.where(p < margin, flags[4], jnp.where(p >= margin + planes, flags[3], 1)).astype(jnp.float32)


def neighbours(ref, p):
    rows, lanes = ref.shape[2], ref.shape[3]
    sums, grads, spread = [], [], 0.0
    for f in range(4):
        c, xn, xp = ref[f, p], ref[f, p + 1], ref[f, p - 1]
        yn, yp = pltpu.roll(c, rows - 1, 0), pltpu.roll(c, 1, 0)
        zn, zp = pltpu.roll(c, lanes - 1, 1), pltpu.roll(c, 1, 1)
        sums.append((xn + xp) + (yn + yp) + (zn + zp))
        if f == 3:
            grads = [xn - xp, yn - yp, zn - zp]
        else:
            spread = spread + (xn - xp, yn - yp, zn - zp)[f]
    return sums, grads + [spread]


def pack_kernel(tile_ref, mask_ref, out_ref, used_ref, *, capacity):
    tiles = out_ref.shape[0]
    count = mask_ref.shape[0]
    out_ref[...] = jnp.zeros(out_ref.shape, jnp.float32)

    def clear(t, _):
        used_ref[t] = 0
        return 0

    lax.fori_loop(0, tiles, clear, 0)

    def row(r, _):
        t = tile_ref[r]
        n = used_ref[t]
        used_ref[t] = n + 1
        out_ref[t, jnp.minimum(n, capacity - 1)] = mask_ref[r]
        return 0

    lax.fori_loop(0, count, row, 0)


def split(refs, nums):
    at, got = 0, []
    for n in nums:
        got.append(refs[at:at + n])
        at += n
    return got, refs[at:]


def first_kernel(flags, rhs, start, *refs, nums):
    got, (rhs_out, start_out, part_out) = split(refs, nums)
    planes = rhs.shape[1]
    place_halo(start_out, START_W, start, got, flags, START_W, START_W, corner=CORNER)
    place_halo(rhs_out, FINE_W, rhs, got, flags, FINE_W, START_W, (4 * planes, 4 * START_W), CORNER)

    def plane(k, _):
        sums, grads = neighbours(start_out, k + START_W - FINE_W)
        for f in range(4):
            part_out[f, k] = rhs_out[f, k] + sums[f] - 0.5 * grads[f]
        return 0

    lax.fori_loop(0, planes + 2 * FINE_W, plane, 0)


def chi_kernel(slot_ref, rows_ref, out, coarse_out, acc, pooled):
    _, planes, rows, lanes = out.shape
    acc[...] = jnp.zeros(acc.shape, jnp.float32)
    per = rows_ref.shape[1]

    def add(s, _):
        for c in range(per):
            at = pl.ds(pl.multiple_of(slot_ref[s * per + c] * 8, 8), 8)
            acc[at, :] = acc[at, :] + rows_ref[s, c]
        return 0

    lax.fori_loop(0, rows_ref.shape[0], add, 0)
    z_tiles = lanes // LANES
    across = rows // 2
    for qx in range(planes // 2):
        for zt in range(z_tiles):
            total = None
            for i in range(2):
                for j in range(2):
                    v = acc[pl.ds(qx * across * 8 + (2 * i + j) * z_tiles + zt, across, stride=8), :]
                    pooled[zt, pl.ds(j, across, stride=2), :] = v
                    total = v if total is None else total + v
                out[0, 2 * qx + i, :, zt * LANES:(zt + 1) * LANES] = pooled[zt]
            coarse_out[qx, :, zt * LANES:(zt + 1) * LANES] = total


def second_kernel(flags, own, pooled_chi, rhs, start, part, *refs, nums):
    got, (state_out, weight_out, coarse_out, chi, ext, tmp, pooled) = split(refs, nums)
    _, planes, rows, lanes = own.shape
    total = ext.shape[2]
    place_halo(chi, FINE_W, own, got, flags, FINE_W, FINE_W)
    mask = inside(flags, rows, lanes, total, FINE_W)
    w_p = (RELAX / (SHIFT + 6.0)) * mask

    def begin(k, _):
        here = plane_inside(flags, k, FINE_W, planes)
        w_u = (RELAX / (SHIFT + 6.0 + chi[0, k])) * (mask * here)
        weight_out[k] = w_u
        for f in range(4):
            w = w_u if f < 3 else w_p * here
            ext[f, k] = KEEP * start[f, k + START_W - FINE_W] + w * part[f, k]
        return 0

    lax.fori_loop(0, planes + 2 * FINE_W, begin, 0)

    def sweep(k, _):
        p = k + 1
        here = plane_inside(flags, p, FINE_W, planes)
        sums, grads = neighbours(ext, p)
        w_u = weight_out[p]
        for f in range(4):
            w = w_u if f < 3 else w_p * here
            state_out[f, p] = KEEP * ext[f, p] + w * (rhs[f, p] + sums[f] - 0.5 * grads[f])
        return 0

    lax.fori_loop(0, planes + 2 * (FINE_W - 1), sweep, 0)

    def pool(cx, _):
        both = [None] * 4
        for i in range(2):
            p = FINE_W + 2 * cx + i
            sums, grads = neighbours(state_out, p)
            for f in range(4):
                diag = SHIFT + 6.0 + (chi[0, p] if f < 3 else 0.0)
                r = rhs[f, p] + sums[f] - 0.5 * grads[f] - diag * state_out[f, p]
                both[f] = r if i == 0 else both[f] + r
        for f in range(4):
            for zt in range(lanes // LANES):
                tmp[f, zt] = both[f][0:rows, zt * LANES:(zt + 1) * LANES]
                v = tmp[f, zt, pl.ds(0, rows // 2, stride=2), :] + tmp[f, zt, pl.ds(1, rows // 2, stride=2), :]
                pooled[f, cx, :, zt * LANES:(zt + 1) * LANES] = v
        return 0

    lax.fori_loop(0, planes // 2, pool, 0)
    pooled[4] = pooled_chi[...]
    lane = lax.broadcasted_iota(jnp.int32, (lanes, lanes // 2), 0)
    cell = lax.broadcasted_iota(jnp.int32, (lanes, lanes // 2), 1)
    gather = jnp.where(lane // 2 == cell, 0.125, 0.0)
    flat_rows = pooled[...].reshape(5 * planes // 2 * rows // 2, lanes)
    coarse = jnp.dot(flat_rows, gather, precision=HIGHEST, preferred_element_type=jnp.float32)
    coarse_out[...] = coarse.reshape(coarse_out.shape)


def last_kernel(flags, own, state, weight, rhs, *refs, nums):
    got, (out, ext, one, two, fine, mid, tmp) = split(refs, nums)
    planes, rows, lanes = own.shape[1:]
    total, wide = ext.shape[2], ext.shape[3]
    place_halo(ext, COARSE_W, own, got, flags, COARSE_W, COARSE_W)
    mask = inside(flags, rows, lanes, total, COARSE_W)
    w_p = (RELAX / (SHIFT + 1.5)) * mask

    def begin(p, _):
        here = plane_inside(flags, p, COARSE_W, planes)
        w_u = (RELAX / (SHIFT + 1.5 + ext[4, p])) * (mask * here)
        ext[4, p] = w_u
        for f in range(4):
            one[f, p] = (w_u if f < 3 else w_p * here) * ext[f, p]
        return 0

    lax.fori_loop(0, planes + 2 * COARSE_W, begin, 0)
    now, then = one, two
    for s in range(1, COARSE_SWEEPS):
        def sweep(k, _, now=now, then=then, s=s):
            p = k + s
            here = plane_inside(flags, p, COARSE_W, planes)
            sums, grads = neighbours(now, p)
            for f in range(4):
                w = ext[4, p] if f < 3 else w_p * here
                then[f, p] = KEEP * now[f, p] + w * (ext[f, p] + 0.25 * (sums[f] - grads[f]))
            return 0

        lax.fori_loop(0, planes + 2 * COARSE_W - 2 * s, sweep, 0)
        now, then = then, now

    f_total, f_wide = fine.shape[2], fine.shape[3]
    f_rows, f_lanes = 2 * rows, 2 * lanes
    cell = lax.broadcasted_iota(jnp.int32, (wide, f_wide), 0)
    lane = lax.broadcasted_iota(jnp.int32, (wide, f_wide), 1)
    from_cell = jnp.where(lane < f_lanes + LANES // 2, lane // 2, wide - 1 - (f_wide - 1 - lane) // 2)
    spread = jnp.where(cell == from_cell, 1.0, 0.0)
    c_planes = planes + 2
    flat = now[:, COARSE_W - 1:COARSE_W - 1 + c_planes].reshape(4 * c_planes * total, wide)
    grown = jnp.dot(flat, spread, precision=HIGHEST, preferred_element_type=jnp.float32)
    for f in range(4):
        for cp in range(c_planes):
            lo = (f * c_planes + cp) * total
            for zt in range(f_wide // LANES):
                v = grown[lo:lo + total, zt * LANES:(zt + 1) * LANES]
                at = f * c_planes + cp
                for j in range(2):
                    tmp[zt, pl.ds(j, rows, stride=2), :] = v[0:rows]
                    tmp[zt, pl.ds(f_rows + j, 2, stride=2), :] = v[rows:rows + 2]
                    tmp[zt, pl.ds(f_total - 4 + j, 2, stride=2), :] = v[total - 2:total]
                for i in range(2):
                    to = slice(zt * LANES, (zt + 1) * LANES)
                    fine[f, 2 * cp + i, :, to] = state[f, 2 * cp + i, :, to] + tmp[zt]
    f_planes = 2 * planes
    f_mask = inside(flags, f_rows, f_lanes, f_total, STATE_W)
    off = FINE_W - STATE_W
    w_q = (RELAX / (SHIFT + 6.0)) * f_mask

    def post(k, _):
        p = k + 1
        here = plane_inside(flags, p, STATE_W, f_planes)
        sums, grads = neighbours(fine, p)
        for f in range(4):
            w = weight[p + off] if f < 3 else w_q * here
            mid[f, p] = KEEP * fine[f, p] + w * (rhs[f, p + off] + sums[f] - 0.5 * grads[f])
        return 0

    lax.fori_loop(0, f_planes + 2, post, 0)

    def final(k, _):
        p = k + 2
        sums, grads = neighbours(mid, p)
        for f in range(4):
            w = weight[p + off] if f < 3 else w_q
            v = KEEP * mid[f, p] + w * (rhs[f, p + off] + sums[f] - 0.5 * grads[f])
            out[f, k] = v[0:f_rows, 0:f_lanes]
        return 0

    lax.fori_loop(0, f_planes, final, 0)


def call(kernel, shapes, scratch, *args, smem=1):
    outs = [jax.ShapeDtypeStruct(s, jnp.float32) for s in shapes]
    return pl.pallas_call(
        kernel,
        out_shape=outs,
        in_specs=[SMEM] * smem + [VMEM] * (len(args) - smem),
        out_specs=[VMEM] * len(outs),
        scratch_shapes=scratch,
        compiler_params=PARAMS,
    )(*args)


def routes(block_tile, block_slot, tiles, count_l, per_device, capacity, slots):
    my_tile = lax.axis_index("gx") * lax.axis_size("gy") + lax.axis_index("gy")
    index_l = lax.axis_index("lvl")
    their_tiles = lax.dynamic_index_in_dim(block_tile.reshape(tiles, count_l, per_device), index_l, 1, keepdims=False)
    their_slots = lax.dynamic_index_in_dim(block_slot.reshape(tiles, count_l, per_device), index_l, 1, keepdims=False)
    arriving = their_tiles == my_tile
    counter = jnp.arange(per_device, dtype=jnp.int32)
    earlier = counter[None, :, None] < counter[None, None, :]
    order = jnp.sum(jnp.where(arriving[:, :, None] & earlier, 1, 0), axis=1)
    places = jnp.arange(capacity, dtype=jnp.int32)
    hit = arriving[:, None, :] & (order[:, None, :] == places[None, :, None])
    slot = jnp.sum(jnp.where(hit, their_slots[:, None, :] - slots, 0), axis=2) + slots
    return slot.reshape(-1)


def body(right_side, start_field, mask_blocks, block_tile, block_slot):
    axes = ("gx", "gy", "lvl")
    counts = [lax.axis_size(a) for a in axes]
    index = [lax.axis_index(a) for a in axes]
    tiles = counts[0] * counts[1]
    per_device, width = mask_blocks.shape
    capacity = max(2, 2 * per_device // tiles)
    _, planes, rows, lanes = right_side.shape
    slots = planes // 2 * (rows // 2)
    c_planes, c_rows, c_lanes = planes // 2, rows // 2, lanes // 2
    flags = [i % 2 == 0 for i in index]
    for i, n in zip(index, counts):
        flags += [i < n - 1, i > 0]
    flags = jnp.stack(flags).astype(jnp.int32)

    my_flat = (index[0] * counts[1] + index[1]) * counts[2] + index[2]
    tile_ids = block_tile[:, 0]
    my_tiles = lax.dynamic_slice_in_dim(tile_ids, my_flat * per_device, per_device)
    (outgoing,) = call(
        functools.partial(pack_kernel, capacity=capacity),
        [(tiles, capacity, width // LANES, LANES)],
        [pltpu.SMEM((tiles,), jnp.int32)],
        my_tiles, mask_blocks.reshape(per_device, width // LANES, LANES),
    )
    outgoing, right_side, start_field = lax.optimization_barrier((outgoing, right_side, start_field))
    arrived = lax.all_to_all(outgoing, ("gx", "gy"), split_axis=0, concat_axis=0, tiled=True)
    slot_of = routes(tile_ids, block_slot, tiles, counts[2], per_device, capacity, slots)

    total, wide = rows + 8, lanes + LANES
    near, far = planes + 2 * STATE_W, planes + 2 * FINE_W
    got = halo([(start_field, START_W), (right_side, FINE_W)], START_W, CORNER)
    nums = [len(g) for g in got]
    rhs, start, part = call(
        functools.partial(first_kernel, nums=nums),
        [(4, far, total, wide), (4, planes + 2 * START_W, total, wide), (4, far, total, wide)],
        [],
        flags, right_side, start_field, *sum(got, []),
    )
    chi, pooled_chi = call(
        chi_kernel,
        [(1, planes, rows, lanes), (c_planes, c_rows, lanes)],
        [pltpu.VMEM(((slots + 1) * 8, LANES), jnp.float32), pltpu.VMEM((lanes // LANES, rows, LANES), jnp.float32)],
        slot_of, arrived,
    )
    got = halo([(chi, FINE_W)], FINE_W)
    nums = [len(g) for g in got]
    state, weight, coarse = call(
        functools.partial(second_kernel, nums=nums),
        [(4, near, total, wide), (far, total, wide), (5, c_planes, c_rows, c_lanes)],
        [
            pltpu.VMEM((1, far, total, wide), jnp.float32),
            pltpu.VMEM((4, far, total, wide), jnp.float32),
            pltpu.VMEM((4, lanes // LANES, rows, LANES), jnp.float32),
            pltpu.VMEM((5, c_planes, c_rows, lanes), jnp.float32),
        ],
        flags, chi, pooled_chi, rhs, start, part, *sum(got, []),
    )
    got = halo([(coarse, COARSE_W)], COARSE_W)
    outer = state_halo(state)
    (state,) = call(
        functools.partial(outer_kernel, nums=[len(g) for g in outer]),
        [state.shape],
        [],
        flags, state, *sum(outer, []),
    )
    c_ext = (c_planes + 2 * COARSE_W, c_rows + 8, c_lanes + LANES)
    (out,) = call(
        functools.partial(last_kernel, nums=nums),
        [right_side.shape],
        [
            pltpu.VMEM((5, *c_ext), jnp.float32),
            pltpu.VMEM((4, *c_ext), jnp.float32),
            pltpu.VMEM((4, *c_ext), jnp.float32),
            pltpu.VMEM((4, near, total, wide), jnp.float32),
            pltpu.VMEM((4, near, total, wide), jnp.float32),
            pltpu.VMEM((wide // LANES, total, LANES), jnp.float32),
        ],
        flags, coarse, state, weight, rhs, *sum(got, []),
    )
    return out


def solution(mesh):
    in_specs = (
        P(None, "gx", "gy", "lvl"),
        P(None, "gx", "gy", "lvl"),
        P(("gx", "gy", "lvl"), None),
        P(),
        P(),
    )
    out_specs = P(None, "gx", "gy", "lvl")
    return jax.shard_map(body, mesh=mesh, in_specs=in_specs, out_specs=out_specs, check_vma=False)
```

```python
import functools

import jax
import jax.numpy as jnp
from jax import lax
from jax.experimental import pallas as pl
from jax.experimental.pallas import tpu as pltpu
from jax.sharding import PartitionSpec as P

COARSE_SWEEPS = 4
SHIFT = 0.05
RELAX = 0.6
KEEP = 1.0 - RELAX
LANES = 128
START_W = 3
FINE_W = 2
CORNER = 2
STATE_W = 2
COARSE_W = 4
PAD = 4
HIGHEST = lax.Precision.HIGHEST
VMEM = pl.BlockSpec(memory_space=pltpu.VMEM)
SMEM = pl.BlockSpec(memory_space=pltpu.SMEM)
PARAMS = pltpu.CompilerParams(vmem_limit_bytes=24 << 20)


def pairs(count, first):
    return [p for i in range(first, count - 1, 2) for p in ((i, i + 1), (i + 1, i))]


def cut(values, dim, width, to_next):
    size = values.shape[dim]
    if size == width:
        return values
    start = jnp.where(to_next, size - width, 0)
    return lax.dynamic_slice_in_dim(values, start, width, axis=dim)


def flat(parts):
    return jnp.concatenate([p.reshape(-1, *p.shape[-2:]) for p in parts], axis=0)


def swap(axis, message):
    count = lax.axis_size(axis)
    even = lax.axis_index(axis) % 2 == 0
    got = [lax.ppermute(message(even, 0), axis, pairs(count, 0))]
    if count > 2:
        got.append(lax.ppermute(message(~even, 1), axis, pairs(count, 1)))
    return got


def ride(messages, n, extra):
    return jnp.concatenate([*messages, *([extra[n]] if extra else [])], axis=0)


def halo_x(groups):
    return swap("gx", lambda up, n: flat([cut(v, 1, w, up) for v, w in groups]))


def halo_y(groups, depth, xs=(), extra=()):
    own = lambda up: [cut(v.reshape(-1, *v.shape[2:]), 1, depth, up) for v, _ in groups]
    return swap("gy", lambda up, n: ride([*own(up), *[cut(x, 1, depth, up) for x in xs]], n, extra))


def halo_z(groups, xs, ys, extra=()):
    rows = groups[0][0].shape[2]

    def last(up, n):
        sent = [flat([cut(v, 3, LANES, up) for v, _ in groups]), *[cut(x, 2, LANES, up) for x in xs]]
        for parts in ys:
            edge = [jnp.pad(cut(y, 2, LANES, up), ((0, 0), (0, PAD - y.shape[1]), (0, 0))) for y in parts]
            edge = jnp.concatenate(edge, axis=0)
            edge = jnp.pad(edge, ((0, -edge.shape[0] % (rows // PAD)), (0, 0), (0, 0)))
            sent.append(edge.reshape(-1, rows, LANES))
        return ride(sent, n, extra)

    return swap("lvl", last)


def place_halo(dst, margin, own, got, flags, width, depth, group=(0, 0), slabs=None, corner=0):
    xs, ys, zs = got
    rows, lanes = own.shape[-2:]
    fields, planes, total = dst.shape[0], dst.shape[1] - 2 * margin, dst.shape[2]
    own_slabs, x_slabs = slabs or (fields * planes, fields * width)
    pairs_y = len(ys) // 2 if corner else len(ys)
    slab_count = own_slabs + len(xs) * x_slabs
    per = rows // PAD
    even_x, even_y, even_z = flags[0] == 1, flags[1] == 1, flags[2] == 1
    near = (lax.broadcasted_iota(jnp.int32, (1, LANES), 1) < LANES // 2) == even_z

    def edge(at, row, size):
        part = slice(row, row + size)
        return jnp.where(near, zs[0][at, part], 0.0 if len(zs) == 1 else zs[1][at, part])

    for f in range(fields):
        for k in range(planes + len(xs) * width):
            deep = depth
            if k < planes:
                at, plane, slab = margin + k, own[f, k] if len(own.shape) == 4 else own[f * planes + k], group[0] + f * planes + k
            else:
                which, j = divmod(k - planes, width)
                up, down = margin + planes + j, margin - width + j
                at = jnp.where(even_x, up, down) if which == 0 else jnp.where(even_x, down, up)
                plane = xs[which][group[1] + f * width + j]
                slab = own_slabs + which * x_slabs + group[1] + f * width + j
                deep = corner or depth
            dst[f, at, 0:rows, 0:lanes] = plane
            dst[f, at, 0:rows, lanes:] = edge(slab, 0, rows)
            sides = []
            for n in range(pairs_y):
                at_z = slab_count + n * (-(-slab_count // per)) + slab // per
                if corner and k >= planes:
                    y = ys[pairs_y + n][slab - own_slabs]
                else:
                    y = ys[n][slab]
                sides.append((y, edge(at_z, slab % per * PAD, deep)))
            if len(sides) == 1:
                sides.append([jnp.zeros_like(v) for v in sides[0]])
            for to, first, second in zip((slice(0, lanes), slice(lanes, lanes + LANES)), *sides):
                dst[f, at, rows:rows + deep, to] = jnp.where(even_y, first, second)
                dst[f, at, total - deep:total, to] = jnp.where(even_y, second, first)
            gap = total - rows - 2 * deep
            if gap:
                dst[f, at, rows + deep:total - deep, :] = jnp.zeros((gap, dst.shape[3]), jnp.float32)


def place_outer(out, state, got, flags, before):
    xs, ys, zs = got
    fields, near, total, wide = state.shape
    planes, rows, lanes = near - 2 * STATE_W, total - 8, wide - LANES
    even_x, even_y, even_z = flags[0] == 1, flags[1] == 1, flags[2] == 1
    side = (lax.broadcasted_iota(jnp.int32, (1, LANES), 1) < LANES // 2) == even_z
    tiles = [(r, z) for r in range(rows // 8) for z in range(lanes // LANES)]
    for f in range(fields):
        for k in range(planes + 2):
            p, slab = STATE_W - 1 + k, f * (planes + 2) + k
            out[f, p, :, 0:lanes] = state[f, p, :, 0:lanes]
            for r in range(total // 8):
                at = before[2] + slab * (total // 8) + r
                z = jnp.where(side, zs[0][at], 0.0 if len(zs) == 1 else zs[1][at])
                out[f, p, r * 8:(r + 1) * 8, lanes:] = z
            for z in range(lanes // LANES):
                part = slice(z * STATE_W, (z + 1) * STATE_W)
                first = ys[0][before[1] + slab, part]
                second = ys[1][before[1] + slab, part] if len(ys) > 1 else jnp.zeros_like(first)
                to = slice(z * LANES, (z + 1) * LANES)
                out[f, p, rows:rows + STATE_W, to] = jnp.where(even_y, first, second)
                out[f, p, total - STATE_W:total, to] = jnp.where(even_y, second, first)
        for p in (0, near - 1):
            out[f, p] = jnp.zeros((total, wide), jnp.float32)
            is_first = even_x if p else ~even_x
            for t, (r, z) in enumerate(tiles):
                at = before[0] + f * len(tiles) + t
                first = xs[0][at]
                second = xs[1][at] if len(xs) > 1 else jnp.zeros_like(first)
                out[f, p, r * 8:(r + 1) * 8, z * LANES:(z + 1) * LANES] = jnp.where(is_first, first, second)


def send_outer(state, flags, x_out, y_out, z_out, before):
    fields, near, total, wide = state.shape
    planes, rows, lanes = near - 2 * STATE_W, total - 8, wide - LANES
    up = [[(flags[a] == 1) == (n == 0) for n in range(2)] for a in range(3)]
    tiles = [(r, z) for r in range(rows // 8) for z in range(lanes // LANES)]
    for n, ref in enumerate(x_out):
        p = jnp.where(up[0][n], STATE_W + planes - 2, STATE_W + 1)
        for f in range(fields):
            for t, (r, z) in enumerate(tiles):
                ref[before + f * len(tiles) + t] = state[f, p, r * 8:(r + 1) * 8, z * LANES:(z + 1) * LANES]
    for f in range(fields):
        for k in range(planes + 2):
            p, slab = STATE_W - 1 + k, f * (planes + 2) + k
            for n, ref in enumerate(y_out):
                v = jnp.where(up[1][n], state[f, p, rows - STATE_W:rows, 0:lanes], state[f, p, 0:STATE_W, 0:lanes])
                for z in range(lanes // LANES):
                    ref[slab, z * STATE_W:(z + 1) * STATE_W] = v[:, z * LANES:(z + 1) * LANES]
            for n, ref in enumerate(z_out):
                for r in range(total // 8):
                    part = slice(r * 8, (r + 1) * 8)
                    v = jnp.where(up[2][n], state[f, p, part, lanes - LANES:lanes], state[f, p, part, 0:LANES])
                    ref[slab * (total // 8) + r] = v


def inside(flags, rows, lanes, total, depth):
    row = lax.broadcasted_iota(jnp.int32, (total, lanes + LANES), 0)
    lane = lax.broadcasted_iota(jnp.int32, (total, lanes + LANES), 1)
    end = lanes + LANES
    row_ok = (row < rows) | ((row < rows + depth) & (flags[5] == 1)) | ((row >= total - depth) & (flags[6] == 1))
    lane_ok = (lane < lanes) | ((lane < lanes + depth) & (flags[7] == 1)) | ((lane >= end - depth) & (flags[8] == 1))
    return jnp.where(row_ok & lane_ok, 1.0, 0.0)


def plane_inside(flags, p, margin, planes):
    return jnp.where(p < margin, flags[4], jnp.where(p >= margin + planes, flags[3], 1)).astype(jnp.float32)


def neighbours(ref, p):
    rows, lanes = ref.shape[2], ref.shape[3]
    sums, grads, spread = [], [], 0.0
    for f in range(4):
        c, xn, xp = ref[f, p], ref[f, p + 1], ref[f, p - 1]
        yn, yp = pltpu.roll(c, rows - 1, 0), pltpu.roll(c, 1, 0)
        zn, zp = pltpu.roll(c, lanes - 1, 1), pltpu.roll(c, 1, 1)
        sums.append((xn + xp) + (yn + yp) + (zn + zp))
        if f == 3:
            grads = [xn - xp, yn - yp, zn - zp]
        else:
            spread = spread + (xn - xp, yn - yp, zn - zp)[f]
    return sums, grads + [spread]


def pack_kernel(tile_ref, mask_ref, out_ref, used_ref, *, capacity):
    tiles = out_ref.shape[0]
    count = mask_ref.shape[0]
    out_ref[...] = jnp.zeros(out_ref.shape, jnp.float32)

    def clear(t, _):
        used_ref[t] = 0
        return 0

    lax.fori_loop(0, tiles, clear, 0)

    def row(r, _):
        t = tile_ref[r]
        n = used_ref[t]
        used_ref[t] = n + 1
        out_ref[t, jnp.minimum(n, capacity - 1)] = mask_ref[r]
        return 0

    lax.fori_loop(0, count, row, 0)


def split(refs, nums):
    at, got = 0, []
    for n in nums:
        got.append(refs[at:at + n])
        at += n
    return got, refs[at:]


def chi_kernel(slot_ref, rows_ref, out, coarse_out, acc, pooled):
    _, planes, rows, lanes = out.shape
    acc[...] = jnp.zeros(acc.shape, jnp.float32)
    per = rows_ref.shape[1]

    def add(s, _):
        for c in range(per):
            at = pl.ds(pl.multiple_of(slot_ref[s * per + c] * 8, 8), 8)
            acc[at, :] = acc[at, :] + rows_ref[s, c]
        return 0

    lax.fori_loop(0, rows_ref.shape[0], add, 0)
    z_tiles = lanes // LANES
    across = rows // 2
    for qx in range(planes // 2):
        for zt in range(z_tiles):
            total = None
            for i in range(2):
                for j in range(2):
                    v = acc[pl.ds(qx * across * 8 + (2 * i + j) * z_tiles + zt, across, stride=8), :]
                    pooled[zt, pl.ds(j, across, stride=2), :] = v
                    total = v if total is None else total + v
                out[0, 2 * qx + i, :, zt * LANES:(zt + 1) * LANES] = pooled[zt]
            coarse_out[qx, :, zt * LANES:(zt + 1) * LANES] = total


def second_kernel(flags, own, pooled_chi, right_side, start_field, *refs, nums):
    (got, refs), (fields_got, refs) = split(refs, nums[:3]), split(refs[sum(nums[:3]):], nums[3:6])
    rhs, state_out, weight_out = refs[:3]
    (x_out, y_out, z_out), (chi, start, ext, tmp, pooled) = split(refs[3:], nums[6:])
    _, planes, rows, lanes = own.shape
    total = ext.shape[2]
    slabs = (8 * planes, 4 * (START_W + FINE_W))
    place_halo(start, START_W, start_field, fields_got, flags, START_W, START_W, (0, 0), slabs, CORNER)
    place_halo(rhs, FINE_W, right_side, fields_got, flags, FINE_W, START_W, (4 * planes, 4 * START_W), slabs, CORNER)
    place_halo(chi, FINE_W, own, got, flags, FINE_W, FINE_W)
    mask = inside(flags, rows, lanes, total, FINE_W)
    w_p = (RELAX / (SHIFT + 6.0)) * mask

    for k in range(planes + 2 * FINE_W):
        here = plane_inside(flags, k, FINE_W, planes)
        w_u = (RELAX / (SHIFT + 6.0 + chi[0, k])) * (mask * here)
        weight_out[k] = w_u
        sums, grads = neighbours(start, k + START_W - FINE_W)
        for f in range(4):
            w = w_u if f < 3 else w_p * here
            ext[f, k] = KEEP * start[f, k + START_W - FINE_W] + w * (rhs[f, k] + sums[f] - 0.5 * grads[f])

    for p in range(1, planes + 2 * FINE_W - 1):
        here = plane_inside(flags, p, FINE_W, planes)
        sums, grads = neighbours(ext, p)
        w_u = weight_out[p]
        for f in range(4):
            w = w_u if f < 3 else w_p * here
            state_out[f, p] = KEEP * ext[f, p] + w * (rhs[f, p] + sums[f] - 0.5 * grads[f])

    for cx in range(planes // 2):
        both = [None] * 4
        for i in range(2):
            p = FINE_W + 2 * cx + i
            sums, grads = neighbours(state_out, p)
            for f in range(4):
                diag = SHIFT + 6.0 + (chi[0, p] if f < 3 else 0.0)
                r = rhs[f, p] + sums[f] - 0.5 * grads[f] - diag * state_out[f, p]
                both[f] = r if i == 0 else both[f] + r
        for f in range(4):
            for zt in range(lanes // LANES):
                tmp[f, zt] = both[f][0:rows, zt * LANES:(zt + 1) * LANES]
                v = tmp[f, zt, pl.ds(0, rows // 2, stride=2), :] + tmp[f, zt, pl.ds(1, rows // 2, stride=2), :]
                pooled[f, cx, :, zt * LANES:(zt + 1) * LANES] = v
    pooled[4] = pooled_chi[...]
    lane = lax.broadcasted_iota(jnp.int32, (lanes, lanes // 2), 0)
    cell = lax.broadcasted_iota(jnp.int32, (lanes, lanes // 2), 1)
    gather = jnp.where(lane // 2 == cell, 0.125, 0.0)
    flat_rows = pooled[...].reshape(5 * planes // 2 * rows // 2, lanes)
    coarse = jnp.dot(flat_rows, gather, precision=HIGHEST, preferred_element_type=jnp.float32)
    coarse = coarse.reshape(5 * planes // 2, rows // 2, lanes // 2)
    for ref in x_out:
        ref[0:coarse.shape[0]] = coarse
    send_outer(state_out, flags, x_out, y_out, z_out, coarse.shape[0])


def last_kernel(flags, own, state, weight, rhs, *refs, nums):
    got, (out, ext, one, two, fine, mid, tmp) = split(refs, nums)
    planes = ext.shape[1] - 2 * COARSE_W
    rows, lanes = own.shape[1:]
    total, wide = ext.shape[2], ext.shape[3]
    own = own.at[0:5 * planes]
    place_halo(ext, COARSE_W, own, got, flags, COARSE_W, COARSE_W)
    x_slabs = 5 * COARSE_W
    slabs = 5 * planes + len(got[0]) * x_slabs
    z_slabs = slabs + len(got[1]) * -(-slabs // (rows // PAD))
    place_outer(fine, state, got, flags, (x_slabs, slabs, z_slabs))
    mask = inside(flags, rows, lanes, total, COARSE_W)
    w_p = (RELAX / (SHIFT + 1.5)) * mask

    for p in range(planes + 2 * COARSE_W):
        here = plane_inside(flags, p, COARSE_W, planes)
        w_u = (RELAX / (SHIFT + 1.5 + ext[4, p])) * (mask * here)
        ext[4, p] = w_u
        for f in range(4):
            one[f, p] = (w_u if f < 3 else w_p * here) * ext[f, p]
    now, then = one, two
    for s in range(1, COARSE_SWEEPS):
        for p in range(s, planes + 2 * COARSE_W - s):
            here = plane_inside(flags, p, COARSE_W, planes)
            sums, grads = neighbours(now, p)
            for f in range(4):
                w = ext[4, p] if f < 3 else w_p * here
                then[f, p] = KEEP * now[f, p] + w * (ext[f, p] + 0.25 * (sums[f] - grads[f]))
        now, then = then, now

    f_total, f_wide = fine.shape[2], fine.shape[3]
    f_rows, f_lanes = 2 * rows, 2 * lanes
    cell = lax.broadcasted_iota(jnp.int32, (wide, f_wide), 0)
    lane = lax.broadcasted_iota(jnp.int32, (wide, f_wide), 1)
    from_cell = jnp.where(lane < f_lanes + LANES // 2, lane // 2, wide - 1 - (f_wide - 1 - lane) // 2)
    spread = jnp.where(cell == from_cell, 1.0, 0.0)
    c_planes = planes + 2
    flat = now[:, COARSE_W - 1:COARSE_W - 1 + c_planes].reshape(4 * c_planes * total, wide)
    grown = jnp.dot(flat, spread, precision=HIGHEST, preferred_element_type=jnp.float32)
    for f in range(4):
        for cp in range(c_planes):
            lo = (f * c_planes + cp) * total
            for zt in range(f_wide // LANES):
                v = grown[lo:lo + total, zt * LANES:(zt + 1) * LANES]
                at = f * c_planes + cp
                for j in range(2):
                    tmp[zt, pl.ds(j, rows, stride=2), :] = v[0:rows]
                    tmp[zt, pl.ds(f_rows + j, 2, stride=2), :] = v[rows:rows + 2]
                    tmp[zt, pl.ds(f_total - 4 + j, 2, stride=2), :] = v[total - 2:total]
                for i in range(2):
                    to = slice(zt * LANES, (zt + 1) * LANES)
                    fine[f, 2 * cp + i, :, to] = fine[f, 2 * cp + i, :, to] + tmp[zt]
    f_planes = 2 * planes
    f_mask = inside(flags, f_rows, f_lanes, f_total, STATE_W)
    off = FINE_W - STATE_W
    w_q = (RELAX / (SHIFT + 6.0)) * f_mask

    for p in range(1, f_planes + 3):
        here = plane_inside(flags, p, STATE_W, f_planes)
        sums, grads = neighbours(fine, p)
        for f in range(4):
            w = weight[p + off] if f < 3 else w_q * here
            mid[f, p] = KEEP * fine[f, p] + w * (rhs[f, p + off] + sums[f] - 0.5 * grads[f])

    for k in range(f_planes):
        p = k + 2
        sums, grads = neighbours(mid, p)
        for f in range(4):
            w = weight[p + off] if f < 3 else w_q
            v = KEEP * mid[f, p] + w * (rhs[f, p + off] + sums[f] - 0.5 * grads[f])
            out[f, k] = v[0:f_rows, 0:f_lanes]


def call(kernel, shapes, scratch, *args, smem=1):
    outs = [jax.ShapeDtypeStruct(s, jnp.float32) for s in shapes]
    return pl.pallas_call(
        kernel,
        out_shape=outs,
        in_specs=[SMEM] * smem + [VMEM] * (len(args) - smem),
        out_specs=[VMEM] * len(outs),
        scratch_shapes=scratch,
        compiler_params=PARAMS,
    )(*args)


def routes(block_tile, block_slot, tiles, count_l, per_device, capacity, slots):
    my_tile = lax.axis_index("gx") * lax.axis_size("gy") + lax.axis_index("gy")
    index_l = lax.axis_index("lvl")
    their_tiles = lax.dynamic_index_in_dim(block_tile.reshape(tiles, count_l, per_device), index_l, 1, keepdims=False)
    their_slots = lax.dynamic_index_in_dim(block_slot.reshape(tiles, count_l, per_device), index_l, 1, keepdims=False)
    arriving = their_tiles == my_tile
    counter = jnp.arange(per_device, dtype=jnp.int32)
    earlier = counter[None, :, None] < counter[None, None, :]
    order = jnp.sum(jnp.where(arriving[:, :, None] & earlier, 1, 0), axis=1)
    places = jnp.arange(capacity, dtype=jnp.int32)
    hit = arriving[:, None, :] & (order[:, None, :] == places[None, :, None])
    slot = jnp.sum(jnp.where(hit, their_slots[:, None, :] - slots, 0), axis=2) + slots
    return slot.reshape(-1)


def body(right_side, start_field, mask_blocks, block_tile, block_slot):
    axes = ("gx", "gy", "lvl")
    counts = [lax.axis_size(a) for a in axes]
    index = [lax.axis_index(a) for a in axes]
    tiles = counts[0] * counts[1]
    per_device, width = mask_blocks.shape
    capacity = max(2, 2 * per_device // tiles)
    _, planes, rows, lanes = right_side.shape
    slots = planes // 2 * (rows // 2)
    c_planes, c_rows, c_lanes = planes // 2, rows // 2, lanes // 2
    flags = [i % 2 == 0 for i in index]
    for i, n in zip(index, counts):
        flags += [i < n - 1, i > 0]
    flags = jnp.stack(flags).astype(jnp.int32)

    my_flat = (index[0] * counts[1] + index[1]) * counts[2] + index[2]
    tile_ids = block_tile[:, 0]
    my_tiles = lax.dynamic_slice_in_dim(tile_ids, my_flat * per_device, per_device)
    (outgoing,) = call(
        functools.partial(pack_kernel, capacity=capacity),
        [(tiles, capacity, width // LANES, LANES)],
        [pltpu.SMEM((tiles,), jnp.int32)],
        my_tiles, mask_blocks.reshape(per_device, width // LANES, LANES),
    )
    outgoing, right_side, start_field = lax.optimization_barrier((outgoing, right_side, start_field))
    arrived = lax.all_to_all(outgoing, ("gx", "gy"), split_axis=0, concat_axis=0, tiled=True)
    slot_of = routes(tile_ids, block_slot, tiles, counts[2], per_device, capacity, slots)

    total, wide = rows + 8, lanes + LANES
    near, far = planes + 2 * STATE_W, planes + 2 * FINE_W
    pair_counts = [1 + (n > 2) for n in counts]
    groups = [(start_field, START_W), (right_side, FINE_W)]
    first_x = halo_x(groups)
    first_y = halo_y(groups, START_W)
    chi, pooled_chi = call(
        chi_kernel,
        [(1, planes, rows, lanes), (c_planes, c_rows, lanes)],
        [pltpu.VMEM(((slots + 1) * 8, LANES), jnp.float32), pltpu.VMEM((lanes // LANES, rows, LANES), jnp.float32)],
        slot_of, arrived,
    )
    first_x, chi = lax.optimization_barrier((first_x, chi))
    group = [(chi, FINE_W)]
    chi_x = halo_x(group)
    corners = swap("gy", lambda up, n: jnp.concatenate([cut(x, 1, CORNER, up) for x in first_x], axis=0))
    chi_y = halo_y(group, FINE_W, chi_x)
    chi_y, corners = lax.optimization_barrier((chi_y, corners))
    chi_z = halo_z(group, chi_x, [[y] for y in chi_y])
    first_z = halo_z(groups, first_x, list(zip(first_y, corners)))
    c_slabs, s_slabs = 5 * c_planes, 4 * (rows // 8) * (lanes // LANES)
    outers = [[(c_slabs + s_slabs, 8, LANES)], [(4 * (planes + 2), PAD, LANES)], [(4 * (planes + 2) * total // 8, 8, LANES)]]
    outers = [shape * n for shape, n in zip(outers, pair_counts)]
    rhs, state, weight, *sent = call(
        functools.partial(second_kernel, nums=[*pair_counts, pair_counts[0], 2 * pair_counts[1], pair_counts[2], *pair_counts]),
        [(4, far, total, wide), (4, near, total, wide), (far, total, wide), *sum(outers, [])],
        [
            pltpu.VMEM((1, far, total, wide), jnp.float32),
            pltpu.VMEM((4, planes + 2 * START_W, total, wide), jnp.float32),
            pltpu.VMEM((4, far, total, wide), jnp.float32),
            pltpu.VMEM((4, lanes // LANES, rows, LANES), jnp.float32),
            pltpu.VMEM((5, c_planes, c_rows, lanes), jnp.float32),
        ],
        flags, chi, pooled_chi, right_side, start_field, *chi_x, *chi_y, *chi_z, *first_x, *first_y, *corners, *first_z,
    )
    (x_out, y_out, z_out), _ = split(sent, pair_counts)
    group = [(x_out[0][:c_slabs].reshape(5, c_planes, c_rows, c_lanes), COARSE_W)]
    last_x = swap("gx", lambda up, n: x_out[n])
    halo_slabs = [x[:5 * COARSE_W] for x in last_x]
    last_y = halo_y(group, COARSE_W, halo_slabs, y_out)
    slabs = c_slabs + len(last_x) * 5 * COARSE_W
    last_z = halo_z(group, halo_slabs, [[y[:slabs]] for y in last_y], z_out)
    c_ext = (c_planes + 2 * COARSE_W, c_rows + 8, c_lanes + LANES)
    (out,) = call(
        functools.partial(last_kernel, nums=pair_counts),
        [right_side.shape],
        [
            pltpu.VMEM((5, *c_ext), jnp.float32),
            pltpu.VMEM((4, *c_ext), jnp.float32),
            pltpu.VMEM((4, *c_ext), jnp.float32),
            pltpu.VMEM((4, near, total, wide), jnp.float32),
            pltpu.VMEM((4, near, total, wide), jnp.float32),
            pltpu.VMEM((wide // LANES, total, LANES), jnp.float32),
        ],
        flags, x_out[0], state, weight, rhs, *last_x, *last_y, *last_z,
    )
    return out


def solution(mesh):
    in_specs = (
        P(None, "gx", "gy", "lvl"),
        P(None, "gx", "gy", "lvl"),
        P(("gx", "gy", "lvl"), None),
        P(),
        P(),
    )
    out_specs = P(None, "gx", "gy", "lvl")
    return jax.shard_map(body, mesh=mesh, in_specs=in_specs, out_specs=out_specs, check_vma=False)
```

```python
import functools

import jax
import jax.numpy as jnp
from jax import lax
from jax.experimental import pallas as pl
from jax.experimental.pallas import tpu as pltpu
from jax.sharding import PartitionSpec as P

COARSE_SWEEPS = 4
SHIFT = 0.05
RELAX = 0.6
KEEP = 1.0 - RELAX
LANES = 128
START_W = 3
FINE_W = 2
CORNER = 2
STATE_W = 2
COARSE_W = 4
PAD = 4
HIGHEST = lax.Precision.HIGHEST
VMEM = pl.BlockSpec(memory_space=pltpu.VMEM)
SMEM = pl.BlockSpec(memory_space=pltpu.SMEM)
PARAMS = pltpu.CompilerParams(vmem_limit_bytes=24 << 20)


def pairs(count, first):
    return [p for i in range(first, count - 1, 2) for p in ((i, i + 1), (i + 1, i))]


def cut(values, dim, width, to_next):
    size = values.shape[dim]
    if size == width:
        return values
    start = jnp.where(to_next, size - width, 0)
    return lax.dynamic_slice_in_dim(values, start, width, axis=dim)


def flat(parts):
    return jnp.concatenate([p.reshape(-1, *p.shape[-2:]) for p in parts], axis=0)


def swap(axis, message):
    count = lax.axis_size(axis)
    even = lax.axis_index(axis) % 2 == 0
    got = [lax.ppermute(message(even, 0), axis, pairs(count, 0))]
    if count > 2:
        got.append(lax.ppermute(message(~even, 1), axis, pairs(count, 1)))
    return got


def ride(messages, n, extra):
    return jnp.concatenate([*messages, *([extra[n]] if extra else [])], axis=0)


def halo_x(groups):
    return swap("gx", lambda up, n: flat([cut(v, 1, w, up) for v, w in groups]))


def halo_y(groups, depth, xs=(), extra=()):
    own = lambda up: [cut(v.reshape(-1, *v.shape[2:]), 1, depth, up) for v, _ in groups]
    return swap("gy", lambda up, n: ride([*own(up), *[cut(x, 1, depth, up) for x in xs]], n, extra))


def halo_z(groups, xs, ys, extra=()):
    rows = groups[0][0].shape[2]

    def last(up, n):
        sent = [flat([cut(v, 3, LANES, up) for v, _ in groups]), *[cut(x, 2, LANES, up) for x in xs]]
        for parts in ys:
            edge = [jnp.pad(cut(y, 2, LANES, up), ((0, 0), (0, PAD - y.shape[1]), (0, 0))) for y in parts]
            edge = jnp.concatenate(edge, axis=0)
            edge = jnp.pad(edge, ((0, -edge.shape[0] % (rows // PAD)), (0, 0), (0, 0)))
            sent.append(edge.reshape(-1, rows, LANES))
        return ride(sent, n, extra)

    return swap("lvl", last)


def place_halo(dst, margin, own, got, flags, width, depth, group=(0, 0), slabs=None, corner=0, base=(0, 0)):
    xs, ys, zs = got
    rows, lanes = own.shape[-2:]
    fields, planes, total = dst.shape[0], dst.shape[1] - 2 * margin, dst.shape[2]
    own_slabs, x_slabs = slabs or (fields * planes, fields * width)
    pairs_y = len(ys) // 2 if corner else len(ys)
    slab_count = own_slabs + len(xs) * x_slabs
    per = rows // PAD
    even_x, even_y, even_z = flags[0] == 1, flags[1] == 1, flags[2] == 1
    near = (lax.broadcasted_iota(jnp.int32, (1, LANES), 1) < LANES // 2) == even_z

    def edge(at, row, size):
        at, part = base[1] + at, slice(row, row + size)
        return jnp.where(near, zs[0][at, part], 0.0 if len(zs) == 1 else zs[1][at, part])

    for f in range(fields):
        for k in range(planes + len(xs) * width):
            deep = depth
            if k < planes:
                at, plane, slab = margin + k, own[f, k] if len(own.shape) == 4 else own[f * planes + k], group[0] + f * planes + k
            else:
                which, j = divmod(k - planes, width)
                up, down = margin + planes + j, margin - width + j
                at = jnp.where(even_x, up, down) if which == 0 else jnp.where(even_x, down, up)
                plane = xs[which][group[1] + f * width + j]
                slab = own_slabs + which * x_slabs + group[1] + f * width + j
                deep = corner or depth
            dst[f, at, 0:rows, 0:lanes] = plane
            dst[f, at, 0:rows, lanes:] = edge(slab, 0, rows)
            sides = []
            for n in range(pairs_y):
                at_z = slab_count + n * (-(-slab_count // per)) + slab // per
                if corner and k >= planes:
                    y = ys[pairs_y + n][base[0] + slab - own_slabs]
                else:
                    y = ys[n][slab]
                sides.append((y, edge(at_z, slab % per * PAD, deep)))
            if len(sides) == 1:
                sides.append([jnp.zeros_like(v) for v in sides[0]])
            for to, first, second in zip((slice(0, lanes), slice(lanes, lanes + LANES)), *sides):
                dst[f, at, rows:rows + deep, to] = jnp.where(even_y, first, second)
                dst[f, at, total - deep:total, to] = jnp.where(even_y, second, first)
            gap = total - rows - 2 * deep
            if gap:
                dst[f, at, rows + deep:total - deep, :] = jnp.zeros((gap, dst.shape[3]), jnp.float32)


def place_outer(out, state, got, flags, before):
    xs, ys, zs = got
    fields, near, total, wide = state.shape
    planes, rows, lanes = near - 2 * STATE_W, total - 8, wide - LANES
    even_x, even_y, even_z = flags[0] == 1, flags[1] == 1, flags[2] == 1
    side = (lax.broadcasted_iota(jnp.int32, (1, LANES), 1) < LANES // 2) == even_z
    tiles = [(r, z) for r in range(rows // 8) for z in range(lanes // LANES)]
    for f in range(fields):
        for k in range(planes + 2):
            p, slab = STATE_W - 1 + k, f * (planes + 2) + k
            out[f, p, :, 0:lanes] = state[f, p, :, 0:lanes]
            for r in range(total // 8):
                at = before[2] + slab * (total // 8) + r
                z = jnp.where(side, zs[0][at], 0.0 if len(zs) == 1 else zs[1][at])
                out[f, p, r * 8:(r + 1) * 8, lanes:] = z
            for z in range(lanes // LANES):
                part = slice(z * STATE_W, (z + 1) * STATE_W)
                first = ys[0][before[1] + slab, part]
                second = ys[1][before[1] + slab, part] if len(ys) > 1 else jnp.zeros_like(first)
                to = slice(z * LANES, (z + 1) * LANES)
                out[f, p, rows:rows + STATE_W, to] = jnp.where(even_y, first, second)
                out[f, p, total - STATE_W:total, to] = jnp.where(even_y, second, first)
        for p in (0, near - 1):
            out[f, p] = jnp.zeros((total, wide), jnp.float32)
            is_first = even_x if p else ~even_x
            for t, (r, z) in enumerate(tiles):
                at = before[0] + f * len(tiles) + t
                first = xs[0][at]
                second = xs[1][at] if len(xs) > 1 else jnp.zeros_like(first)
                out[f, p, r * 8:(r + 1) * 8, z * LANES:(z + 1) * LANES] = jnp.where(is_first, first, second)


def send_outer(state, flags, x_out, y_out, z_out, before):
    fields, near, total, wide = state.shape
    planes, rows, lanes = near - 2 * STATE_W, total - 8, wide - LANES
    up = [[(flags[a] == 1) == (n == 0) for n in range(2)] for a in range(3)]
    tiles = [(r, z) for r in range(rows // 8) for z in range(lanes // LANES)]
    for n, ref in enumerate(x_out):
        p = jnp.where(up[0][n], STATE_W + planes - 2, STATE_W + 1)
        for f in range(fields):
            for t, (r, z) in enumerate(tiles):
                ref[before + f * len(tiles) + t] = state[f, p, r * 8:(r + 1) * 8, z * LANES:(z + 1) * LANES]
    for f in range(fields):
        for k in range(planes + 2):
            p, slab = STATE_W - 1 + k, f * (planes + 2) + k
            for n, ref in enumerate(y_out):
                v = jnp.where(up[1][n], state[f, p, rows - STATE_W:rows, 0:lanes], state[f, p, 0:STATE_W, 0:lanes])
                for z in range(lanes // LANES):
                    ref[slab, z * STATE_W:(z + 1) * STATE_W] = v[:, z * LANES:(z + 1) * LANES]
            for n, ref in enumerate(z_out):
                for r in range(total // 8):
                    part = slice(r * 8, (r + 1) * 8)
                    v = jnp.where(up[2][n], state[f, p, part, lanes - LANES:lanes], state[f, p, part, 0:LANES])
                    ref[slab * (total // 8) + r] = v


def inside(flags, rows, lanes, total, depth):
    row = lax.broadcasted_iota(jnp.int32, (total, lanes + LANES), 0)
    lane = lax.broadcasted_iota(jnp.int32, (total, lanes + LANES), 1)
    end = lanes + LANES
    row_ok = (row < rows) | ((row < rows + depth) & (flags[5] == 1)) | ((row >= total - depth) & (flags[6] == 1))
    lane_ok = (lane < lanes) | ((lane < lanes + depth) & (flags[7] == 1)) | ((lane >= end - depth) & (flags[8] == 1))
    return jnp.where(row_ok & lane_ok, 1.0, 0.0)


def plane_inside(flags, p, margin, planes):
    return jnp.where(p < margin, flags[4], jnp.where(p >= margin + planes, flags[3], 1)).astype(jnp.float32)


def neighbours(ref, p):
    rows, lanes = ref.shape[2], ref.shape[3]
    sums, grads, spread = [], [], 0.0
    for f in range(4):
        c, xn, xp = ref[f, p], ref[f, p + 1], ref[f, p - 1]
        yn, yp = pltpu.roll(c, rows - 1, 0), pltpu.roll(c, 1, 0)
        zn, zp = pltpu.roll(c, lanes - 1, 1), pltpu.roll(c, 1, 1)
        sums.append((xn + xp) + (yn + yp) + (zn + zp))
        if f == 3:
            grads = [xn - xp, yn - yp, zn - zp]
        else:
            spread = spread + (xn - xp, yn - yp, zn - zp)[f]
    return sums, grads + [spread]


def pack_kernel(tile_ref, mask_ref, out_ref, used_ref, *, capacity):
    tiles = out_ref.shape[0]
    count = mask_ref.shape[0]
    out_ref[...] = jnp.zeros(out_ref.shape, jnp.float32)

    def clear(t, _):
        used_ref[t] = 0
        return 0

    lax.fori_loop(0, tiles, clear, 0)

    def row(r, _):
        t = tile_ref[r]
        n = used_ref[t]
        used_ref[t] = n + 1
        out_ref[t, jnp.minimum(n, capacity - 1)] = mask_ref[r]
        return 0

    lax.fori_loop(0, count, row, 0)


def split(refs, nums):
    at, got = 0, []
    for n in nums:
        got.append(refs[at:at + n])
        at += n
    return got, refs[at:]


def chi_kernel(slot_ref, rows_ref, out, coarse_out, acc, pooled):
    _, planes, rows, lanes = out.shape
    acc[...] = jnp.zeros(acc.shape, jnp.float32)
    per = rows_ref.shape[1]

    def add(s, _):
        for c in range(per):
            at = pl.ds(pl.multiple_of(slot_ref[s * per + c] * 8, 8), 8)
            acc[at, :] = acc[at, :] + rows_ref[s, c]
        return 0

    lax.fori_loop(0, rows_ref.shape[0], add, 0)
    z_tiles = lanes // LANES
    across = rows // 2
    for qx in range(planes // 2):
        for zt in range(z_tiles):
            total = None
            for i in range(2):
                for j in range(2):
                    v = acc[pl.ds(qx * across * 8 + (2 * i + j) * z_tiles + zt, across, stride=8), :]
                    pooled[zt, pl.ds(j, across, stride=2), :] = v
                    total = v if total is None else total + v
                out[0, 2 * qx + i, :, zt * LANES:(zt + 1) * LANES] = pooled[zt]
            coarse_out[qx, :, zt * LANES:(zt + 1) * LANES] = total


def side(up, v, dim, width):
    size = v.shape[dim]
    low = v[..., 0:width] if dim == 1 else v[0:width]
    high = v[..., size - width:] if dim == 1 else v[size - width:]
    return jnp.where(up, high, low)


def y_kernel(flags, *refs, nums):
    (chi_x, first_x), outs = split(refs[1:], [nums[0]] * 2)
    for n, out in enumerate(outs):
        up = (flags[1] == 1) == (n == 0)
        at = 0
        for ref in (refs[0], *chi_x, *first_x):
            for s in range(ref.shape[0]):
                out[at] = side(up, ref[s], 0, out.shape[1])
                at += 1


def z_kernel(flags, *refs, nums):
    (chi, chi_x, start, rhs, first_x, first_y, corners), outs = split(refs, [1, nums[0], 1, 1, nums[0], nums[1], nums[1]])
    rows = chi[0].shape[1]
    per = rows // PAD
    chi_slabs = chi[0].shape[0] + sum(x.shape[0] for x in chi_x)
    for n, out in enumerate(outs):
        up = (flags[2] == 1) == (n == 0)
        at = 0
        for slabs, edges in (
            ((*chi, *chi_x), [[(c, 0, chi_slabs)] for c in corners]),
            ((*start, *rhs, *first_x), [[(y, 0, y.shape[0]), (c, chi_slabs, c.shape[0])] for y, c in zip(first_y, corners)]),
        ):
            for ref in slabs:
                for s in range(ref.shape[0]):
                    out[at] = side(up, ref[s], 1, LANES)
                    at += 1
            for parts in edges:
                k = 0
                for ref, low, high in parts:
                    for s in range(low, high):
                        depth = ref.shape[1]
                        row = k % per * PAD
                        out[at + k // per, row:row + depth] = side(up, ref[s], 1, LANES)
                        out[at + k // per, row + depth:row + PAD] = jnp.zeros((PAD - depth, LANES), jnp.float32)
                        k += 1
                while k % per:
                    row = k % per * PAD
                    out[at + k // per, row:row + PAD] = jnp.zeros((PAD, LANES), jnp.float32)
                    k += 1
                at += k // per


def second_kernel(flags, own, pooled_chi, right_side, start_field, *refs, nums):
    n_x, n_y, n_z = nums
    (chi_x, first_x, first_y, far_y, far_z), refs = split(refs, [n_x, n_x, n_y, n_y, n_z])
    rhs, state_out, weight_out = refs[:3]
    (x_out, y_out, z_out), (chi, start, ext, tmp, pooled) = split(refs[3:], nums)
    _, planes, rows, lanes = own.shape
    total = ext.shape[2]
    chi_slabs = planes + n_x * FINE_W
    base = (chi_slabs, chi_slabs + n_y * -(-chi_slabs // (rows // PAD)))
    slabs = (8 * planes, 4 * (START_W + FINE_W))
    fields_got = (first_x, (*first_y, *far_y), far_z)
    place_halo(chi, FINE_W, own, (chi_x, far_y, far_z), flags, FINE_W, FINE_W)
    place_halo(start, START_W, start_field, fields_got, flags, START_W, START_W, (0, 0), slabs, CORNER, base)
    place_halo(rhs, FINE_W, right_side, fields_got, flags, FINE_W, START_W, (4 * planes, 4 * START_W), slabs, CORNER, base)
    mask = inside(flags, rows, lanes, total, FINE_W)
    w_p = (RELAX / (SHIFT + 6.0)) * mask

    for k in range(planes + 2 * FINE_W):
        here = plane_inside(flags, k, FINE_W, planes)
        w_u = (RELAX / (SHIFT + 6.0 + chi[0, k])) * (mask * here)
        weight_out[k] = w_u
        sums, grads = neighbours(start, k + START_W - FINE_W)
        for f in range(4):
            w = w_u if f < 3 else w_p * here
            ext[f, k] = KEEP * start[f, k + START_W - FINE_W] + w * (rhs[f, k] + sums[f] - 0.5 * grads[f])

    for p in range(1, planes + 2 * FINE_W - 1):
        here = plane_inside(flags, p, FINE_W, planes)
        sums, grads = neighbours(ext, p)
        w_u = weight_out[p]
        for f in range(4):
            w = w_u if f < 3 else w_p * here
            state_out[f, p] = KEEP * ext[f, p] + w * (rhs[f, p] + sums[f] - 0.5 * grads[f])

    for cx in range(planes // 2):
        both = [None] * 4
        for i in range(2):
            p = FINE_W + 2 * cx + i
            sums, grads = neighbours(state_out, p)
            for f in range(4):
                diag = SHIFT + 6.0 + (chi[0, p] if f < 3 else 0.0)
                r = rhs[f, p] + sums[f] - 0.5 * grads[f] - diag * state_out[f, p]
                both[f] = r if i == 0 else both[f] + r
        for f in range(4):
            for zt in range(lanes // LANES):
                tmp[f, zt] = both[f][0:rows, zt * LANES:(zt + 1) * LANES]
                v = tmp[f, zt, pl.ds(0, rows // 2, stride=2), :] + tmp[f, zt, pl.ds(1, rows // 2, stride=2), :]
                pooled[f, cx, :, zt * LANES:(zt + 1) * LANES] = v
    pooled[4] = pooled_chi[...]
    lane = lax.broadcasted_iota(jnp.int32, (lanes, lanes // 2), 0)
    cell = lax.broadcasted_iota(jnp.int32, (lanes, lanes // 2), 1)
    gather = jnp.where(lane // 2 == cell, 0.125, 0.0)
    flat_rows = pooled[...].reshape(5 * planes // 2 * rows // 2, lanes)
    coarse = jnp.dot(flat_rows, gather, precision=HIGHEST, preferred_element_type=jnp.float32)
    coarse = coarse.reshape(5 * planes // 2, rows // 2, lanes // 2)
    for ref in x_out:
        ref[0:coarse.shape[0]] = coarse
    send_outer(state_out, flags, x_out, y_out, z_out, coarse.shape[0])


def last_kernel(flags, own, state, weight, rhs, *refs, nums):
    got, (out, ext, one, two, fine, mid, tmp) = split(refs, nums)
    planes = ext.shape[1] - 2 * COARSE_W
    rows, lanes = own.shape[1:]
    total, wide = ext.shape[2], ext.shape[3]
    own = own.at[0:5 * planes]
    place_halo(ext, COARSE_W, own, got, flags, COARSE_W, COARSE_W)
    x_slabs = 5 * COARSE_W
    slabs = 5 * planes + len(got[0]) * x_slabs
    z_slabs = slabs + len(got[1]) * -(-slabs // (rows // PAD))
    place_outer(fine, state, got, flags, (x_slabs, slabs, z_slabs))
    mask = inside(flags, rows, lanes, total, COARSE_W)
    w_p = (RELAX / (SHIFT + 1.5)) * mask

    for p in range(planes + 2 * COARSE_W):
        here = plane_inside(flags, p, COARSE_W, planes)
        w_u = (RELAX / (SHIFT + 1.5 + ext[4, p])) * (mask * here)
        ext[4, p] = w_u
        for f in range(4):
            one[f, p] = (w_u if f < 3 else w_p * here) * ext[f, p]
    now, then = one, two
    for s in range(1, COARSE_SWEEPS):
        for p in range(s, planes + 2 * COARSE_W - s):
            here = plane_inside(flags, p, COARSE_W, planes)
            sums, grads = neighbours(now, p)
            for f in range(4):
                w = ext[4, p] if f < 3 else w_p * here
                then[f, p] = KEEP * now[f, p] + w * (ext[f, p] + 0.25 * (sums[f] - grads[f]))
        now, then = then, now

    f_total, f_wide = fine.shape[2], fine.shape[3]
    f_rows, f_lanes = 2 * rows, 2 * lanes
    cell = lax.broadcasted_iota(jnp.int32, (wide, f_wide), 0)
    lane = lax.broadcasted_iota(jnp.int32, (wide, f_wide), 1)
    from_cell = jnp.where(lane < f_lanes + LANES // 2, lane // 2, wide - 1 - (f_wide - 1 - lane) // 2)
    spread = jnp.where(cell == from_cell, 1.0, 0.0)
    c_planes = planes + 2
    flat = now[:, COARSE_W - 1:COARSE_W - 1 + c_planes].reshape(4 * c_planes * total, wide)
    grown = jnp.dot(flat, spread, precision=HIGHEST, preferred_element_type=jnp.float32)
    for f in range(4):
        for cp in range(c_planes):
            lo = (f * c_planes + cp) * total
            for zt in range(f_wide // LANES):
                v = grown[lo:lo + total, zt * LANES:(zt + 1) * LANES]
                at = f * c_planes + cp
                for j in range(2):
                    tmp[zt, pl.ds(j, rows, stride=2), :] = v[0:rows]
                    tmp[zt, pl.ds(f_rows + j, 2, stride=2), :] = v[rows:rows + 2]
                    tmp[zt, pl.ds(f_total - 4 + j, 2, stride=2), :] = v[total - 2:total]
                for i in range(2):
                    to = slice(zt * LANES, (zt + 1) * LANES)
                    fine[f, 2 * cp + i, :, to] = fine[f, 2 * cp + i, :, to] + tmp[zt]
    f_planes = 2 * planes
    f_mask = inside(flags, f_rows, f_lanes, f_total, STATE_W)
    off = FINE_W - STATE_W
    w_q = (RELAX / (SHIFT + 6.0)) * f_mask

    for p in range(1, f_planes + 3):
        here = plane_inside(flags, p, STATE_W, f_planes)
        sums, grads = neighbours(fine, p)
        for f in range(4):
            w = weight[p + off] if f < 3 else w_q * here
            mid[f, p] = KEEP * fine[f, p] + w * (rhs[f, p + off] + sums[f] - 0.5 * grads[f])

    for k in range(f_planes):
        p = k + 2
        sums, grads = neighbours(mid, p)
        for f in range(4):
            w = weight[p + off] if f < 3 else w_q
            v = KEEP * mid[f, p] + w * (rhs[f, p + off] + sums[f] - 0.5 * grads[f])
            out[f, k] = v[0:f_rows, 0:f_lanes]


def call(kernel, shapes, scratch, *args, smem=1):
    outs = [jax.ShapeDtypeStruct(s, jnp.float32) for s in shapes]
    return pl.pallas_call(
        kernel,
        out_shape=outs,
        in_specs=[SMEM] * smem + [VMEM] * (len(args) - smem),
        out_specs=[VMEM] * len(outs),
        scratch_shapes=scratch,
        compiler_params=PARAMS,
    )(*args)


def routes(block_tile, block_slot, tiles, count_l, per_device, capacity, slots):
    my_tile = lax.axis_index("gx") * lax.axis_size("gy") + lax.axis_index("gy")
    index_l = lax.axis_index("lvl")
    their_tiles = lax.dynamic_index_in_dim(block_tile.reshape(tiles, count_l, per_device), index_l, 1, keepdims=False)
    their_slots = lax.dynamic_index_in_dim(block_slot.reshape(tiles, count_l, per_device), index_l, 1, keepdims=False)
    arriving = their_tiles == my_tile
    counter = jnp.arange(per_device, dtype=jnp.int32)
    earlier = counter[None, :, None] < counter[None, None, :]
    order = jnp.sum(jnp.where(arriving[:, :, None] & earlier, 1, 0), axis=1)
    places = jnp.arange(capacity, dtype=jnp.int32)
    hit = arriving[:, None, :] & (order[:, None, :] == places[None, :, None])
    slot = jnp.sum(jnp.where(hit, their_slots[:, None, :] - slots, 0), axis=2) + slots
    return slot.reshape(-1)


def body(right_side, start_field, mask_blocks, block_tile, block_slot):
    axes = ("gx", "gy", "lvl")
    counts = [lax.axis_size(a) for a in axes]
    index = [lax.axis_index(a) for a in axes]
    tiles = counts[0] * counts[1]
    per_device, width = mask_blocks.shape
    capacity = max(2, 2 * per_device // tiles)
    _, planes, rows, lanes = right_side.shape
    slots = planes // 2 * (rows // 2)
    c_planes, c_rows, c_lanes = planes // 2, rows // 2, lanes // 2
    flags = [i % 2 == 0 for i in index]
    for i, n in zip(index, counts):
        flags += [i < n - 1, i > 0]
    flags = jnp.stack(flags).astype(jnp.int32)

    my_flat = (index[0] * counts[1] + index[1]) * counts[2] + index[2]
    tile_ids = block_tile[:, 0]
    my_tiles = lax.dynamic_slice_in_dim(tile_ids, my_flat * per_device, per_device)
    (outgoing,) = call(
        functools.partial(pack_kernel, capacity=capacity),
        [(tiles, capacity, width // LANES, LANES)],
        [pltpu.SMEM((tiles,), jnp.int32)],
        my_tiles, mask_blocks.reshape(per_device, width // LANES, LANES),
    )
    outgoing, right_side, start_field = lax.optimization_barrier((outgoing, right_side, start_field))
    arrived = lax.all_to_all(outgoing, ("gx", "gy"), split_axis=0, concat_axis=0, tiled=True)
    slot_of = routes(tile_ids, block_slot, tiles, counts[2], per_device, capacity, slots)

    total, wide = rows + 8, lanes + LANES
    near, far = planes + 2 * STATE_W, planes + 2 * FINE_W
    pair_counts = [1 + (n > 2) for n in counts]
    groups = [(start_field, START_W), (right_side, FINE_W)]
    first_x = halo_x(groups)
    first_y = halo_y(groups, START_W)
    chi, pooled_chi = call(
        chi_kernel,
        [(1, planes, rows, lanes), (c_planes, c_rows, lanes)],
        [pltpu.VMEM(((slots + 1) * 8, LANES), jnp.float32), pltpu.VMEM((lanes // LANES, rows, LANES), jnp.float32)],
        slot_of, arrived,
    )
    group = [(chi, FINE_W)]
    chi_x = halo_x(group)
    first_x, chi_x = lax.optimization_barrier((first_x, chi_x))
    slabs = lambda v: v.reshape(-1, rows, lanes)
    far_x = len(first_x) * 4 * (START_W + FINE_W)
    chi_slabs = planes + len(chi_x) * FINE_W
    y_sent = call(
        functools.partial(y_kernel, nums=pair_counts),
        [(chi_slabs + far_x, CORNER, lanes)] * pair_counts[1],
        [],
        flags, slabs(chi), *chi_x, *first_x,
    )
    far_y = swap("gy", lambda up, n: y_sent[n])
    per = rows // PAD
    edges = -(-chi_slabs // per) + -(-(8 * planes + far_x) // per)
    z_sent = call(
        functools.partial(z_kernel, nums=pair_counts),
        [(chi_slabs + 8 * planes + far_x + pair_counts[1] * edges, rows, LANES)] * pair_counts[2],
        [],
        flags, slabs(chi), *chi_x, slabs(start_field), slabs(right_side), *first_x, *first_y, *far_y,
    )
    far_z = swap("lvl", lambda up, n: z_sent[n])
    c_slabs, s_slabs = 5 * c_planes, 4 * (rows // 8) * (lanes // LANES)
    outers = [[(c_slabs + s_slabs, 8, LANES)], [(4 * (planes + 2), PAD, LANES)], [(4 * (planes + 2) * total // 8, 8, LANES)]]
    outers = [shape * n for shape, n in zip(outers, pair_counts)]
    rhs, state, weight, *sent = call(
        functools.partial(second_kernel, nums=pair_counts),
        [(4, far, total, wide), (4, near, total, wide), (far, total, wide), *sum(outers, [])],
        [
            pltpu.VMEM((1, far, total, wide), jnp.float32),
            pltpu.VMEM((4, planes + 2 * START_W, total, wide), jnp.float32),
            pltpu.VMEM((4, far, total, wide), jnp.float32),
            pltpu.VMEM((4, lanes // LANES, rows, LANES), jnp.float32),
            pltpu.VMEM((5, c_planes, c_rows, lanes), jnp.float32),
        ],
        flags, chi, pooled_chi, right_side, start_field, *chi_x, *first_x, *first_y, *far_y, *far_z,
    )
    (x_out, y_out, z_out), _ = split(sent, pair_counts)
    group = [(x_out[0][:c_slabs].reshape(5, c_planes, c_rows, c_lanes), COARSE_W)]
    last_x = swap("gx", lambda up, n: x_out[n])
    halo_slabs = [x[:5 * COARSE_W] for x in last_x]
    last_y = halo_y(group, COARSE_W, halo_slabs, y_out)
    slabs = c_slabs + len(last_x) * 5 * COARSE_W
    last_z = halo_z(group, halo_slabs, [[y[:slabs]] for y in last_y], z_out)
    c_ext = (c_planes + 2 * COARSE_W, c_rows + 8, c_lanes + LANES)
    (out,) = call(
        functools.partial(last_kernel, nums=pair_counts),
        [right_side.shape],
        [
            pltpu.VMEM((5, *c_ext), jnp.float32),
            pltpu.VMEM((4, *c_ext), jnp.float32),
            pltpu.VMEM((4, *c_ext), jnp.float32),
            pltpu.VMEM((4, near, total, wide), jnp.float32),
            pltpu.VMEM((4, near, total, wide), jnp.float32),
            pltpu.VMEM((wide // LANES, total, LANES), jnp.float32),
        ],
        flags, x_out[0], state, weight, rhs, *last_x, *last_y, *last_z,
    )
    return out


def solution(mesh):
    in_specs = (
        P(None, "gx", "gy", "lvl"),
        P(None, "gx", "gy", "lvl"),
        P(("gx", "gy", "lvl"), None),
        P(),
        P(),
    )
    out_specs = P(None, "gx", "gy", "lvl")
    return jax.shard_map(body, mesh=mesh, in_specs=in_specs, out_specs=out_specs, check_vma=False)
```

```python
import functools

import jax
import jax.numpy as jnp
from jax import lax
from jax.experimental import pallas as pl
from jax.experimental.pallas import tpu as pltpu
from jax.sharding import PartitionSpec as P

COARSE_SWEEPS = 4
SHIFT = 0.05
RELAX = 0.6
KEEP = 1.0 - RELAX
LANES = 128
START_W = 3
FINE_W = 2
CORNER = 2
STATE_W = 2
COARSE_W = 4
PAD = 4
HIGHEST = lax.Precision.HIGHEST
VMEM = pl.BlockSpec(memory_space=pltpu.VMEM)
SMEM = pl.BlockSpec(memory_space=pltpu.SMEM)
PARAMS = pltpu.CompilerParams(vmem_limit_bytes=24 << 20)


def pairs(count, first):
    return [p for i in range(first, count - 1, 2) for p in ((i, i + 1), (i + 1, i))]


def cut(values, dim, width, to_next):
    size = values.shape[dim]
    if size == width:
        return values
    start = jnp.where(to_next, size - width, 0)
    return lax.dynamic_slice_in_dim(values, start, width, axis=dim)


def flat(parts):
    return jnp.concatenate([p.reshape(-1, *p.shape[-2:]) for p in parts], axis=0)


def swap(axis, message):
    count = lax.axis_size(axis)
    even = lax.axis_index(axis) % 2 == 0
    got = [lax.ppermute(message(~even, 1), axis, pairs(count, 1))] if count > 2 else []
    got.insert(0, lax.ppermute(message(even, 0), axis, pairs(count, 0)))
    return got


def halo_x(groups):
    return swap("gx", lambda up, n: flat([cut(v, 1, w, up) for v, w in groups]))


def place_halo(dst, margin, own, got, flags, width, depth, group=(0, 0), slabs=None, corner=0, base=(0, 0), early=()):
    xs, ys, zs = got
    rows, lanes = own.shape[-2:]
    fields, planes, total = dst.shape[0], dst.shape[1] - 2 * margin, dst.shape[2]
    own_slabs, x_slabs = slabs or (fields * planes, fields * width)
    pairs_y = len(ys) // 2 if corner else len(ys)
    slab_count = own_slabs + len(xs) * x_slabs
    per = rows // PAD
    even_x, even_y, even_z = flags[0] == 1, flags[1] == 1, flags[2] == 1
    near = (lax.broadcasted_iota(jnp.int32, (1, LANES), 1) < LANES // 2) == even_z

    def edge(at, row, size):
        part = slice(row, row + size)
        if early and at < own_slabs:
            return jnp.where(near, early[0][at, part], 0.0 if len(zs) == 1 else early[1][at, part])
        at = base[1] + at - (own_slabs if early else 0)
        return jnp.where(near, zs[0][at, part], 0.0 if len(zs) == 1 else zs[1][at, part])

    for f in range(fields):
        for k in range(planes + len(xs) * width):
            deep = depth
            if k < planes:
                at, plane, slab = margin + k, own[f, k] if len(own.shape) == 4 else own[f * planes + k], group[0] + f * planes + k
            else:
                which, j = divmod(k - planes, width)
                up, down = margin + planes + j, margin - width + j
                at = jnp.where(even_x, up, down) if which == 0 else jnp.where(even_x, down, up)
                plane = xs[which][group[1] + f * width + j]
                slab = own_slabs + which * x_slabs + group[1] + f * width + j
                deep = corner or depth
            dst[f, at, 0:rows, 0:lanes] = plane
            dst[f, at, 0:rows, lanes:] = edge(slab, 0, rows)
            sides = []
            for n in range(pairs_y):
                at_z = slab_count + n * (-(-slab_count // per)) + slab // per
                if corner and k >= planes:
                    y = ys[pairs_y + n][base[0] + slab - own_slabs]
                else:
                    y = ys[n][slab]
                sides.append((y, edge(at_z, slab % per * PAD, deep)))
            if len(sides) == 1:
                sides.append([jnp.zeros_like(v) for v in sides[0]])
            for to, first, second in zip((slice(0, lanes), slice(lanes, lanes + LANES)), *sides):
                dst[f, at, rows:rows + deep, to] = jnp.where(even_y, first, second)
                dst[f, at, total - deep:total, to] = jnp.where(even_y, second, first)
            gap = total - rows - 2 * deep
            if gap:
                dst[f, at, rows + deep:total - deep, :] = jnp.zeros((gap, dst.shape[3]), jnp.float32)


def place_outer(out, state, got, flags, before):
    xs, ys, zs = got
    fields, near, total, wide = state.shape
    planes, rows, lanes = near - 2 * STATE_W, total - 8, wide - LANES
    even_x, even_y, even_z = flags[0] == 1, flags[1] == 1, flags[2] == 1
    side = (lax.broadcasted_iota(jnp.int32, (1, LANES), 1) < LANES // 2) == even_z
    tiles = [(r, z) for r in range(rows // 8) for z in range(lanes // LANES)]
    for f in range(fields):
        for k in range(planes + 2):
            p, slab = STATE_W - 1 + k, f * (planes + 2) + k
            out[f, p, :, 0:lanes] = state[f, p, :, 0:lanes]
            for r in range(total // 8):
                at = before[2] + slab * (total // 8) + r
                z = jnp.where(side, zs[0][at], 0.0 if len(zs) == 1 else zs[1][at])
                out[f, p, r * 8:(r + 1) * 8, lanes:] = z
            for z in range(lanes // LANES):
                part = slice(z * STATE_W, (z + 1) * STATE_W)
                first = ys[0][before[1] + slab, part]
                second = ys[1][before[1] + slab, part] if len(ys) > 1 else jnp.zeros_like(first)
                to = slice(z * LANES, (z + 1) * LANES)
                out[f, p, rows:rows + STATE_W, to] = jnp.where(even_y, first, second)
                out[f, p, total - STATE_W:total, to] = jnp.where(even_y, second, first)
        for p in (0, near - 1):
            out[f, p] = jnp.zeros((total, wide), jnp.float32)
            is_first = even_x if p else ~even_x
            for t, (r, z) in enumerate(tiles):
                at = before[0] + f * len(tiles) + t
                first = xs[0][at]
                second = xs[1][at] if len(xs) > 1 else jnp.zeros_like(first)
                out[f, p, r * 8:(r + 1) * 8, z * LANES:(z + 1) * LANES] = jnp.where(is_first, first, second)


def send_outer(state, flags, x_out, y_out, z_out, before):
    fields, near, total, wide = state.shape
    planes, rows, lanes = near - 2 * STATE_W, total - 8, wide - LANES
    up = [[(flags[a] == 1) == (n == 0) for n in range(2)] for a in range(3)]
    tiles = [(r, z) for r in range(rows // 8) for z in range(lanes // LANES)]
    for n, ref in enumerate(x_out):
        p = jnp.where(up[0][n], STATE_W + planes - 2, STATE_W + 1)
        for f in range(fields):
            for t, (r, z) in enumerate(tiles):
                ref[before + f * len(tiles) + t] = state[f, p, r * 8:(r + 1) * 8, z * LANES:(z + 1) * LANES]
    for f in range(fields):
        for k in range(planes + 2):
            p, slab = STATE_W - 1 + k, f * (planes + 2) + k
            for n, ref in enumerate(y_out):
                v = jnp.where(up[1][n], state[f, p, rows - STATE_W:rows, 0:lanes], state[f, p, 0:STATE_W, 0:lanes])
                for z in range(lanes // LANES):
                    ref[slab, z * STATE_W:(z + 1) * STATE_W] = v[:, z * LANES:(z + 1) * LANES]
            for n, ref in enumerate(z_out):
                for r in range(total // 8):
                    part = slice(r * 8, (r + 1) * 8)
                    v = jnp.where(up[2][n], state[f, p, part, lanes - LANES:lanes], state[f, p, part, 0:LANES])
                    ref[slab * (total // 8) + r] = v


def inside(flags, rows, lanes, total, depth):
    row = lax.broadcasted_iota(jnp.int32, (total, lanes + LANES), 0)
    lane = lax.broadcasted_iota(jnp.int32, (total, lanes + LANES), 1)
    end = lanes + LANES
    row_ok = (row < rows) | ((row < rows + depth) & (flags[5] == 1)) | ((row >= total - depth) & (flags[6] == 1))
    lane_ok = (lane < lanes) | ((lane < lanes + depth) & (flags[7] == 1)) | ((lane >= end - depth) & (flags[8] == 1))
    return jnp.where(row_ok & lane_ok, 1.0, 0.0)


def plane_inside(flags, p, margin, planes):
    return jnp.where(p < margin, flags[4], jnp.where(p >= margin + planes, flags[3], 1)).astype(jnp.float32)


def neighbours(ref, p):
    rows, lanes = ref.shape[2], ref.shape[3]
    sums, grads, spread = [], [], 0.0
    for f in range(4):
        c, xn, xp = ref[f, p], ref[f, p + 1], ref[f, p - 1]
        yn, yp = pltpu.roll(c, rows - 1, 0), pltpu.roll(c, 1, 0)
        zn, zp = pltpu.roll(c, lanes - 1, 1), pltpu.roll(c, 1, 1)
        sums.append((xn + xp) + (yn + yp) + (zn + zp))
        if f == 3:
            grads = [xn - xp, yn - yp, zn - zp]
        else:
            spread = spread + (xn - xp, yn - yp, zn - zp)[f]
    return sums, grads + [spread]


def pack_kernel(tile_ref, mask_ref, out_ref, used_ref, rows_ref, *, capacity):
    tiles = out_ref.shape[0]
    count, width = mask_ref.shape
    out_ref[...] = jnp.zeros(out_ref.shape, jnp.float32)
    for r in range(0, count, 8):
        rows_ref[r:r + 8] = mask_ref[r:r + 8].reshape(8, width // LANES, LANES)

    def clear(t, _):
        used_ref[t] = 0
        return 0

    lax.fori_loop(0, tiles, clear, 0, unroll=8)

    def row(r, _):
        t = tile_ref[r]
        n = used_ref[t]
        used_ref[t] = n + 1
        out_ref[t, jnp.minimum(n, capacity - 1)] = rows_ref[r]
        return 0

    lax.fori_loop(0, count, row, 0, unroll=8)


def split(refs, nums):
    at, got = 0, []
    for n in nums:
        got.append(refs[at:at + n])
        at += n
    return got, refs[at:]


def chi_kernel(slot_ref, rows_ref, out, coarse_out, acc, pooled):
    _, planes, rows, lanes = out.shape
    acc[...] = jnp.zeros(acc.shape, jnp.float32)
    per = rows_ref.shape[1]

    def add(s, _):
        for c in range(per):
            at = pl.ds(pl.multiple_of(slot_ref[s * per + c] * 8, 8), 8)
            acc[at, :] = acc[at, :] + rows_ref[s, c]
        return 0

    lax.fori_loop(0, rows_ref.shape[0], add, 0)
    z_tiles = lanes // LANES
    across = rows // 2
    for qx in range(planes // 2):
        for zt in range(z_tiles):
            total = None
            for i in range(2):
                for j in range(2):
                    v = acc[pl.ds(qx * across * 8 + (2 * i + j) * z_tiles + zt, across, stride=8), :]
                    pooled[zt, pl.ds(j, across, stride=2), :] = v
                    total = v if total is None else total + v
                out[0, 2 * qx + i, :, zt * LANES:(zt + 1) * LANES] = pooled[zt]
            coarse_out[qx, :, zt * LANES:(zt + 1) * LANES] = total


def side(up, v, dim, width):
    size = v.shape[dim]
    low = v[..., 0:width] if dim == 1 else v[0:width]
    high = v[..., size - width:] if dim == 1 else v[size - width:]
    return jnp.where(up, high, low)


def y_kernel(flags, *refs, take, order, added):
    ready, (_, *outs) = split(refs[len(take):], [added])
    for n, out in enumerate(outs):
        up = (flags[1] == 1) == (n == 0)
        at = 0
        for i in order:
            ref, count = refs[i], take[i]
            for s in range(count):
                out[at] = side(up, ref[s], 0, out.shape[1])
                at += 1
        if added:
            out[at:] = ready[0][n][...]


def z_kernel(flags, *refs, plan, count, added):
    ready, outs = split(refs[count:], [added])
    for n, out in enumerate(outs):
        up = (flags[2] == 1) == (n == 0)
        per = out.shape[1] // PAD
        at = 0
        for slabs, edges in plan:
            for i, low, high in slabs:
                for s in range(low, high):
                    out[at] = side(up, refs[i][s], 1, LANES)
                    at += 1
            for parts in edges:
                k = 0
                for i, low, high in parts:
                    for s in range(low, high):
                        depth = refs[i].shape[1]
                        row = k % per * PAD
                        out[at + k // per, row:row + depth] = side(up, refs[i][s], 1, LANES)
                        if depth < PAD:
                            out[at + k // per, row + depth:row + PAD] = jnp.zeros((PAD - depth, LANES), jnp.float32)
                        k += 1
                while k % per:
                    row = k % per * PAD
                    out[at + k // per, row:row + PAD] = jnp.zeros((PAD, LANES), jnp.float32)
                    k += 1
                at += k // per
        if added:
            out[at:] = ready[0][n][...]


def second_kernel(flags, own, pooled_chi, right_side, start_field, *refs, nums):
    n_x, n_y, n_z = nums
    (chi_x, first_x, first_y, first_z, far_y, far_z), refs = split(refs, [n_x, n_x, n_y, n_z, n_y, n_z])
    rhs, state_out, weight_out = refs[:3]
    (x_out, y_out, z_out), (chi, start, ext, tmp, pooled) = split(refs[3:], nums)
    _, planes, rows, lanes = own.shape
    total = ext.shape[2]
    chi_slabs = planes + n_x * FINE_W
    base = (chi_slabs, chi_slabs + n_y * -(-chi_slabs // (rows // PAD)))
    slabs = (8 * planes, 4 * (START_W + FINE_W))
    fields_got = (first_x, (*first_y, *far_y), far_z)
    place_halo(chi, FINE_W, own, (chi_x, far_y, far_z), flags, FINE_W, FINE_W)
    place_halo(start, START_W, start_field, fields_got, flags, START_W, START_W, (0, 0), slabs, CORNER, base, first_z)
    place_halo(rhs, FINE_W, right_side, fields_got, flags, FINE_W, START_W, (4 * planes, 4 * START_W), slabs, CORNER, base, first_z)
    mask = inside(flags, rows, lanes, total, FINE_W)
    w_p = (RELAX / (SHIFT + 6.0)) * mask

    for k in range(planes + 2 * FINE_W):
        here = plane_inside(flags, k, FINE_W, planes)
        w_u = (RELAX / (SHIFT + 6.0 + chi[0, k])) * (mask * here)
        weight_out[k] = w_u
        sums, grads = neighbours(start, k + START_W - FINE_W)
        for f in range(4):
            w = w_u if f < 3 else w_p * here
            ext[f, k] = KEEP * start[f, k + START_W - FINE_W] + w * (rhs[f, k] + sums[f] - 0.5 * grads[f])

    for p in range(1, planes + 2 * FINE_W - 1):
        here = plane_inside(flags, p, FINE_W, planes)
        sums, grads = neighbours(ext, p)
        w_u = weight_out[p]
        for f in range(4):
            w = w_u if f < 3 else w_p * here
            state_out[f, p] = KEEP * ext[f, p] + w * (rhs[f, p] + sums[f] - 0.5 * grads[f])

    for cx in range(planes // 2):
        both = [None] * 4
        for i in range(2):
            p = FINE_W + 2 * cx + i
            sums, grads = neighbours(state_out, p)
            for f in range(4):
                diag = SHIFT + 6.0 + (chi[0, p] if f < 3 else 0.0)
                r = rhs[f, p] + sums[f] - 0.5 * grads[f] - diag * state_out[f, p]
                both[f] = r if i == 0 else both[f] + r
        for f in range(4):
            for zt in range(lanes // LANES):
                tmp[f, zt] = both[f][0:rows, zt * LANES:(zt + 1) * LANES]
                v = tmp[f, zt, pl.ds(0, rows // 2, stride=2), :] + tmp[f, zt, pl.ds(1, rows // 2, stride=2), :]
                pooled[f, cx, :, zt * LANES:(zt + 1) * LANES] = v
    pooled[4] = pooled_chi[...]
    lane = lax.broadcasted_iota(jnp.int32, (lanes, lanes // 2), 0)
    cell = lax.broadcasted_iota(jnp.int32, (lanes, lanes // 2), 1)
    gather = jnp.where(lane // 2 == cell, 0.125, 0.0)
    flat_rows = pooled[...].reshape(5 * planes // 2 * rows // 2, lanes)
    coarse = jnp.dot(flat_rows, gather, precision=HIGHEST, preferred_element_type=jnp.float32)
    coarse = coarse.reshape(5 * planes // 2, rows // 2, lanes // 2)
    for ref in x_out:
        ref[0:coarse.shape[0]] = coarse
    send_outer(state_out, flags, x_out, y_out, z_out, coarse.shape[0])


def last_kernel(flags, own, state, weight, rhs, *refs, nums):
    got, (out, ext, one, two, fine, mid, tmp) = split(refs, nums)
    planes = ext.shape[1] - 2 * COARSE_W
    rows, lanes = own.shape[1:]
    total, wide = ext.shape[2], ext.shape[3]
    own = own.at[0:5 * planes]
    place_halo(ext, COARSE_W, own, got[:3], flags, COARSE_W, COARSE_W)
    x_slabs = 5 * COARSE_W
    slabs = 5 * planes + len(got[0]) * x_slabs
    z_slabs = slabs + len(got[1]) * -(-slabs // (rows // PAD))
    place_outer(fine, state, got, flags, (x_slabs, slabs, z_slabs))
    mask = inside(flags, rows, lanes, total, COARSE_W)
    w_p = (RELAX / (SHIFT + 1.5)) * mask

    for p in range(planes + 2 * COARSE_W):
        here = plane_inside(flags, p, COARSE_W, planes)
        w_u = (RELAX / (SHIFT + 1.5 + ext[4, p])) * (mask * here)
        ext[4, p] = w_u
        for f in range(4):
            one[f, p] = (w_u if f < 3 else w_p * here) * ext[f, p]
    now, then = one, two
    for s in range(1, COARSE_SWEEPS):
        for p in range(s, planes + 2 * COARSE_W - s):
            here = plane_inside(flags, p, COARSE_W, planes)
            sums, grads = neighbours(now, p)
            for f in range(4):
                w = ext[4, p] if f < 3 else w_p * here
                then[f, p] = KEEP * now[f, p] + w * (ext[f, p] + 0.25 * (sums[f] - grads[f]))
        now, then = then, now

    f_total, f_wide = fine.shape[2], fine.shape[3]
    f_rows, f_lanes = 2 * rows, 2 * lanes
    cell = lax.broadcasted_iota(jnp.int32, (wide, f_wide), 0)
    lane = lax.broadcasted_iota(jnp.int32, (wide, f_wide), 1)
    from_cell = jnp.where(lane < f_lanes + LANES // 2, lane // 2, wide - 1 - (f_wide - 1 - lane) // 2)
    spread = jnp.where(cell == from_cell, 1.0, 0.0)
    c_planes = planes + 2
    flat = now[:, COARSE_W - 1:COARSE_W - 1 + c_planes].reshape(4 * c_planes * total, wide)
    grown = jnp.dot(flat, spread, precision=HIGHEST, preferred_element_type=jnp.float32)
    for f in range(4):
        for cp in range(c_planes):
            lo = (f * c_planes + cp) * total
            for zt in range(f_wide // LANES):
                v = grown[lo:lo + total, zt * LANES:(zt + 1) * LANES]
                at = f * c_planes + cp
                for j in range(2):
                    tmp[zt, pl.ds(j, rows, stride=2), :] = v[0:rows]
                    tmp[zt, pl.ds(f_rows + j, 2, stride=2), :] = v[rows:rows + 2]
                    tmp[zt, pl.ds(f_total - 4 + j, 2, stride=2), :] = v[total - 2:total]
                for i in range(2):
                    to = slice(zt * LANES, (zt + 1) * LANES)
                    fine[f, 2 * cp + i, :, to] = fine[f, 2 * cp + i, :, to] + tmp[zt]
    f_planes = 2 * planes
    f_mask = inside(flags, f_rows, f_lanes, f_total, STATE_W)
    off = FINE_W - STATE_W
    w_q = (RELAX / (SHIFT + 6.0)) * f_mask

    for p in range(1, f_planes + 3):
        here = plane_inside(flags, p, STATE_W, f_planes)
        sums, grads = neighbours(fine, p)
        for f in range(4):
            w = weight[p + off] if f < 3 else w_q * here
            mid[f, p] = KEEP * fine[f, p] + w * (rhs[f, p + off] + sums[f] - 0.5 * grads[f])

    for k in range(f_planes):
        p = k + 2
        sums, grads = neighbours(mid, p)
        for f in range(4):
            w = weight[p + off] if f < 3 else w_q
            v = KEEP * mid[f, p] + w * (rhs[f, p + off] + sums[f] - 0.5 * grads[f])
            out[f, k] = v[0:f_rows, 0:f_lanes]


def call(kernel, shapes, scratch, *args, smem=1):
    outs = [jax.ShapeDtypeStruct(s, jnp.float32) for s in shapes]
    return pl.pallas_call(
        kernel,
        out_shape=outs,
        in_specs=[SMEM] * smem + [VMEM] * (len(args) - smem),
        out_specs=[VMEM] * len(outs),
        scratch_shapes=scratch,
        compiler_params=PARAMS,
    )(*args)


def routes(block_tile, block_slot, tiles, count_l, per_device, capacity, slots):
    my_tile = lax.axis_index("gx") * lax.axis_size("gy") + lax.axis_index("gy")
    index_l = lax.axis_index("lvl")
    their_tiles = lax.dynamic_index_in_dim(block_tile.reshape(tiles, count_l, per_device), index_l, 1, keepdims=False)
    their_slots = lax.dynamic_index_in_dim(block_slot.reshape(tiles, count_l, per_device), index_l, 1, keepdims=False)
    arriving = their_tiles == my_tile
    counter = jnp.arange(per_device, dtype=jnp.int32)
    earlier = counter[None, :, None] < counter[None, None, :]
    order = jnp.sum(jnp.where(arriving[:, :, None] & earlier, 1, 0), axis=1)
    places = jnp.arange(capacity, dtype=jnp.int32)
    hit = arriving[:, None, :] & (order[:, None, :] == places[None, :, None])
    slot = jnp.sum(jnp.where(hit, their_slots[:, None, :] - slots, 0), axis=2) + slots
    return slot.reshape(-1)


def body(right_side, start_field, mask_blocks, block_tile, block_slot):
    axes = ("gx", "gy", "lvl")
    counts = [lax.axis_size(a) for a in axes]
    index = [lax.axis_index(a) for a in axes]
    tiles = counts[0] * counts[1]
    per_device, width = mask_blocks.shape
    capacity = max(2, 2 * per_device // tiles)
    _, planes, rows, lanes = right_side.shape
    slots = planes // 2 * (rows // 2)
    c_planes, c_rows, c_lanes = planes // 2, rows // 2, lanes // 2
    flags = [i % 2 == 0 for i in index]
    for i, n in zip(index, counts):
        flags += [i < n - 1, i > 0]
    flags = jnp.stack(flags).astype(jnp.int32)

    my_flat = (index[0] * counts[1] + index[1]) * counts[2] + index[2]
    tile_ids = block_tile[:, 0]
    my_tiles = lax.dynamic_slice_in_dim(tile_ids, my_flat * per_device, per_device)
    (outgoing,) = call(
        functools.partial(pack_kernel, capacity=capacity),
        [(tiles, capacity, width // LANES, LANES)],
        [pltpu.SMEM((tiles,), jnp.int32), pltpu.VMEM((per_device, width // LANES, LANES), jnp.float32)],
        my_tiles, mask_blocks,
    )
    outgoing, right_side, start_field = lax.optimization_barrier((outgoing, right_side, start_field))
    arrived = lax.all_to_all(outgoing, ("gx", "gy"), split_axis=0, concat_axis=0, tiled=True)
    slot_of = routes(tile_ids, block_slot, tiles, counts[2], per_device, capacity, slots)

    total, wide = rows + 8, lanes + LANES
    near, far = planes + 2 * STATE_W, planes + 2 * FINE_W
    pair_counts = [1 + (n > 2) for n in counts]
    groups = [(start_field, START_W), (right_side, FINE_W)]
    first_x = halo_x(groups)
    first_y = swap("gy", lambda up, n: flat([cut(v, 2, START_W, up) for v, _ in groups]))
    first_z = swap("lvl", lambda up, n: flat([cut(v, 3, LANES, up) for v, _ in groups]))
    first_y, first_z, slot_of = lax.optimization_barrier((first_y, first_z, slot_of))
    chi, pooled_chi = call(
        chi_kernel,
        [(1, planes, rows, lanes), (c_planes, c_rows, lanes)],
        [pltpu.VMEM(((slots + 1) * 8, LANES), jnp.float32), pltpu.VMEM((lanes // LANES, rows, LANES), jnp.float32)],
        slot_of, arrived,
    )
    group = [(chi, FINE_W)]
    chi_x = halo_x(group)
    first_x, chi_x = lax.optimization_barrier((first_x, chi_x))
    slabs = lambda v: v.reshape(-1, rows, lanes)
    far_x = len(first_x) * 4 * (START_W + FINE_W)
    chi_slabs = planes + len(chi_x) * FINE_W
    n_x, n_y, n_z = pair_counts
    y_sent = call(
        functools.partial(
            y_kernel,
            take=[planes, *[x.shape[0] for x in (*chi_x[::-1], *first_x[::-1])]],
            order=[0, *range(n_x, 0, -1), *range(2 * n_x, n_x, -1)],
            added=0,
        ),
        [(chi_slabs + far_x, CORNER, lanes)] * n_y,
        [],
        flags, slabs(chi), *chi_x[::-1], *first_x[::-1], chi_x[0][0, :1, :LANES],
    )
    far_y = swap("gy", lambda up, n: y_sent[n])
    per = rows // PAD
    edges = -(-chi_slabs // per) + -(-(8 * planes + far_x) // per)
    whole = lambda first, refs: [(first + i, 0, r.shape[0]) for i, r in enumerate(refs)]
    far_at = 1 + 2 * n_x + n_y
    plan = [
        ([(0, 0, planes), *whole(1, chi_x)], [[(far_at + n, 0, chi_slabs)] for n in range(n_y)]),
        (
            whole(1 + n_x, first_x),
            [[(1 + 2 * n_x + n, 0, 8 * planes), (far_at + n, chi_slabs, chi_slabs + far_x)] for n in range(n_y)],
        ),
    ]
    z_sent = call(
        functools.partial(z_kernel, plan=plan, count=far_at + n_y, added=0),
        [(chi_slabs + far_x + n_y * edges, rows, LANES)] * n_z,
        [],
        flags, slabs(chi), *chi_x, *first_x, *first_y, *far_y,
    )
    far_z = swap("lvl", lambda up, n: z_sent[n])
    c_slabs, s_slabs = 5 * c_planes, 4 * (rows // 8) * (lanes // LANES)
    outers = [[(c_slabs + s_slabs, 8, LANES)], [(4 * (planes + 2), PAD, LANES)], [(4 * (planes + 2) * total // 8, 8, LANES)]]
    outers = [shape * n for shape, n in zip(outers, pair_counts)]
    rhs, state, weight, *sent = call(
        functools.partial(second_kernel, nums=pair_counts),
        [(4, far, total, wide), (4, near, total, wide), (far, total, wide), *sum(outers, [])],
        [
            pltpu.VMEM((1, far, total, wide), jnp.float32),
            pltpu.VMEM((4, planes + 2 * START_W, total, wide), jnp.float32),
            pltpu.VMEM((4, far, total, wide), jnp.float32),
            pltpu.VMEM((4, lanes // LANES, rows, LANES), jnp.float32),
            pltpu.VMEM((5, c_planes, c_rows, lanes), jnp.float32),
        ],
        flags, chi, pooled_chi, right_side, start_field, *chi_x, *first_x, *first_y, *first_z, *far_y, *far_z,
    )
    (x_out, y_out, z_out), _ = split(sent, pair_counts)
    last_x = swap("gx", lambda up, n: x_out[n])
    take = [c_slabs, *[5 * COARSE_W] * n_x]
    y_sent = call(
        functools.partial(y_kernel, take=take, order=[0, *range(n_x, 0, -1)], added=n_y),
        [(sum(take) + y_out[0].shape[0], COARSE_W, c_lanes)] * n_y,
        [],
        flags, x_out[0], *last_x[::-1], *y_out, last_x[0][0, :1, :LANES],
    )
    last_y = swap("gy", lambda up, n: y_sent[n])
    plan = [([(i, 0, t) for i, t in enumerate(take)], [[(1 + n_x + n, 0, sum(take))] for n in range(n_y)])]
    z_slabs = sum(take) + n_y * -(-sum(take) // (c_rows // PAD))
    z_sent = call(
        functools.partial(z_kernel, plan=plan, count=1 + n_x + n_y, added=n_z),
        [(z_slabs + z_out[0].shape[0], c_rows, LANES)] * n_z,
        [],
        flags, x_out[0], *last_x, *last_y, *z_out,
    )
    last_z = swap("lvl", lambda up, n: z_sent[n])
    c_ext = (c_planes + 2 * COARSE_W, c_rows + 8, c_lanes + LANES)
    (out,) = call(
        functools.partial(last_kernel, nums=pair_counts),
        [right_side.shape],
        [
            pltpu.VMEM((5, *c_ext), jnp.float32),
            pltpu.VMEM((4, *c_ext), jnp.float32),
            pltpu.VMEM((4, *c_ext), jnp.float32),
            pltpu.VMEM((4, near, total, wide), jnp.float32),
            pltpu.VMEM((4, near, total, wide), jnp.float32),
            pltpu.VMEM((wide // LANES, total, LANES), jnp.float32),
        ],
        flags, x_out[0], state, weight, rhs, *last_x, *last_y, *last_z,
    )
    return out


def solution(mesh):
    in_specs = (
        P(None, "gx", "gy", "lvl"),
        P(None, "gx", "gy", "lvl"),
        P(("gx", "gy", "lvl"), None),
        P(),
        P(),
    )
    out_specs = P(None, "gx", "gy", "lvl")
    return jax.shard_map(body, mesh=mesh, in_specs=in_specs, out_specs=out_specs, check_vma=False)
```

```python
import functools

import jax
import jax.numpy as jnp
from jax import lax
from jax.experimental import pallas as pl
from jax.experimental.pallas import tpu as pltpu
from jax.sharding import PartitionSpec as P

COARSE_SWEEPS = 4
SHIFT = 0.05
RELAX = 0.6
KEEP = 1.0 - RELAX
LANES = 128
START_W = 3
FINE_W = 2
CORNER = 2
STATE_W = 2
COARSE_W = 4
PAD = 4
HIGHEST = lax.Precision.HIGHEST
VMEM = pl.BlockSpec(memory_space=pltpu.VMEM)
SMEM = pl.BlockSpec(memory_space=pltpu.SMEM)
PARAMS = pltpu.CompilerParams(vmem_limit_bytes=24 << 20)


def pairs(count, first):
    return [p for i in range(first, count - 1, 2) for p in ((i, i + 1), (i + 1, i))]


def cut(values, dim, width, to_next):
    size = values.shape[dim]
    if size == width:
        return values
    start = jnp.where(to_next, size - width, 0)
    return lax.dynamic_slice_in_dim(values, start, width, axis=dim)


def flat(parts):
    return jnp.concatenate([p.reshape(-1, *p.shape[-2:]) for p in parts], axis=0)


def swap(axis, message):
    count = lax.axis_size(axis)
    even = lax.axis_index(axis) % 2 == 0
    got = [lax.ppermute(message(~even, 1), axis, pairs(count, 1))] if count > 2 else []
    got.insert(0, lax.ppermute(message(even, 0), axis, pairs(count, 0)))
    return got


def halo_x(groups):
    return swap("gx", lambda up, n: flat([cut(v, 1, w, up) for v, w in groups]))


def place_halo(dst, margin, own, got, flags, width, depth, group=(0, 0), slabs=None, corner=0, base=(0, 0), early=()):
    xs, ys, zs = got
    rows, lanes = own.shape[-2:]
    fields, planes, total = dst.shape[0], dst.shape[1] - 2 * margin, dst.shape[2]
    own_slabs, x_slabs = slabs or (fields * planes, fields * width)
    pairs_y = len(ys) // 2 if corner else len(ys)
    slab_count = own_slabs + len(xs) * x_slabs
    per = rows // PAD
    even_x, even_y, even_z = flags[0] == 1, flags[1] == 1, flags[2] == 1
    near = (lax.broadcasted_iota(jnp.int32, (1, LANES), 1) < LANES // 2) == even_z

    def edge(at, row, size):
        part = slice(row, row + size)
        if early and at < own_slabs:
            return jnp.where(near, early[0][at, part], 0.0 if len(zs) == 1 else early[1][at, part])
        at = base[1] + at - (own_slabs if early else 0)
        return jnp.where(near, zs[0][at, part], 0.0 if len(zs) == 1 else zs[1][at, part])

    for f in range(fields):
        for k in range(planes + len(xs) * width):
            deep = depth
            if k < planes:
                at, plane, slab = margin + k, own[f, k] if len(own.shape) == 4 else own[f * planes + k], group[0] + f * planes + k
            else:
                which, j = divmod(k - planes, width)
                up, down = margin + planes + j, margin - width + j
                at = jnp.where(even_x, up, down) if which == 0 else jnp.where(even_x, down, up)
                plane = xs[which][group[1] + f * width + j]
                slab = own_slabs + which * x_slabs + group[1] + f * width + j
                deep = corner or depth
            dst[f, at, 0:rows, 0:lanes] = plane
            dst[f, at, 0:rows, lanes:] = edge(slab, 0, rows)
            sides = []
            for n in range(pairs_y):
                at_z = slab_count + n * (-(-slab_count // per)) + slab // per
                if corner and k >= planes:
                    y = ys[pairs_y + n][base[0] + slab - own_slabs]
                else:
                    y = ys[n][slab]
                sides.append((y, edge(at_z, slab % per * PAD, deep)))
            if len(sides) == 1:
                sides.append([jnp.zeros_like(v) for v in sides[0]])
            for to, first, second in zip((slice(0, lanes), slice(lanes, lanes + LANES)), *sides):
                dst[f, at, rows:rows + deep, to] = jnp.where(even_y, first, second)
                dst[f, at, total - deep:total, to] = jnp.where(even_y, second, first)
            gap = total - rows - 2 * deep
            if gap:
                dst[f, at, rows + deep:total - deep, :] = jnp.zeros((gap, dst.shape[3]), jnp.float32)


def place_outer(out, state, got, flags, before):
    xs, ys, zs = got
    fields, near, total, wide = state.shape
    planes, rows, lanes = near - 2 * STATE_W, total - 8, wide - LANES
    even_x, even_y, even_z = flags[0] == 1, flags[1] == 1, flags[2] == 1
    side = (lax.broadcasted_iota(jnp.int32, (1, LANES), 1) < LANES // 2) == even_z
    tiles = [(r, z) for r in range(rows // 8) for z in range(lanes // LANES)]
    for f in range(fields):
        for k in range(planes + 2):
            p, slab = STATE_W - 1 + k, f * (planes + 2) + k
            out[f, p, :, 0:lanes] = state[f, p, :, 0:lanes]
            for r in range(total // 8):
                at = before[2] + slab * (total // 8) + r
                z = jnp.where(side, zs[0][at], 0.0 if len(zs) == 1 else zs[1][at])
                out[f, p, r * 8:(r + 1) * 8, lanes:] = z
            for z in range(lanes // LANES):
                part = slice(z * STATE_W, (z + 1) * STATE_W)
                first = ys[0][before[1] + slab, part]
                second = ys[1][before[1] + slab, part] if len(ys) > 1 else jnp.zeros_like(first)
                to = slice(z * LANES, (z + 1) * LANES)
                out[f, p, rows:rows + STATE_W, to] = jnp.where(even_y, first, second)
                out[f, p, total - STATE_W:total, to] = jnp.where(even_y, second, first)
        for p in (0, near - 1):
            out[f, p] = jnp.zeros((total, wide), jnp.float32)
            is_first = even_x if p else ~even_x
            for t, (r, z) in enumerate(tiles):
                at = before[0] + f * len(tiles) + t
                first = xs[0][at]
                second = xs[1][at] if len(xs) > 1 else jnp.zeros_like(first)
                out[f, p, r * 8:(r + 1) * 8, z * LANES:(z + 1) * LANES] = jnp.where(is_first, first, second)


def send_outer(state, flags, x_out, y_out, z_out, before):
    fields, near, total, wide = state.shape
    planes, rows, lanes = near - 2 * STATE_W, total - 8, wide - LANES
    up = [[(flags[a] == 1) == (n == 0) for n in range(2)] for a in range(3)]
    tiles = [(r, z) for r in range(rows // 8) for z in range(lanes // LANES)]
    for n, ref in enumerate(x_out):
        p = jnp.where(up[0][n], STATE_W + planes - 2, STATE_W + 1)
        for f in range(fields):
            for t, (r, z) in enumerate(tiles):
                ref[before + f * len(tiles) + t] = state[f, p, r * 8:(r + 1) * 8, z * LANES:(z + 1) * LANES]
    for f in range(fields):
        for k in range(planes + 2):
            p, slab = STATE_W - 1 + k, f * (planes + 2) + k
            for n, ref in enumerate(y_out):
                v = jnp.where(up[1][n], state[f, p, rows - STATE_W:rows, 0:lanes], state[f, p, 0:STATE_W, 0:lanes])
                for z in range(lanes // LANES):
                    ref[slab, z * STATE_W:(z + 1) * STATE_W] = v[:, z * LANES:(z + 1) * LANES]
            for n, ref in enumerate(z_out):
                for r in range(total // 8):
                    part = slice(r * 8, (r + 1) * 8)
                    v = jnp.where(up[2][n], state[f, p, part, lanes - LANES:lanes], state[f, p, part, 0:LANES])
                    ref[slab * (total // 8) + r] = v


def inside(flags, rows, lanes, total, depth):
    row = lax.broadcasted_iota(jnp.int32, (total, lanes + LANES), 0)
    lane = lax.broadcasted_iota(jnp.int32, (total, lanes + LANES), 1)
    end = lanes + LANES
    row_ok = (row < rows) | ((row < rows + depth) & (flags[5] == 1)) | ((row >= total - depth) & (flags[6] == 1))
    lane_ok = (lane < lanes) | ((lane < lanes + depth) & (flags[7] == 1)) | ((lane >= end - depth) & (flags[8] == 1))
    return jnp.where(row_ok & lane_ok, 1.0, 0.0)


def plane_inside(flags, p, margin, planes):
    return jnp.where(p < margin, flags[4], jnp.where(p >= margin + planes, flags[3], 1)).astype(jnp.float32)


def put(ref, at, v, margin, planes, rows, lanes, reach):
    p = at[-1]
    reach = reach - max(margin - p, p - margin - planes + 1, 0)
    if reach >= 2:
        ref[at] = v
        return
    ends = v.shape
    ref[(*at, slice(0, rows), slice(0, lanes))] = v[0:rows, 0:lanes]
    for r, z in ((slice(0, rows), slice(lanes, ends[1])), (slice(rows, ends[0]), slice(0, lanes))):
        ref[(*at, r, z)] = v[r, z] if reach == 1 else jnp.zeros((r.stop - r.start, z.stop - z.start), jnp.float32)
    ref[(*at, slice(rows, ends[0]), slice(lanes, ends[1]))] = jnp.zeros((ends[0] - rows, ends[1] - lanes), jnp.float32)


def neighbours(ref, p):
    rows, lanes = ref.shape[2], ref.shape[3]
    sums, grads, spread = [], [], 0.0
    for f in range(4):
        c, xn, xp = ref[f, p], ref[f, p + 1], ref[f, p - 1]
        yn, yp = pltpu.roll(c, rows - 1, 0), pltpu.roll(c, 1, 0)
        zn, zp = pltpu.roll(c, lanes - 1, 1), pltpu.roll(c, 1, 1)
        sums.append((xn + xp) + (yn + yp) + (zn + zp))
        if f == 3:
            grads = [xn - xp, yn - yp, zn - zp]
        else:
            spread = spread + (xn - xp, yn - yp, zn - zp)[f]
    return sums, grads + [spread]


def pack_kernel(tile_ref, mask_ref, out_ref, used_ref, rows_ref, *, capacity):
    tiles = out_ref.shape[0]
    count, width = mask_ref.shape
    out_ref[...] = jnp.zeros(out_ref.shape, jnp.float32)
    for r in range(0, count, 8):
        rows_ref[r:r + 8] = mask_ref[r:r + 8].reshape(8, width // LANES, LANES)

    def clear(t, _):
        used_ref[t] = 0
        return 0

    lax.fori_loop(0, tiles, clear, 0, unroll=8)

    def row(r, _):
        t = tile_ref[r]
        n = used_ref[t]
        used_ref[t] = n + 1
        out_ref[t, jnp.minimum(n, capacity - 1)] = rows_ref[r]
        return 0

    lax.fori_loop(0, count, row, 0, unroll=8)


def split(refs, nums):
    at, got = 0, []
    for n in nums:
        got.append(refs[at:at + n])
        at += n
    return got, refs[at:]


def chi_kernel(flags, slot_ref, rows_ref, out, coarse_out, *refs):
    *x_out, acc, pooled = refs
    _, planes, rows, lanes = out.shape
    acc[...] = jnp.zeros(acc.shape, jnp.float32)
    per = rows_ref.shape[1]

    def add(s, _):
        for c in range(per):
            at = pl.ds(pl.multiple_of(slot_ref[s * per + c] * 8, 8), 8)
            acc[at, :] = acc[at, :] + rows_ref[s, c]
        return 0

    lax.fori_loop(0, rows_ref.shape[0], add, 0)
    z_tiles = lanes // LANES
    across = rows // 2
    for qx in range(planes // 2):
        for zt in range(z_tiles):
            total = None
            for i in range(2):
                for j in range(2):
                    v = acc[pl.ds(qx * across * 8 + (2 * i + j) * z_tiles + zt, across, stride=8), :]
                    pooled[zt, pl.ds(j, across, stride=2), :] = v
                    total = v if total is None else total + v
                out[0, 2 * qx + i, :, zt * LANES:(zt + 1) * LANES] = pooled[zt]
            coarse_out[qx, :, zt * LANES:(zt + 1) * LANES] = total
    for n, ref in enumerate(x_out):
        start = jnp.where((flags[0] == 1) == (n == 0), planes - FINE_W, 0)
        for j in range(FINE_W):
            ref[j] = out[0, start + j]


def side(up, v, dim, width):
    size = v.shape[dim]
    low = v[..., 0:width] if dim == 1 else v[0:width]
    high = v[..., size - width:] if dim == 1 else v[size - width:]
    return jnp.where(up, high, low)


def y_kernel(flags, *refs, take, order, added):
    ready, (_, *outs) = split(refs[len(take):], [added])
    for n, out in enumerate(outs):
        up = (flags[1] == 1) == (n == 0)
        at = 0
        for i in order:
            ref, count = refs[i], take[i]
            for s in range(count):
                out[at] = side(up, ref[s], 0, out.shape[1])
                at += 1
        if added:
            out[at:] = ready[0][n][...]


def z_kernel(flags, *refs, plan, count, added):
    ready, outs = split(refs[count:], [added])
    for n, out in enumerate(outs):
        up = (flags[2] == 1) == (n == 0)
        per = out.shape[1] // PAD
        at = 0
        for slabs, edges in plan:
            for i, low, high in slabs:
                for s in range(low, high):
                    out[at] = side(up, refs[i][s], 1, LANES)
                    at += 1
            for parts in edges:
                k = 0
                for i, low, high in parts:
                    for s in range(low, high):
                        depth = refs[i].shape[1]
                        row = k % per * PAD
                        out[at + k // per, row:row + depth] = side(up, refs[i][s], 1, LANES)
                        if depth < PAD:
                            out[at + k // per, row + depth:row + PAD] = jnp.zeros((PAD - depth, LANES), jnp.float32)
                        k += 1
                while k % per:
                    row = k % per * PAD
                    out[at + k // per, row:row + PAD] = jnp.zeros((PAD, LANES), jnp.float32)
                    k += 1
                at += k // per
        if added:
            out[at:] = ready[0][n][...]


def second_kernel(flags, own, pooled_chi, right_side, start_field, *refs, nums):
    n_x, n_y, n_z = nums
    (chi_x, first_x, first_y, first_z, far_y, far_z), refs = split(refs, [n_x, n_x, n_y, n_z, n_y, n_z])
    rhs, state_out, weight_out = refs[:3]
    (x_out, y_out, z_out), (chi, start, ext, tmp, pooled) = split(refs[3:], nums)
    _, planes, rows, lanes = own.shape
    total = ext.shape[2]
    chi_slabs = planes + n_x * FINE_W
    base = (chi_slabs, chi_slabs + n_y * -(-chi_slabs // (rows // PAD)))
    slabs = (8 * planes, 4 * (START_W + FINE_W))
    fields_got = (first_x, (*first_y, *far_y), far_z)
    place_halo(chi, FINE_W, own, (chi_x, far_y, far_z), flags, FINE_W, FINE_W)
    place_halo(start, START_W, start_field, fields_got, flags, START_W, START_W, (0, 0), slabs, CORNER, base, first_z)
    place_halo(rhs, FINE_W, right_side, fields_got, flags, FINE_W, START_W, (4 * planes, 4 * START_W), slabs, CORNER, base, first_z)
    mask = inside(flags, rows, lanes, total, FINE_W)
    w_p = (RELAX / (SHIFT + 6.0)) * mask

    for k in range(planes + 2 * FINE_W):
        here = plane_inside(flags, k, FINE_W, planes)
        w_u = (RELAX / (SHIFT + 6.0 + chi[0, k])) * (mask * here)
        put(weight_out, (k,), w_u, FINE_W, planes, rows, lanes, FINE_W)
        sums, grads = neighbours(start, k + START_W - FINE_W)
        for f in range(4):
            w = w_u if f < 3 else w_p * here
            v = KEEP * start[f, k + START_W - FINE_W] + w * (rhs[f, k] + sums[f] - 0.5 * grads[f])
            put(ext, (f, k), v, FINE_W, planes, rows, lanes, FINE_W)

    for p in range(1, planes + 2 * FINE_W - 1):
        here = plane_inside(flags, p, FINE_W, planes)
        sums, grads = neighbours(ext, p)
        w_u = weight_out[p]
        for f in range(4):
            w = w_u if f < 3 else w_p * here
            v = KEEP * ext[f, p] + w * (rhs[f, p] + sums[f] - 0.5 * grads[f])
            put(state_out, (f, p), v, FINE_W, planes, rows, lanes, FINE_W - 1)

    for cx in range(planes // 2):
        both = [None] * 4
        for i in range(2):
            p = FINE_W + 2 * cx + i
            sums, grads = neighbours(state_out, p)
            for f in range(4):
                diag = SHIFT + 6.0 + (chi[0, p] if f < 3 else 0.0)
                r = rhs[f, p] + sums[f] - 0.5 * grads[f] - diag * state_out[f, p]
                both[f] = r if i == 0 else both[f] + r
        for f in range(4):
            for zt in range(lanes // LANES):
                tmp[f, zt] = both[f][0:rows, zt * LANES:(zt + 1) * LANES]
                v = tmp[f, zt, pl.ds(0, rows // 2, stride=2), :] + tmp[f, zt, pl.ds(1, rows // 2, stride=2), :]
                pooled[f, cx, :, zt * LANES:(zt + 1) * LANES] = v
    pooled[4] = pooled_chi[...]
    lane = lax.broadcasted_iota(jnp.int32, (lanes, lanes // 2), 0)
    cell = lax.broadcasted_iota(jnp.int32, (lanes, lanes // 2), 1)
    gather = jnp.where(lane // 2 == cell, 0.125, 0.0)
    flat_rows = pooled[...].reshape(5 * planes // 2 * rows // 2, lanes)
    coarse = jnp.dot(flat_rows, gather, precision=HIGHEST, preferred_element_type=jnp.float32)
    coarse = coarse.reshape(5 * planes // 2, rows // 2, lanes // 2)
    for ref in x_out:
        ref[0:coarse.shape[0]] = coarse
    send_outer(state_out, flags, x_out, y_out, z_out, coarse.shape[0])


def last_kernel(flags, own, state, weight, rhs, *refs, nums):
    got, (out, ext, one, two, fine, mid, tmp) = split(refs, nums)
    planes = ext.shape[1] - 2 * COARSE_W
    rows, lanes = own.shape[1:]
    total, wide = ext.shape[2], ext.shape[3]
    own = own.at[0:5 * planes]
    place_halo(ext, COARSE_W, own, got[:3], flags, COARSE_W, COARSE_W)
    x_slabs = 5 * COARSE_W
    slabs = 5 * planes + len(got[0]) * x_slabs
    z_slabs = slabs + len(got[1]) * -(-slabs // (rows // PAD))
    place_outer(fine, state, got, flags, (x_slabs, slabs, z_slabs))
    mask = inside(flags, rows, lanes, total, COARSE_W)
    w_p = (RELAX / (SHIFT + 1.5)) * mask

    for p in range(planes + 2 * COARSE_W):
        here = plane_inside(flags, p, COARSE_W, planes)
        w_u = (RELAX / (SHIFT + 1.5 + ext[4, p])) * (mask * here)
        ext[4, p] = w_u
        for f in range(4):
            one[f, p] = (w_u if f < 3 else w_p * here) * ext[f, p]
    now, then = one, two
    for s in range(1, COARSE_SWEEPS):
        for p in range(s, planes + 2 * COARSE_W - s):
            here = plane_inside(flags, p, COARSE_W, planes)
            sums, grads = neighbours(now, p)
            for f in range(4):
                w = ext[4, p] if f < 3 else w_p * here
                v = KEEP * now[f, p] + w * (ext[f, p] + 0.25 * (sums[f] - grads[f]))
                put(then, (f, p), v, COARSE_W, planes, rows, lanes, COARSE_W + 1 - s)
        now, then = then, now

    f_total, f_wide = fine.shape[2], fine.shape[3]
    f_rows, f_lanes = 2 * rows, 2 * lanes
    cell = lax.broadcasted_iota(jnp.int32, (wide, f_wide), 0)
    lane = lax.broadcasted_iota(jnp.int32, (wide, f_wide), 1)
    from_cell = jnp.where(lane < f_lanes + LANES // 2, lane // 2, wide - 1 - (f_wide - 1 - lane) // 2)
    spread = jnp.where(cell == from_cell, 1.0, 0.0)
    c_planes = planes + 2
    flat = now[:, COARSE_W - 1:COARSE_W - 1 + c_planes].reshape(4 * c_planes * total, wide)
    grown = jnp.dot(flat, spread, precision=HIGHEST, preferred_element_type=jnp.float32)
    for f in range(4):
        for cp in range(c_planes):
            lo = (f * c_planes + cp) * total
            for zt in range(f_wide // LANES):
                v = grown[lo:lo + total, zt * LANES:(zt + 1) * LANES]
                at = f * c_planes + cp
                for j in range(2):
                    tmp[zt, pl.ds(j, rows, stride=2), :] = v[0:rows]
                    tmp[zt, pl.ds(f_rows + j, 2, stride=2), :] = v[rows:rows + 2]
                    tmp[zt, pl.ds(f_total - 4 + j, 2, stride=2), :] = v[total - 2:total]
                for i in range(2):
                    to = slice(zt * LANES, (zt + 1) * LANES)
                    fine[f, 2 * cp + i, :, to] = fine[f, 2 * cp + i, :, to] + tmp[zt]
    f_planes = 2 * planes
    f_mask = inside(flags, f_rows, f_lanes, f_total, STATE_W)
    off = FINE_W - STATE_W
    w_q = (RELAX / (SHIFT + 6.0)) * f_mask

    for p in range(1, f_planes + 3):
        here = plane_inside(flags, p, STATE_W, f_planes)
        sums, grads = neighbours(fine, p)
        for f in range(4):
            w = weight[p + off] if f < 3 else w_q * here
            v = KEEP * fine[f, p] + w * (rhs[f, p + off] + sums[f] - 0.5 * grads[f])
            put(mid, (f, p), v, STATE_W, f_planes, f_rows, f_lanes, 1)

    for k in range(f_planes):
        p = k + 2
        sums, grads = neighbours(mid, p)
        for f in range(4):
            w = weight[p + off] if f < 3 else w_q
            v = KEEP * mid[f, p] + w * (rhs[f, p + off] + sums[f] - 0.5 * grads[f])
            out[f, k] = v[0:f_rows, 0:f_lanes]


def call(kernel, shapes, scratch, *args, smem=1):
    outs = [jax.ShapeDtypeStruct(s, jnp.float32) for s in shapes]
    return pl.pallas_call(
        kernel,
        out_shape=outs,
        in_specs=[SMEM] * smem + [VMEM] * (len(args) - smem),
        out_specs=[VMEM] * len(outs),
        scratch_shapes=scratch,
        compiler_params=PARAMS,
    )(*args)


def routes(block_tile, block_slot, tiles, count_l, per_device, capacity, slots):
    my_tile = lax.axis_index("gx") * lax.axis_size("gy") + lax.axis_index("gy")
    index_l = lax.axis_index("lvl")
    their_tiles = lax.dynamic_index_in_dim(block_tile.reshape(tiles, count_l, per_device), index_l, 1, keepdims=False)
    their_slots = lax.dynamic_index_in_dim(block_slot.reshape(tiles, count_l, per_device), index_l, 1, keepdims=False)
    arriving = their_tiles == my_tile
    counter = jnp.arange(per_device, dtype=jnp.int32)
    earlier = counter[None, :, None] < counter[None, None, :]
    order = jnp.sum(jnp.where(arriving[:, :, None] & earlier, 1, 0), axis=1)
    places = jnp.arange(capacity, dtype=jnp.int32)
    hit = arriving[:, None, :] & (order[:, None, :] == places[None, :, None])
    slot = jnp.sum(jnp.where(hit, their_slots[:, None, :] - slots, 0), axis=2) + slots
    return slot.reshape(-1)


def body(right_side, start_field, mask_blocks, block_tile, block_slot):
    axes = ("gx", "gy", "lvl")
    counts = [lax.axis_size(a) for a in axes]
    index = [lax.axis_index(a) for a in axes]
    tiles = counts[0] * counts[1]
    per_device, width = mask_blocks.shape
    capacity = max(2, 2 * per_device // tiles)
    _, planes, rows, lanes = right_side.shape
    slots = planes // 2 * (rows // 2)
    c_planes, c_rows, c_lanes = planes // 2, rows // 2, lanes // 2
    flags = [i % 2 == 0 for i in index]
    for i, n in zip(index, counts):
        flags += [i < n - 1, i > 0]
    flags = jnp.stack(flags).astype(jnp.int32)

    my_flat = (index[0] * counts[1] + index[1]) * counts[2] + index[2]
    tile_ids = block_tile[:, 0]
    my_tiles = lax.dynamic_slice_in_dim(tile_ids, my_flat * per_device, per_device)
    (outgoing,) = call(
        functools.partial(pack_kernel, capacity=capacity),
        [(tiles, capacity, width // LANES, LANES)],
        [pltpu.SMEM((tiles,), jnp.int32), pltpu.VMEM((per_device, width // LANES, LANES), jnp.float32)],
        my_tiles, mask_blocks,
    )
    outgoing, right_side, start_field = lax.optimization_barrier((outgoing, right_side, start_field))
    arrived = lax.all_to_all(outgoing, ("gx", "gy"), split_axis=0, concat_axis=0, tiled=True)
    slot_of = routes(tile_ids, block_slot, tiles, counts[2], per_device, capacity, slots)

    total, wide = rows + 8, lanes + LANES
    near, far = planes + 2 * STATE_W, planes + 2 * FINE_W
    pair_counts = [1 + (n > 2) for n in counts]
    flags, slot_of, start_late, right_late = lax.optimization_barrier((flags, slot_of, start_field, right_side))
    groups = [(start_late, START_W), (right_late, FINE_W)]
    first_x = halo_x(groups)
    first_y = swap("gy", lambda up, n: flat([cut(v, 2, START_W, up) for v, _ in groups]))
    first_z = swap("lvl", lambda up, n: flat([cut(v, 3, LANES, up) for v, _ in groups]))
    first_z, slot_of = lax.optimization_barrier((first_z, slot_of))
    chi, pooled_chi, *chi_out = call(
        chi_kernel,
        [(1, planes, rows, lanes), (c_planes, c_rows, lanes), *[(FINE_W, rows, lanes)] * pair_counts[0]],
        [pltpu.VMEM(((slots + 1) * 8, LANES), jnp.float32), pltpu.VMEM((lanes // LANES, rows, LANES), jnp.float32)],
        flags, slot_of, arrived, smem=2,
    )
    chi_x = swap("gx", lambda up, n: chi_out[n])
    first_x, first_y, chi_x = lax.optimization_barrier((first_x, first_y, chi_x))
    slabs = lambda v: v.reshape(-1, rows, lanes)
    far_x = len(first_x) * 4 * (START_W + FINE_W)
    chi_slabs = planes + len(chi_x) * FINE_W
    n_x, n_y, n_z = pair_counts
    y_sent = call(
        functools.partial(
            y_kernel,
            take=[planes, *[x.shape[0] for x in (*chi_x[::-1], *first_x[::-1])]],
            order=[0, *range(n_x, 0, -1), *range(2 * n_x, n_x, -1)],
            added=0,
        ),
        [(chi_slabs + far_x, CORNER, lanes)] * n_y,
        [],
        flags, slabs(chi), *chi_x[::-1], *first_x[::-1], chi_x[0][0, :1, :LANES],
    )
    far_y = swap("gy", lambda up, n: y_sent[n])
    per = rows // PAD
    edges = -(-chi_slabs // per) + -(-(8 * planes + far_x) // per)
    whole = lambda first, refs: [(first + i, 0, r.shape[0]) for i, r in enumerate(refs)]
    far_at = 1 + 2 * n_x + n_y
    plan = [
        ([(0, 0, planes), *whole(1, chi_x)], [[(far_at + n, 0, chi_slabs)] for n in range(n_y)]),
        (
            whole(1 + n_x, first_x),
            [[(1 + 2 * n_x + n, 0, 8 * planes), (far_at + n, chi_slabs, chi_slabs + far_x)] for n in range(n_y)],
        ),
    ]
    z_sent = call(
        functools.partial(z_kernel, plan=plan, count=far_at + n_y, added=0),
        [(chi_slabs + far_x + n_y * edges, rows, LANES)] * n_z,
        [],
        flags, slabs(chi), *chi_x, *first_x, *first_y, *far_y,
    )
    far_z = swap("lvl", lambda up, n: z_sent[n])
    c_slabs, s_slabs = 5 * c_planes, 4 * (rows // 8) * (lanes // LANES)
    outers = [[(c_slabs + s_slabs, 8, LANES)], [(4 * (planes + 2), PAD, LANES)], [(4 * (planes + 2) * total // 8, 8, LANES)]]
    outers = [shape * n for shape, n in zip(outers, pair_counts)]
    rhs, state, weight, *sent = call(
        functools.partial(second_kernel, nums=pair_counts),
        [(4, far, total, wide), (4, near, total, wide), (far, total, wide), *sum(outers, [])],
        [
            pltpu.VMEM((1, far, total, wide), jnp.float32),
            pltpu.VMEM((4, planes + 2 * START_W, total, wide), jnp.float32),
            pltpu.VMEM((4, far, total, wide), jnp.float32),
            pltpu.VMEM((4, lanes // LANES, rows, LANES), jnp.float32),
            pltpu.VMEM((5, c_planes, c_rows, lanes), jnp.float32),
        ],
        flags, chi, pooled_chi, right_side, start_field, *chi_x, *first_x, *first_y, *first_z, *far_y, *far_z,
    )
    (x_out, y_out, z_out), _ = split(sent, pair_counts)
    last_x = swap("gx", lambda up, n: x_out[n])
    take = [c_slabs, *[5 * COARSE_W] * n_x]
    y_sent = call(
        functools.partial(y_kernel, take=take, order=[0, *range(n_x, 0, -1)], added=n_y),
        [(sum(take) + y_out[0].shape[0], COARSE_W, c_lanes)] * n_y,
        [],
        flags, x_out[0], *last_x[::-1], *y_out, last_x[0][0, :1, :LANES],
    )
    last_y = swap("gy", lambda up, n: y_sent[n])
    plan = [([(i, 0, t) for i, t in enumerate(take)], [[(1 + n_x + n, 0, sum(take))] for n in range(n_y)])]
    z_slabs = sum(take) + n_y * -(-sum(take) // (c_rows // PAD))
    z_sent = call(
        functools.partial(z_kernel, plan=plan, count=1 + n_x + n_y, added=n_z),
        [(z_slabs + z_out[0].shape[0], c_rows, LANES)] * n_z,
        [],
        flags, x_out[0], *last_x, *last_y, *z_out,
    )
    last_z = swap("lvl", lambda up, n: z_sent[n])
    c_ext = (c_planes + 2 * COARSE_W, c_rows + 8, c_lanes + LANES)
    (out,) = call(
        functools.partial(last_kernel, nums=pair_counts),
        [right_side.shape],
        [
            pltpu.VMEM((5, *c_ext), jnp.float32),
            pltpu.VMEM((4, *c_ext), jnp.float32),
            pltpu.VMEM((4, *c_ext), jnp.float32),
            pltpu.VMEM((4, near, total, wide), jnp.float32),
            pltpu.VMEM((4, near, total, wide), jnp.float32),
            pltpu.VMEM((wide // LANES, total, LANES), jnp.float32),
        ],
        flags, x_out[0], state, weight, rhs, *last_x, *last_y, *last_z,
    )
    return out


def solution(mesh):
    in_specs = (
        P(None, "gx", "gy", "lvl"),
        P(None, "gx", "gy", "lvl"),
        P(("gx", "gy", "lvl"), None),
        P(),
        P(),
    )
    out_specs = P(None, "gx", "gy", "lvl")
    return jax.shard_map(body, mesh=mesh, in_specs=in_specs, out_specs=out_specs, check_vma=False)
```

```python
import functools

import jax
import jax.numpy as jnp
from jax import lax
from jax.experimental import pallas as pl
from jax.experimental.pallas import tpu as pltpu
from jax.sharding import PartitionSpec as P

COARSE_SWEEPS = 4
SHIFT = 0.05
RELAX = 0.6
KEEP = 1.0 - RELAX
LANES = 128
START_W = 3
FINE_W = 2
CORNER = 2
STATE_W = 2
COARSE_W = 4
PAD = 4
HIGHEST = lax.Precision.HIGHEST
VMEM = pl.BlockSpec(memory_space=pltpu.VMEM)
SMEM = pl.BlockSpec(memory_space=pltpu.SMEM)
PARAMS = pltpu.CompilerParams(vmem_limit_bytes=24 << 20)


def pairs(count, first):
    return [p for i in range(first, count - 1, 2) for p in ((i, i + 1), (i + 1, i))]


def cut(values, dim, width, to_next):
    size = values.shape[dim]
    if size == width:
        return values
    start = jnp.where(to_next, size - width, 0)
    return lax.dynamic_slice_in_dim(values, start, width, axis=dim)


def flat(parts):
    return jnp.concatenate([p.reshape(-1, *p.shape[-2:]) for p in parts], axis=0)


def swap(axis, message):
    count = lax.axis_size(axis)
    even = lax.axis_index(axis) % 2 == 0
    got = [lax.ppermute(message(~even, 1), axis, pairs(count, 1))] if count > 2 else []
    got.insert(0, lax.ppermute(message(even, 0), axis, pairs(count, 0)))
    return got


def halo_x(groups):
    return swap("gx", lambda up, n: flat([cut(v, 1, w, up) for v, w in groups]))


def place_halo(dst, margin, own, got, flags, width, depth, group=(0, 0), slabs=None, corner=0, base=(0, 0), early=()):
    xs, ys, zs = got
    rows, lanes = own.shape[-2:]
    fields, planes, total = dst.shape[0], dst.shape[1] - 2 * margin, dst.shape[2]
    own_slabs, x_slabs = slabs or (fields * planes, fields * width)
    pairs_y = len(ys) // 2 if corner else len(ys)
    slab_count = own_slabs + len(xs) * x_slabs
    per = rows // PAD
    even_x, even_y, even_z = flags[0] == 1, flags[1] == 1, flags[2] == 1
    near = (lax.broadcasted_iota(jnp.int32, (1, LANES), 1) < LANES // 2) == even_z

    def edge(at, row, size):
        part = slice(row, row + size)
        if early and at < own_slabs:
            return jnp.where(near, early[0][at, part], 0.0 if len(zs) == 1 else early[1][at, part])
        at = base[1] + at - (own_slabs if early else 0)
        return jnp.where(near, zs[0][at, part], 0.0 if len(zs) == 1 else zs[1][at, part])

    for f in range(fields):
        for k in range(planes + len(xs) * width):
            deep = depth
            if k < planes:
                at, plane, slab = margin + k, own[f, k] if len(own.shape) == 4 else own[f * planes + k], group[0] + f * planes + k
            else:
                which, j = divmod(k - planes, width)
                up, down = margin + planes + j, margin - width + j
                at = jnp.where(even_x, up, down) if which == 0 else jnp.where(even_x, down, up)
                plane = xs[which][group[1] + f * width + j]
                slab = own_slabs + which * x_slabs + group[1] + f * width + j
                deep = corner or depth
            dst[f, at, 0:rows, 0:lanes] = plane
            dst[f, at, 0:rows, lanes:] = edge(slab, 0, rows)
            sides = []
            for n in range(pairs_y):
                at_z = slab_count + n * (-(-slab_count // per)) + slab // per
                if corner and k >= planes:
                    y = ys[pairs_y + n][base[0] + slab - own_slabs]
                else:
                    y = ys[n][slab]
                sides.append((y, edge(at_z, slab % per * PAD, deep)))
            if len(sides) == 1:
                sides.append([jnp.zeros_like(v) for v in sides[0]])
            for to, first, second in zip((slice(0, lanes), slice(lanes, lanes + LANES)), *sides):
                dst[f, at, rows:rows + deep, to] = jnp.where(even_y, first, second)
                dst[f, at, total - deep:total, to] = jnp.where(even_y, second, first)
            gap = total - rows - 2 * deep
            if gap:
                dst[f, at, rows + deep:total - deep, :] = jnp.zeros((gap, dst.shape[3]), jnp.float32)


def place_outer(out, state, got, flags, before):
    xs, ys, zs = got
    fields, near, total, wide = state.shape
    planes, rows, lanes = near - 2 * STATE_W, total - 8, wide - LANES
    even_x, even_y, even_z = flags[0] == 1, flags[1] == 1, flags[2] == 1
    side = (lax.broadcasted_iota(jnp.int32, (1, LANES), 1) < LANES // 2) == even_z
    tiles = [(r, z) for r in range(rows // 8) for z in range(lanes // LANES)]
    for f in range(fields):
        for k in range(planes + 2):
            p, slab = STATE_W - 1 + k, f * (planes + 2) + k
            out[f, p, :, 0:lanes] = state[f, p, :, 0:lanes]
            for r in range(total // 8):
                at = before[2] + slab * (total // 8) + r
                z = jnp.where(side, zs[0][at], 0.0 if len(zs) == 1 else zs[1][at])
                out[f, p, r * 8:(r + 1) * 8, lanes:] = z
            out_by = 1 if 0 < k <= planes else 0
            for z in range(lanes // LANES):
                at, row = before[1] + slab // 2, slab % 2 * 2 + z
                first = ys[0][at, row:row + 1]
                second = ys[1][at, row:row + 1] if len(ys) > 1 else jnp.zeros_like(first)
                to = slice(z * LANES, (z + 1) * LANES)
                out[f, p, rows + out_by:rows + out_by + 1, to] = jnp.where(even_y, first, second)
                out[f, p, total - 1 - out_by:total - out_by, to] = jnp.where(even_y, second, first)
        for p in (0, near - 1):
            out[f, p] = jnp.zeros((total, wide), jnp.float32)
            is_first = even_x if p else ~even_x
            for t, (r, z) in enumerate(tiles):
                at = before[0] + f * len(tiles) + t
                first = xs[0][at]
                second = xs[1][at] if len(xs) > 1 else jnp.zeros_like(first)
                out[f, p, r * 8:(r + 1) * 8, z * LANES:(z + 1) * LANES] = jnp.where(is_first, first, second)


def send_outer(state, flags, x_out, y_out, z_out, before):
    fields, near, total, wide = state.shape
    planes, rows, lanes = near - 2 * STATE_W, total - 8, wide - LANES
    up = [[(flags[a] == 1) == (n == 0) for n in range(2)] for a in range(3)]
    tiles = [(r, z) for r in range(rows // 8) for z in range(lanes // LANES)]
    for n, ref in enumerate(x_out):
        p = jnp.where(up[0][n], STATE_W + planes - 2, STATE_W + 1)
        for f in range(fields):
            for t, (r, z) in enumerate(tiles):
                ref[before + f * len(tiles) + t] = state[f, p, r * 8:(r + 1) * 8, z * LANES:(z + 1) * LANES]
    for f in range(fields):
        for k in range(planes + 2):
            p, slab = STATE_W - 1 + k, f * (planes + 2) + k
            out_by = 1 if 0 < k <= planes else 0
            for n, ref in enumerate(y_out):
                high = state[f, p, rows - 1 - out_by:rows - out_by, 0:lanes]
                v = jnp.where(up[1][n], high, state[f, p, out_by:out_by + 1, 0:lanes])
                for z in range(lanes // LANES):
                    row = slab % 2 * 2 + z
                    ref[slab // 2, row:row + 1] = v[:, z * LANES:(z + 1) * LANES]
            for n, ref in enumerate(z_out):
                for r in range(total // 8):
                    part = slice(r * 8, (r + 1) * 8)
                    v = jnp.where(up[2][n], state[f, p, part, lanes - LANES:lanes], state[f, p, part, 0:LANES])
                    ref[slab * (total // 8) + r] = v


def inside(flags, rows, lanes, total, depth):
    row = lax.broadcasted_iota(jnp.int32, (total, lanes + LANES), 0)
    lane = lax.broadcasted_iota(jnp.int32, (total, lanes + LANES), 1)
    end = lanes + LANES
    row_ok = (row < rows) | ((row < rows + depth) & (flags[5] == 1)) | ((row >= total - depth) & (flags[6] == 1))
    lane_ok = (lane < lanes) | ((lane < lanes + depth) & (flags[7] == 1)) | ((lane >= end - depth) & (flags[8] == 1))
    return jnp.where(row_ok & lane_ok, 1.0, 0.0)


def plane_inside(flags, p, margin, planes):
    return jnp.where(p < margin, flags[4], jnp.where(p >= margin + planes, flags[3], 1)).astype(jnp.float32)


def put(ref, at, v, margin, planes, rows, lanes, reach):
    p = at[-1]
    reach = reach - max(margin - p, p - margin - planes + 1, 0)
    if reach >= 2:
        ref[at] = v
        return
    ends = v.shape
    ref[(*at, slice(0, rows), slice(0, lanes))] = v[0:rows, 0:lanes]
    for r, z in ((slice(0, rows), slice(lanes, ends[1])), (slice(rows, ends[0]), slice(0, lanes))):
        ref[(*at, r, z)] = v[r, z] if reach == 1 else jnp.zeros((r.stop - r.start, z.stop - z.start), jnp.float32)
    ref[(*at, slice(rows, ends[0]), slice(lanes, ends[1]))] = jnp.zeros((ends[0] - rows, ends[1] - lanes), jnp.float32)


def neighbours(ref, p):
    rows, lanes = ref.shape[2], ref.shape[3]
    sums, grads, spread = [], [], 0.0
    for f in range(4):
        c, xn, xp = ref[f, p], ref[f, p + 1], ref[f, p - 1]
        yn, yp = pltpu.roll(c, rows - 1, 0), pltpu.roll(c, 1, 0)
        zn, zp = pltpu.roll(c, lanes - 1, 1), pltpu.roll(c, 1, 1)
        sums.append((xn + xp) + (yn + yp) + (zn + zp))
        if f == 3:
            grads = [xn - xp, yn - yp, zn - zp]
        else:
            spread = spread + (xn - xp, yn - yp, zn - zp)[f]
    return sums, grads + [spread]


def pack_kernel(tile_ref, mask_ref, out_ref, used_ref, rows_ref, *, capacity):
    tiles = out_ref.shape[0]
    count, width = mask_ref.shape
    out_ref[...] = jnp.zeros(out_ref.shape, jnp.float32)
    for r in range(0, count, 8):
        rows_ref[r:r + 8] = mask_ref[r:r + 8].reshape(8, width // LANES, LANES)

    def clear(t, _):
        used_ref[t] = 0
        return 0

    lax.fori_loop(0, tiles, clear, 0, unroll=8)

    def row(r, _):
        t = tile_ref[r]
        n = used_ref[t]
        used_ref[t] = n + 1
        out_ref[t, jnp.minimum(n, capacity - 1)] = rows_ref[r]
        return 0

    lax.fori_loop(0, count, row, 0, unroll=8)


def split(refs, nums):
    at, got = 0, []
    for n in nums:
        got.append(refs[at:at + n])
        at += n
    return got, refs[at:]


def chi_kernel(flags, slot_ref, rows_ref, out, coarse_out, *refs):
    *x_out, acc, pooled = refs
    _, planes, rows, lanes = out.shape
    acc[...] = jnp.zeros(acc.shape, jnp.float32)
    per = rows_ref.shape[1]

    def add(s, _):
        for c in range(per):
            at = pl.ds(pl.multiple_of(slot_ref[s * per + c] * 8, 8), 8)
            acc[at, :] = acc[at, :] + rows_ref[s, c]
        return 0

    lax.fori_loop(0, rows_ref.shape[0], add, 0)
    z_tiles = lanes // LANES
    across = rows // 2
    for qx in range(planes // 2):
        for zt in range(z_tiles):
            total = None
            for i in range(2):
                for j in range(2):
                    v = acc[pl.ds(qx * across * 8 + (2 * i + j) * z_tiles + zt, across, stride=8), :]
                    pooled[zt, pl.ds(j, across, stride=2), :] = v
                    total = v if total is None else total + v
                out[0, 2 * qx + i, :, zt * LANES:(zt + 1) * LANES] = pooled[zt]
            coarse_out[qx, :, zt * LANES:(zt + 1) * LANES] = total
    for n, ref in enumerate(x_out):
        start = jnp.where((flags[0] == 1) == (n == 0), planes - FINE_W, 0)
        for j in range(FINE_W):
            ref[j] = out[0, start + j]


def side(up, v, dim, width):
    size = v.shape[dim]
    low = v[..., 0:width] if dim == 1 else v[0:width]
    high = v[..., size - width:] if dim == 1 else v[size - width:]
    return jnp.where(up, high, low)


def y_kernel(flags, *refs, take, order, added):
    ready, (_, *outs) = split(refs[len(take):], [added])
    for n, out in enumerate(outs):
        up = (flags[1] == 1) == (n == 0)
        at = 0
        for i in order:
            ref, count = refs[i], take[i]
            for s in range(count):
                out[at] = side(up, ref[s], 0, out.shape[1])
                at += 1
        if added:
            out[at:] = ready[0][n][...]


def z_kernel(flags, *refs, plan, count, added):
    ready, outs = split(refs[count:], [added])
    for n, out in enumerate(outs):
        up = (flags[2] == 1) == (n == 0)
        per = out.shape[1] // PAD
        at = 0
        for slabs, edges in plan:
            for i, low, high in slabs:
                for s in range(low, high):
                    out[at] = side(up, refs[i][s], 1, LANES)
                    at += 1
            for parts in edges:
                k = 0
                for i, low, high in parts:
                    for s in range(low, high):
                        depth = refs[i].shape[1]
                        row = k % per * PAD
                        out[at + k // per, row:row + depth] = side(up, refs[i][s], 1, LANES)
                        if depth < PAD:
                            out[at + k // per, row + depth:row + PAD] = jnp.zeros((PAD - depth, LANES), jnp.float32)
                        k += 1
                while k % per:
                    row = k % per * PAD
                    out[at + k // per, row:row + PAD] = jnp.zeros((PAD, LANES), jnp.float32)
                    k += 1
                at += k // per
        if added:
            out[at:] = ready[0][n][...]


def second_kernel(flags, own, pooled_chi, right_side, start_field, *refs, nums):
    n_x, n_y, n_z = nums
    (chi_x, first_x, first_y, first_z, far_y, far_z), refs = split(refs, [n_x, n_x, n_y, n_z, n_y, n_z])
    rhs, state_out, weight_out = refs[:3]
    (x_out, y_out, z_out), (chi, start, ext, tmp, pooled) = split(refs[3:], nums)
    _, planes, rows, lanes = own.shape
    total = ext.shape[2]
    chi_slabs = planes + n_x * FINE_W
    base = (chi_slabs, chi_slabs + n_y * -(-chi_slabs // (rows // PAD)))
    slabs = (8 * planes, 4 * (START_W + FINE_W))
    fields_got = (first_x, (*first_y, *far_y), far_z)
    place_halo(chi, FINE_W, own, (chi_x, far_y, far_z), flags, FINE_W, FINE_W)
    place_halo(start, START_W, start_field, fields_got, flags, START_W, START_W, (0, 0), slabs, CORNER, base, first_z)
    place_halo(rhs, FINE_W, right_side, fields_got, flags, FINE_W, START_W, (4 * planes, 4 * START_W), slabs, CORNER, base, first_z)
    mask = inside(flags, rows, lanes, total, FINE_W)
    w_p = (RELAX / (SHIFT + 6.0)) * mask

    for k in range(planes + 2 * FINE_W):
        here = plane_inside(flags, k, FINE_W, planes)
        w_u = (RELAX / (SHIFT + 6.0 + chi[0, k])) * (mask * here)
        put(weight_out, (k,), w_u, FINE_W, planes, rows, lanes, FINE_W)
        sums, grads = neighbours(start, k + START_W - FINE_W)
        for f in range(4):
            w = w_u if f < 3 else w_p * here
            v = KEEP * start[f, k + START_W - FINE_W] + w * (rhs[f, k] + sums[f] - 0.5 * grads[f])
            put(ext, (f, k), v, FINE_W, planes, rows, lanes, FINE_W)

    for p in range(1, planes + 2 * FINE_W - 1):
        here = plane_inside(flags, p, FINE_W, planes)
        sums, grads = neighbours(ext, p)
        w_u = weight_out[p]
        for f in range(4):
            w = w_u if f < 3 else w_p * here
            v = KEEP * ext[f, p] + w * (rhs[f, p] + sums[f] - 0.5 * grads[f])
            put(state_out, (f, p), v, FINE_W, planes, rows, lanes, FINE_W - 1)

    for cx in range(planes // 2):
        both = [None] * 4
        for i in range(2):
            p = FINE_W + 2 * cx + i
            sums, grads = neighbours(state_out, p)
            for f in range(4):
                diag = SHIFT + 6.0 + (chi[0, p] if f < 3 else 0.0)
                r = rhs[f, p] + sums[f] - 0.5 * grads[f] - diag * state_out[f, p]
                both[f] = r if i == 0 else both[f] + r
        for f in range(4):
            for zt in range(lanes // LANES):
                tmp[f, zt] = both[f][0:rows, zt * LANES:(zt + 1) * LANES]
                v = tmp[f, zt, pl.ds(0, rows // 2, stride=2), :] + tmp[f, zt, pl.ds(1, rows // 2, stride=2), :]
                pooled[f, cx, :, zt * LANES:(zt + 1) * LANES] = v
    pooled[4] = pooled_chi[...]
    lane = lax.broadcasted_iota(jnp.int32, (lanes, lanes // 2), 0)
    cell = lax.broadcasted_iota(jnp.int32, (lanes, lanes // 2), 1)
    gather = jnp.where(lane // 2 == cell, 0.125, 0.0)
    flat_rows = pooled[...].reshape(5 * planes // 2 * rows // 2, lanes)
    coarse = jnp.dot(flat_rows, gather, precision=HIGHEST, preferred_element_type=jnp.float32)
    coarse = coarse.reshape(5 * planes // 2, rows // 2, lanes // 2)
    for ref in x_out:
        ref[0:coarse.shape[0]] = coarse
    send_outer(state_out, flags, x_out, y_out, z_out, coarse.shape[0])


def last_kernel(flags, own, state, weight, rhs, *refs, nums):
    got, (out, ext, one, two, fine, mid, tmp) = split(refs, nums)
    planes = ext.shape[1] - 2 * COARSE_W
    rows, lanes = own.shape[1:]
    total, wide = ext.shape[2], ext.shape[3]
    own = own.at[0:5 * planes]
    place_halo(ext, COARSE_W, own, got[:3], flags, COARSE_W, COARSE_W)
    x_slabs = 5 * COARSE_W
    slabs = 5 * planes + len(got[0]) * x_slabs
    z_slabs = slabs + len(got[1]) * -(-slabs // (rows // PAD))
    place_outer(fine, state, got, flags, (x_slabs, slabs, z_slabs))
    mask = inside(flags, rows, lanes, total, COARSE_W)
    w_p = (RELAX / (SHIFT + 1.5)) * mask

    for p in range(planes + 2 * COARSE_W):
        here = plane_inside(flags, p, COARSE_W, planes)
        w_u = (RELAX / (SHIFT + 1.5 + ext[4, p])) * (mask * here)
        ext[4, p] = w_u
        for f in range(4):
            one[f, p] = (w_u if f < 3 else w_p * here) * ext[f, p]
    now, then = one, two
    for s in range(1, COARSE_SWEEPS):
        for p in range(s, planes + 2 * COARSE_W - s):
            here = plane_inside(flags, p, COARSE_W, planes)
            sums, grads = neighbours(now, p)
            for f in range(4):
                w = ext[4, p] if f < 3 else w_p * here
                v = KEEP * now[f, p] + w * (ext[f, p] + 0.25 * (sums[f] - grads[f]))
                put(then, (f, p), v, COARSE_W, planes, rows, lanes, COARSE_W + 1 - s)
        now, then = then, now

    f_total, f_wide = fine.shape[2], fine.shape[3]
    f_rows, f_lanes = 2 * rows, 2 * lanes
    cell = lax.broadcasted_iota(jnp.int32, (wide, f_wide), 0)
    lane = lax.broadcasted_iota(jnp.int32, (wide, f_wide), 1)
    from_cell = jnp.where(lane < f_lanes + LANES // 2, lane // 2, wide - 1 - (f_wide - 1 - lane) // 2)
    spread = jnp.where(cell == from_cell, 1.0, 0.0)
    c_planes = planes + 2
    flat = now[:, COARSE_W - 1:COARSE_W - 1 + c_planes].reshape(4 * c_planes * total, wide)
    grown = jnp.dot(flat, spread, precision=HIGHEST, preferred_element_type=jnp.float32)
    for f in range(4):
        for cp in range(c_planes):
            lo = (f * c_planes + cp) * total
            for zt in range(f_wide // LANES):
                v = grown[lo:lo + total, zt * LANES:(zt + 1) * LANES]
                at = f * c_planes + cp
                for j in range(2):
                    tmp[zt, pl.ds(j, rows, stride=2), :] = v[0:rows]
                    tmp[zt, pl.ds(f_rows + j, 2, stride=2), :] = v[rows:rows + 2]
                    tmp[zt, pl.ds(f_total - 4 + j, 2, stride=2), :] = v[total - 2:total]
                for i in range(2):
                    to = slice(zt * LANES, (zt + 1) * LANES)
                    fine[f, 2 * cp + i, :, to] = fine[f, 2 * cp + i, :, to] + tmp[zt]
    f_planes = 2 * planes
    f_mask = inside(flags, f_rows, f_lanes, f_total, STATE_W)
    off = FINE_W - STATE_W
    w_q = (RELAX / (SHIFT + 6.0)) * f_mask

    for p in range(1, f_planes + 3):
        here = plane_inside(flags, p, STATE_W, f_planes)
        sums, grads = neighbours(fine, p)
        for f in range(4):
            w = weight[p + off] if f < 3 else w_q * here
            v = KEEP * fine[f, p] + w * (rhs[f, p + off] + sums[f] - 0.5 * grads[f])
            put(mid, (f, p), v, STATE_W, f_planes, f_rows, f_lanes, 1)

    for k in range(f_planes):
        p = k + 2
        sums, grads = neighbours(mid, p)
        for f in range(4):
            w = weight[p + off] if f < 3 else w_q
            v = KEEP * mid[f, p] + w * (rhs[f, p + off] + sums[f] - 0.5 * grads[f])
            out[f, k] = v[0:f_rows, 0:f_lanes]


def call(kernel, shapes, scratch, *args, smem=1):
    outs = [jax.ShapeDtypeStruct(s, jnp.float32) for s in shapes]
    return pl.pallas_call(
        kernel,
        out_shape=outs,
        in_specs=[SMEM] * smem + [VMEM] * (len(args) - smem),
        out_specs=[VMEM] * len(outs),
        scratch_shapes=scratch,
        compiler_params=PARAMS,
    )(*args)


def routes(block_tile, block_slot, tiles, count_l, per_device, capacity, slots):
    my_tile = lax.axis_index("gx") * lax.axis_size("gy") + lax.axis_index("gy")
    index_l = lax.axis_index("lvl")
    their_tiles = lax.dynamic_index_in_dim(block_tile.reshape(tiles, count_l, per_device), index_l, 1, keepdims=False)
    their_slots = lax.dynamic_index_in_dim(block_slot.reshape(tiles, count_l, per_device), index_l, 1, keepdims=False)
    arriving = their_tiles == my_tile
    counter = jnp.arange(per_device, dtype=jnp.int32)
    earlier = counter[None, :, None] < counter[None, None, :]
    order = jnp.sum(jnp.where(arriving[:, :, None] & earlier, 1, 0), axis=1)
    places = jnp.arange(capacity, dtype=jnp.int32)
    hit = arriving[:, None, :] & (order[:, None, :] == places[None, :, None])
    slot = jnp.sum(jnp.where(hit, their_slots[:, None, :] - slots, 0), axis=2) + slots
    return slot.reshape(-1)


def body(right_side, start_field, mask_blocks, block_tile, block_slot):
    axes = ("gx", "gy", "lvl")
    counts = [lax.axis_size(a) for a in axes]
    index = [lax.axis_index(a) for a in axes]
    tiles = counts[0] * counts[1]
    per_device, width = mask_blocks.shape
    capacity = max(2, 2 * per_device // tiles)
    _, planes, rows, lanes = right_side.shape
    slots = planes // 2 * (rows // 2)
    c_planes, c_rows, c_lanes = planes // 2, rows // 2, lanes // 2
    flags = [i % 2 == 0 for i in index]
    for i, n in zip(index, counts):
        flags += [i < n - 1, i > 0]
    flags = jnp.stack(flags).astype(jnp.int32)

    my_flat = (index[0] * counts[1] + index[1]) * counts[2] + index[2]
    tile_ids = block_tile[:, 0]
    my_tiles = lax.dynamic_slice_in_dim(tile_ids, my_flat * per_device, per_device)
    (outgoing,) = call(
        functools.partial(pack_kernel, capacity=capacity),
        [(tiles, capacity, width // LANES, LANES)],
        [pltpu.SMEM((tiles,), jnp.int32), pltpu.VMEM((per_device, width // LANES, LANES), jnp.float32)],
        my_tiles, mask_blocks,
    )
    outgoing, right_side, start_field = lax.optimization_barrier((outgoing, right_side, start_field))
    arrived = lax.all_to_all(outgoing, ("gx", "gy"), split_axis=0, concat_axis=0, tiled=True)
    slot_of = routes(tile_ids, block_slot, tiles, counts[2], per_device, capacity, slots)

    total, wide = rows + 8, lanes + LANES
    near, far = planes + 2 * STATE_W, planes + 2 * FINE_W
    pair_counts = [1 + (n > 2) for n in counts]
    groups = [(start_field, START_W), (right_side, FINE_W)]
    first_x = halo_x(groups)
    first_y = swap("gy", lambda up, n: flat([cut(v, 2, START_W, up) for v, _ in groups]))
    first_z = swap("lvl", lambda up, n: flat([cut(v, 3, LANES, up) for v, _ in groups]))
    first_z, slot_of = lax.optimization_barrier((first_z, slot_of))
    chi, pooled_chi, *chi_out = call(
        chi_kernel,
        [(1, planes, rows, lanes), (c_planes, c_rows, lanes), *[(FINE_W, rows, lanes)] * pair_counts[0]],
        [pltpu.VMEM(((slots + 1) * 8, LANES), jnp.float32), pltpu.VMEM((lanes // LANES, rows, LANES), jnp.float32)],
        flags, slot_of, arrived, smem=2,
    )
    chi_x = swap("gx", lambda up, n: chi_out[n])
    first_x, first_y, chi_x = lax.optimization_barrier((first_x, first_y, chi_x))
    slabs = lambda v: v.reshape(-1, rows, lanes)
    far_x = len(first_x) * 4 * (START_W + FINE_W)
    chi_slabs = planes + len(chi_x) * FINE_W
    n_x, n_y, n_z = pair_counts
    y_sent = call(
        functools.partial(
            y_kernel,
            take=[planes, *[x.shape[0] for x in (*chi_x[::-1], *first_x[::-1])]],
            order=[0, *range(n_x, 0, -1), *range(2 * n_x, n_x, -1)],
            added=0,
        ),
        [(chi_slabs + far_x, CORNER, lanes)] * n_y,
        [],
        flags, slabs(chi), *chi_x[::-1], *first_x[::-1], chi_x[0][0, :1, :LANES],
    )
    far_y = swap("gy", lambda up, n: y_sent[n])
    per = rows // PAD
    edges = -(-chi_slabs // per) + -(-(8 * planes + far_x) // per)
    whole = lambda first, refs: [(first + i, 0, r.shape[0]) for i, r in enumerate(refs)]
    far_at = 1 + 2 * n_x + n_y
    plan = [
        ([(0, 0, planes), *whole(1, chi_x)], [[(far_at + n, 0, chi_slabs)] for n in range(n_y)]),
        (
            whole(1 + n_x, first_x),
            [[(1 + 2 * n_x + n, 0, 8 * planes), (far_at + n, chi_slabs, chi_slabs + far_x)] for n in range(n_y)],
        ),
    ]
    z_sent = call(
        functools.partial(z_kernel, plan=plan, count=far_at + n_y, added=0),
        [(chi_slabs + far_x + n_y * edges, rows, LANES)] * n_z,
        [],
        flags, slabs(chi), *chi_x, *first_x, *first_y, *far_y,
    )
    far_z = swap("lvl", lambda up, n: z_sent[n])
    c_slabs, s_slabs = 5 * c_planes, 4 * (rows // 8) * (lanes // LANES)
    outers = [[(c_slabs + s_slabs, 8, LANES)], [(4 * (planes + 2) // 2, PAD, LANES)], [(4 * (planes + 2) * total // 8, 8, LANES)]]
    outers = [shape * n for shape, n in zip(outers, pair_counts)]
    rhs, state, weight, *sent = call(
        functools.partial(second_kernel, nums=pair_counts),
        [(4, far, total, wide), (4, near, total, wide), (far, total, wide), *sum(outers, [])],
        [
            pltpu.VMEM((1, far, total, wide), jnp.float32),
            pltpu.VMEM((4, planes + 2 * START_W, total, wide), jnp.float32),
            pltpu.VMEM((4, far, total, wide), jnp.float32),
            pltpu.VMEM((4, lanes // LANES, rows, LANES), jnp.float32),
            pltpu.VMEM((5, c_planes, c_rows, lanes), jnp.float32),
        ],
        flags, chi, pooled_chi, right_side, start_field, *chi_x, *first_x, *first_y, *first_z, *far_y, *far_z,
    )
    (x_out, y_out, z_out), _ = split(sent, pair_counts)
    last_x = swap("gx", lambda up, n: x_out[n])
    take = [c_slabs, *[5 * COARSE_W] * n_x]
    y_sent = call(
        functools.partial(y_kernel, take=take, order=[0, *range(n_x, 0, -1)], added=n_y),
        [(sum(take) + y_out[0].shape[0], COARSE_W, c_lanes)] * n_y,
        [],
        flags, x_out[0], *last_x[::-1], *y_out, last_x[0][0, :1, :LANES],
    )
    last_y = swap("gy", lambda up, n: y_sent[n])
    plan = [([(i, 0, t) for i, t in enumerate(take)], [[(1 + n_x + n, 0, sum(take))] for n in range(n_y)])]
    z_slabs = sum(take) + n_y * -(-sum(take) // (c_rows // PAD))
    z_sent = call(
        functools.partial(z_kernel, plan=plan, count=1 + n_x + n_y, added=n_z),
        [(z_slabs + z_out[0].shape[0], c_rows, LANES)] * n_z,
        [],
        flags, x_out[0], *last_x, *last_y, *z_out,
    )
    last_z = swap("lvl", lambda up, n: z_sent[n])
    c_ext = (c_planes + 2 * COARSE_W, c_rows + 8, c_lanes + LANES)
    (out,) = call(
        functools.partial(last_kernel, nums=pair_counts),
        [right_side.shape],
        [
            pltpu.VMEM((5, *c_ext), jnp.float32),
            pltpu.VMEM((4, *c_ext), jnp.float32),
            pltpu.VMEM((4, *c_ext), jnp.float32),
            pltpu.VMEM((4, near, total, wide), jnp.float32),
            pltpu.VMEM((4, near, total, wide), jnp.float32),
            pltpu.VMEM((wide // LANES, total, LANES), jnp.float32),
        ],
        flags, x_out[0], state, weight, rhs, *last_x, *last_y, *last_z,
    )
    return out


def solution(mesh):
    in_specs = (
        P(None, "gx", "gy", "lvl"),
        P(None, "gx", "gy", "lvl"),
        P(("gx", "gy", "lvl"), None),
        P(),
        P(),
    )
    out_specs = P(None, "gx", "gy", "lvl")
    return jax.shard_map(body, mesh=mesh, in_specs=in_specs, out_specs=out_specs, check_vma=False)
```

```python
import functools

import jax
import jax.numpy as jnp
from jax import lax
from jax.experimental import pallas as pl
from jax.experimental.pallas import tpu as pltpu
from jax.sharding import PartitionSpec as P

COARSE_SWEEPS = 4
SHIFT = 0.05
RELAX = 0.6
KEEP = 1.0 - RELAX
LANES = 128
START_W = 3
FINE_W = 2
CORNER = 2
STATE_W = 2
COARSE_W = 4
PAD = 4
HIGHEST = lax.Precision.HIGHEST
VMEM = pl.BlockSpec(memory_space=pltpu.VMEM)
SMEM = pl.BlockSpec(memory_space=pltpu.SMEM)
PARAMS = pltpu.CompilerParams(vmem_limit_bytes=24 << 20)


def pairs(count, first):
    return [p for i in range(first, count - 1, 2) for p in ((i, i + 1), (i + 1, i))]


def cut(values, dim, width, to_next):
    size = values.shape[dim]
    if size == width:
        return values
    start = jnp.where(to_next, size - width, 0)
    return lax.dynamic_slice_in_dim(values, start, width, axis=dim)


def flat(parts):
    return jnp.concatenate([p.reshape(-1, *p.shape[-2:]) for p in parts], axis=0)


def swap(axis, message):
    count = lax.axis_size(axis)
    even = lax.axis_index(axis) % 2 == 0
    got = [lax.ppermute(message(~even, 1), axis, pairs(count, 1))] if count > 2 else []
    got.insert(0, lax.ppermute(message(even, 0), axis, pairs(count, 0)))
    return got


def halo_x(groups):
    return swap("gx", lambda up, n: flat([cut(v, 1, w, up) for v, w in groups]))


def place_halo(dst, margin, own, got, flags, width, depth, group=(0, 0), slabs=None, corner=0, base=(0, 0), early=()):
    xs, ys, zs = got
    rows, lanes = own.shape[-2:]
    fields, planes, total = dst.shape[0], dst.shape[1] - 2 * margin, dst.shape[2]
    own_slabs, x_slabs = slabs or (fields * planes, fields * width)
    pairs_y = len(ys) // 2 if corner else len(ys)
    slab_count = own_slabs + len(xs) * x_slabs
    per = rows // PAD
    even_x, even_y, even_z = flags[0] == 1, flags[1] == 1, flags[2] == 1
    near = (lax.broadcasted_iota(jnp.int32, (1, LANES), 1) < LANES // 2) == even_z

    def edge(at, row, size):
        part = slice(row, row + size)
        if early and at < own_slabs:
            return jnp.where(near, early[0][at, part], 0.0 if len(zs) == 1 else early[1][at, part])
        at = base[1] + at - (own_slabs if early else 0)
        return jnp.where(near, zs[0][at, part], 0.0 if len(zs) == 1 else zs[1][at, part])

    for f in range(fields):
        for k in range(planes + len(xs) * width):
            deep = depth
            if k < planes:
                at, plane, slab = margin + k, own[f, k] if len(own.shape) == 4 else own[f * planes + k], group[0] + f * planes + k
            else:
                which, j = divmod(k - planes, width)
                up, down = margin + planes + j, margin - width + j
                at = jnp.where(even_x, up, down) if which == 0 else jnp.where(even_x, down, up)
                plane = xs[which][group[1] + f * width + j]
                slab = own_slabs + which * x_slabs + group[1] + f * width + j
                deep = corner or depth
            dst[f, at, 0:rows, 0:lanes] = plane
            dst[f, at, 0:rows, lanes:] = edge(slab, 0, rows)
            sides = []
            for n in range(pairs_y):
                at_z = slab_count + n * (-(-slab_count // per)) + slab // per
                if corner and k >= planes:
                    y = ys[pairs_y + n][base[0] + slab - own_slabs]
                else:
                    y = ys[n][slab]
                sides.append((y, edge(at_z, slab % per * PAD, deep)))
            if len(sides) == 1:
                sides.append([jnp.zeros_like(v) for v in sides[0]])
            for to, first, second in zip((slice(0, lanes), slice(lanes, lanes + LANES)), *sides):
                dst[f, at, rows:rows + deep, to] = jnp.where(even_y, first, second)
                dst[f, at, total - deep:total, to] = jnp.where(even_y, second, first)
            gap = total - rows - 2 * deep
            if gap:
                dst[f, at, rows + deep:total - deep, :] = jnp.zeros((gap, dst.shape[3]), jnp.float32)


def place_outer(out, state, got, flags, before):
    xs, ys, zs = got
    fields, near, total, wide = state.shape
    planes, rows, lanes = near - 2 * STATE_W, total - 8, wide - LANES
    even_x, even_y, even_z = flags[0] == 1, flags[1] == 1, flags[2] == 1
    side = (lax.broadcasted_iota(jnp.int32, (1, LANES), 1) < LANES // 2) == even_z
    tiles = [(r, z) for r in range(rows // 8) for z in range(lanes // LANES)]
    for f in range(fields):
        for k in range(planes + 2):
            p, slab = STATE_W - 1 + k, f * (planes + 2) + k
            out[f, p, :, 0:lanes] = state[f, p, :, 0:lanes]
            for r in range(total // 8):
                at = before[2] + slab * (total // 8) + r
                z = jnp.where(side, zs[0][at], 0.0 if len(zs) == 1 else zs[1][at])
                out[f, p, r * 8:(r + 1) * 8, lanes:] = z
            out_by = 1 if 0 < k <= planes else 0
            for z in range(lanes // LANES):
                at, row = before[1] + slab // 2, slab % 2 * 2 + z
                first = ys[0][at, row:row + 1]
                second = ys[1][at, row:row + 1] if len(ys) > 1 else jnp.zeros_like(first)
                to = slice(z * LANES, (z + 1) * LANES)
                out[f, p, rows + out_by:rows + out_by + 1, to] = jnp.where(even_y, first, second)
                out[f, p, total - 1 - out_by:total - out_by, to] = jnp.where(even_y, second, first)
        for p in (0, near - 1):
            out[f, p] = jnp.zeros((total, wide), jnp.float32)
            is_first = even_x if p else ~even_x
            for t, (r, z) in enumerate(tiles):
                at = before[0] + f * len(tiles) + t
                first = xs[0][at]
                second = xs[1][at] if len(xs) > 1 else jnp.zeros_like(first)
                out[f, p, r * 8:(r + 1) * 8, z * LANES:(z + 1) * LANES] = jnp.where(is_first, first, second)


def send_outer(state, flags, x_out, y_out, z_out, before):
    fields, near, total, wide = state.shape
    planes, rows, lanes = near - 2 * STATE_W, total - 8, wide - LANES
    up = [[(flags[a] == 1) == (n == 0) for n in range(2)] for a in range(3)]
    tiles = [(r, z) for r in range(rows // 8) for z in range(lanes // LANES)]
    for n, ref in enumerate(x_out):
        p = jnp.where(up[0][n], STATE_W + planes - 2, STATE_W + 1)
        for f in range(fields):
            for t, (r, z) in enumerate(tiles):
                ref[before + f * len(tiles) + t] = state[f, p, r * 8:(r + 1) * 8, z * LANES:(z + 1) * LANES]
    for f in range(fields):
        for k in range(planes + 2):
            p, slab = STATE_W - 1 + k, f * (planes + 2) + k
            out_by = 1 if 0 < k <= planes else 0
            for n, ref in enumerate(y_out):
                high = state[f, p, rows - 1 - out_by:rows - out_by, 0:lanes]
                v = jnp.where(up[1][n], high, state[f, p, out_by:out_by + 1, 0:lanes])
                for z in range(lanes // LANES):
                    row = slab % 2 * 2 + z
                    ref[slab // 2, row:row + 1] = v[:, z * LANES:(z + 1) * LANES]
            for n, ref in enumerate(z_out):
                for r in range(total // 8):
                    part = slice(r * 8, (r + 1) * 8)
                    v = jnp.where(up[2][n], state[f, p, part, lanes - LANES:lanes], state[f, p, part, 0:LANES])
                    ref[slab * (total // 8) + r] = v


def inside(flags, rows, lanes, total, depth):
    row = lax.broadcasted_iota(jnp.int32, (total, lanes + LANES), 0)
    lane = lax.broadcasted_iota(jnp.int32, (total, lanes + LANES), 1)
    end = lanes + LANES
    row_ok = (row < rows) | ((row < rows + depth) & (flags[5] == 1)) | ((row >= total - depth) & (flags[6] == 1))
    lane_ok = (lane < lanes) | ((lane < lanes + depth) & (flags[7] == 1)) | ((lane >= end - depth) & (flags[8] == 1))
    return jnp.where(row_ok & lane_ok, 1.0, 0.0)


def plane_inside(flags, p, margin, planes):
    return jnp.where(p < margin, flags[4], jnp.where(p >= margin + planes, flags[3], 1)).astype(jnp.float32)


def put(ref, at, v, margin, planes, rows, lanes, reach):
    p = at[-1]
    reach = reach - max(margin - p, p - margin - planes + 1, 0)
    if reach >= 2:
        ref[at] = v
        return
    ends = v.shape
    ref[(*at, slice(0, rows), slice(0, lanes))] = v[0:rows, 0:lanes]
    for r, z in ((slice(0, rows), slice(lanes, ends[1])), (slice(rows, ends[0]), slice(0, lanes))):
        ref[(*at, r, z)] = v[r, z] if reach == 1 else jnp.zeros((r.stop - r.start, z.stop - z.start), jnp.float32)
    ref[(*at, slice(rows, ends[0]), slice(lanes, ends[1]))] = jnp.zeros((ends[0] - rows, ends[1] - lanes), jnp.float32)


def neighbours(ref, p):
    rows, lanes = ref.shape[2], ref.shape[3]
    sums, grads, spread = [], [], 0.0
    for f in range(4):
        c, xn, xp = ref[f, p], ref[f, p + 1], ref[f, p - 1]
        yn, yp = pltpu.roll(c, rows - 1, 0), pltpu.roll(c, 1, 0)
        zn, zp = pltpu.roll(c, lanes - 1, 1), pltpu.roll(c, 1, 1)
        sums.append((xn + xp) + (yn + yp) + (zn + zp))
        if f == 3:
            grads = [xn - xp, yn - yp, zn - zp]
        else:
            spread = spread + (xn - xp, yn - yp, zn - zp)[f]
    return sums, grads + [spread]


def pack_kernel(tile_ref, mask_ref, out_ref, used_ref, rows_ref, *, capacity):
    tiles = out_ref.shape[0]
    count, width = mask_ref.shape
    out_ref[...] = jnp.zeros(out_ref.shape, jnp.float32)
    for r in range(0, count, 8):
        rows_ref[r:r + 8] = mask_ref[r:r + 8].reshape(8, width // LANES, LANES)

    def clear(t, _):
        used_ref[t] = 0
        return 0

    lax.fori_loop(0, tiles, clear, 0, unroll=8)

    def row(r, _):
        t = tile_ref[r]
        n = used_ref[t]
        used_ref[t] = n + 1
        out_ref[t, jnp.minimum(n, capacity - 1)] = rows_ref[r]
        return 0

    lax.fori_loop(0, count, row, 0, unroll=8)


def split(refs, nums):
    at, got = 0, []
    for n in nums:
        got.append(refs[at:at + n])
        at += n
    return got, refs[at:]


def chi_kernel(slot_ref, rows_ref, out, coarse_out, acc, pooled):
    _, planes, rows, lanes = out.shape
    acc[...] = jnp.zeros(acc.shape, jnp.float32)
    per = rows_ref.shape[1]

    def add(s, _):
        for c in range(per):
            at = pl.ds(pl.multiple_of(slot_ref[s * per + c] * 8, 8), 8)
            acc[at, :] = acc[at, :] + rows_ref[s, c]
        return 0

    lax.fori_loop(0, rows_ref.shape[0], add, 0)
    z_tiles = lanes // LANES
    across = rows // 2
    for qx in range(planes // 2):
        for zt in range(z_tiles):
            total = None
            for i in range(2):
                for j in range(2):
                    v = acc[pl.ds(qx * across * 8 + (2 * i + j) * z_tiles + zt, across, stride=8), :]
                    pooled[zt, pl.ds(j, across, stride=2), :] = v
                    total = v if total is None else total + v
                out[0, 2 * qx + i, :, zt * LANES:(zt + 1) * LANES] = pooled[zt]
            coarse_out[qx, :, zt * LANES:(zt + 1) * LANES] = total


def side(up, v, dim, width):
    size = v.shape[dim]
    low = v[..., 0:width] if dim == 1 else v[0:width]
    high = v[..., size - width:] if dim == 1 else v[size - width:]
    return jnp.where(up, high, low)


def y_kernel(flags, *refs, take, order, added):
    ready, (_, *outs) = split(refs[len(take):], [added])
    for n, out in enumerate(outs):
        up = (flags[1] == 1) == (n == 0)
        at = 0
        for i in order:
            ref, count = refs[i], take[i]
            for s in range(count):
                out[at] = side(up, ref[s], 0, out.shape[1])
                at += 1
        if added:
            out[at:] = ready[0][n][...]


def z_kernel(flags, *refs, plan, count, added):
    ready, outs = split(refs[count:], [added])
    for n, out in enumerate(outs):
        up = (flags[2] == 1) == (n == 0)
        per = out.shape[1] // PAD
        at = 0
        for slabs, edges in plan:
            for i, low, high in slabs:
                for s in range(low, high):
                    out[at] = side(up, refs[i][s], 1, LANES)
                    at += 1
            for parts in edges:
                k = 0
                for i, low, high in parts:
                    for s in range(low, high):
                        depth = refs[i].shape[1]
                        row = k % per * PAD
                        out[at + k // per, row:row + depth] = side(up, refs[i][s], 1, LANES)
                        if depth < PAD:
                            out[at + k // per, row + depth:row + PAD] = jnp.zeros((PAD - depth, LANES), jnp.float32)
                        k += 1
                while k % per:
                    row = k % per * PAD
                    out[at + k // per, row:row + PAD] = jnp.zeros((PAD, LANES), jnp.float32)
                    k += 1
                at += k // per
        if added:
            out[at:] = ready[0][n][...]


def second_kernel(flags, own, pooled_chi, right_side, start_field, *refs, nums):
    n_x, n_y, n_z = nums
    (chi_x, first_x, first_y, first_z, far_y, far_z), refs = split(refs, [n_x, n_x, n_y, n_z, n_y, n_z])
    rhs, state_out, weight_out = refs[:3]
    (x_out, y_out, z_out), (chi, start, ext, tmp, pooled) = split(refs[3:], nums)
    _, planes, rows, lanes = own.shape
    total = ext.shape[2]
    chi_slabs = planes + n_x * FINE_W
    base = (chi_slabs, chi_slabs + n_y * -(-chi_slabs // (rows // PAD)))
    slabs = (8 * planes, 4 * (START_W + FINE_W))
    fields_got = (first_x, (*first_y, *far_y), far_z)
    place_halo(chi, FINE_W, own, (chi_x, far_y, far_z), flags, FINE_W, FINE_W)
    place_halo(start, START_W, start_field, fields_got, flags, START_W, START_W, (0, 0), slabs, CORNER, base, first_z)
    place_halo(rhs, FINE_W, right_side, fields_got, flags, FINE_W, START_W, (4 * planes, 4 * START_W), slabs, CORNER, base, first_z)
    mask = inside(flags, rows, lanes, total, FINE_W)
    w_p = (RELAX / (SHIFT + 6.0)) * mask

    for k in range(planes + 2 * FINE_W):
        here = plane_inside(flags, k, FINE_W, planes)
        w_u = (RELAX / (SHIFT + 6.0 + chi[0, k])) * (mask * here)
        put(weight_out, (k,), w_u, FINE_W, planes, rows, lanes, FINE_W)
        sums, grads = neighbours(start, k + START_W - FINE_W)
        for f in range(4):
            w = w_u if f < 3 else w_p * here
            v = KEEP * start[f, k + START_W - FINE_W] + w * (rhs[f, k] + sums[f] - 0.5 * grads[f])
            put(ext, (f, k), v, FINE_W, planes, rows, lanes, FINE_W)

    for p in range(1, planes + 2 * FINE_W - 1):
        here = plane_inside(flags, p, FINE_W, planes)
        sums, grads = neighbours(ext, p)
        w_u = weight_out[p]
        for f in range(4):
            w = w_u if f < 3 else w_p * here
            v = KEEP * ext[f, p] + w * (rhs[f, p] + sums[f] - 0.5 * grads[f])
            put(state_out, (f, p), v, FINE_W, planes, rows, lanes, FINE_W - 1)

    for cx in range(planes // 2):
        both = [None] * 4
        for i in range(2):
            p = FINE_W + 2 * cx + i
            sums, grads = neighbours(state_out, p)
            for f in range(4):
                diag = SHIFT + 6.0 + (chi[0, p] if f < 3 else 0.0)
                r = rhs[f, p] + sums[f] - 0.5 * grads[f] - diag * state_out[f, p]
                both[f] = r if i == 0 else both[f] + r
        for f in range(4):
            for zt in range(lanes // LANES):
                tmp[f, zt] = both[f][0:rows, zt * LANES:(zt + 1) * LANES]
                v = tmp[f, zt, pl.ds(0, rows // 2, stride=2), :] + tmp[f, zt, pl.ds(1, rows // 2, stride=2), :]
                pooled[f, cx, :, zt * LANES:(zt + 1) * LANES] = v
    pooled[4] = pooled_chi[...]
    lane = lax.broadcasted_iota(jnp.int32, (lanes, lanes // 2), 0)
    cell = lax.broadcasted_iota(jnp.int32, (lanes, lanes // 2), 1)
    gather = jnp.where(lane // 2 == cell, 0.125, 0.0)
    flat_rows = pooled[...].reshape(5 * planes // 2 * rows // 2, lanes)
    coarse = jnp.dot(flat_rows, gather, precision=HIGHEST, preferred_element_type=jnp.float32)
    coarse = coarse.reshape(5 * planes // 2, rows // 2, lanes // 2)
    for ref in x_out:
        ref[0:coarse.shape[0]] = coarse
    send_outer(state_out, flags, x_out, y_out, z_out, coarse.shape[0])


def last_kernel(flags, own, state, weight, rhs, *refs, nums):
    got, (out, ext, one, two, fine, mid, tmp) = split(refs, nums)
    planes = ext.shape[1] - 2 * COARSE_W
    rows, lanes = own.shape[1:]
    total, wide = ext.shape[2], ext.shape[3]
    own = own.at[0:5 * planes]
    place_halo(ext, COARSE_W, own, got[:3], flags, COARSE_W, COARSE_W)
    x_slabs = 5 * COARSE_W
    slabs = 5 * planes + len(got[0]) * x_slabs
    z_slabs = slabs + len(got[1]) * -(-slabs // (rows // PAD))
    place_outer(fine, state, got, flags, (x_slabs, slabs, z_slabs))
    mask = inside(flags, rows, lanes, total, COARSE_W)
    w_p = (RELAX / (SHIFT + 1.5)) * mask

    for p in range(planes + 2 * COARSE_W):
        here = plane_inside(flags, p, COARSE_W, planes)
        w_u = (RELAX / (SHIFT + 1.5 + ext[4, p])) * (mask * here)
        ext[4, p] = w_u
        for f in range(4):
            one[f, p] = (w_u if f < 3 else w_p * here) * ext[f, p]
    now, then = one, two
    for s in range(1, COARSE_SWEEPS):
        for p in range(s, planes + 2 * COARSE_W - s):
            here = plane_inside(flags, p, COARSE_W, planes)
            sums, grads = neighbours(now, p)
            for f in range(4):
                w = ext[4, p] if f < 3 else w_p * here
                v = KEEP * now[f, p] + w * (ext[f, p] + 0.25 * (sums[f] - grads[f]))
                put(then, (f, p), v, COARSE_W, planes, rows, lanes, COARSE_W + 1 - s)
        now, then = then, now

    f_total, f_wide = fine.shape[2], fine.shape[3]
    f_rows, f_lanes = 2 * rows, 2 * lanes
    cell = lax.broadcasted_iota(jnp.int32, (wide, f_wide), 0)
    lane = lax.broadcasted_iota(jnp.int32, (wide, f_wide), 1)
    from_cell = jnp.where(lane < f_lanes + LANES // 2, lane // 2, wide - 1 - (f_wide - 1 - lane) // 2)
    spread = jnp.where(cell == from_cell, 1.0, 0.0)
    c_planes = planes + 2
    flat = now[:, COARSE_W - 1:COARSE_W - 1 + c_planes].reshape(4 * c_planes * total, wide)
    grown = jnp.dot(flat, spread, precision=HIGHEST, preferred_element_type=jnp.float32)
    for f in range(4):
        for cp in range(c_planes):
            lo = (f * c_planes + cp) * total
            for zt in range(f_wide // LANES):
                v = grown[lo:lo + total, zt * LANES:(zt + 1) * LANES]
                at = f * c_planes + cp
                for j in range(2):
                    tmp[zt, pl.ds(j, rows, stride=2), :] = v[0:rows]
                    tmp[zt, pl.ds(f_rows + j, 2, stride=2), :] = v[rows:rows + 2]
                    tmp[zt, pl.ds(f_total - 4 + j, 2, stride=2), :] = v[total - 2:total]
                for i in range(2):
                    to = slice(zt * LANES, (zt + 1) * LANES)
                    fine[f, 2 * cp + i, :, to] = fine[f, 2 * cp + i, :, to] + tmp[zt]
    f_planes = 2 * planes
    f_mask = inside(flags, f_rows, f_lanes, f_total, STATE_W)
    off = FINE_W - STATE_W
    w_q = (RELAX / (SHIFT + 6.0)) * f_mask

    for p in range(1, f_planes + 3):
        here = plane_inside(flags, p, STATE_W, f_planes)
        sums, grads = neighbours(fine, p)
        for f in range(4):
            w = weight[p + off] if f < 3 else w_q * here
            v = KEEP * fine[f, p] + w * (rhs[f, p + off] + sums[f] - 0.5 * grads[f])
            put(mid, (f, p), v, STATE_W, f_planes, f_rows, f_lanes, 1)

    for k in range(f_planes):
        p = k + 2
        sums, grads = neighbours(mid, p)
        for f in range(4):
            w = weight[p + off] if f < 3 else w_q
            v = KEEP * mid[f, p] + w * (rhs[f, p + off] + sums[f] - 0.5 * grads[f])
            out[f, k] = v[0:f_rows, 0:f_lanes]


def call(kernel, shapes, scratch, *args, smem=1):
    outs = [jax.ShapeDtypeStruct(s, jnp.float32) for s in shapes]
    return pl.pallas_call(
        kernel,
        out_shape=outs,
        in_specs=[SMEM] * smem + [VMEM] * (len(args) - smem),
        out_specs=[VMEM] * len(outs),
        scratch_shapes=scratch,
        compiler_params=PARAMS,
    )(*args)


def routes(block_tile, block_slot, tiles, count_l, per_device, capacity, slots):
    my_tile = lax.axis_index("gx") * lax.axis_size("gy") + lax.axis_index("gy")
    index_l = lax.axis_index("lvl")
    their_tiles = lax.dynamic_index_in_dim(block_tile.reshape(tiles, count_l, per_device), index_l, 1, keepdims=False)
    their_slots = lax.dynamic_index_in_dim(block_slot.reshape(tiles, count_l, per_device), index_l, 1, keepdims=False)
    arriving = their_tiles == my_tile
    counter = jnp.arange(per_device, dtype=jnp.int32)
    earlier = counter[None, :, None] < counter[None, None, :]
    order = jnp.sum(jnp.where(arriving[:, :, None] & earlier, 1, 0), axis=1)
    places = jnp.arange(capacity, dtype=jnp.int32)
    hit = arriving[:, None, :] & (order[:, None, :] == places[None, :, None])
    slot = jnp.sum(jnp.where(hit, their_slots[:, None, :] - slots, 0), axis=2) + slots
    return slot.reshape(-1)


def body(right_side, start_field, mask_blocks, block_tile, block_slot):
    axes = ("gx", "gy", "lvl")
    counts = [lax.axis_size(a) for a in axes]
    index = [lax.axis_index(a) for a in axes]
    tiles = counts[0] * counts[1]
    per_device, width = mask_blocks.shape
    capacity = max(2, 2 * per_device // tiles)
    _, planes, rows, lanes = right_side.shape
    slots = planes // 2 * (rows // 2)
    c_planes, c_rows, c_lanes = planes // 2, rows // 2, lanes // 2
    flags = [i % 2 == 0 for i in index]
    for i, n in zip(index, counts):
        flags += [i < n - 1, i > 0]
    flags = jnp.stack(flags).astype(jnp.int32)

    my_flat = (index[0] * counts[1] + index[1]) * counts[2] + index[2]
    tile_ids = block_tile[:, 0]
    my_tiles = lax.dynamic_slice_in_dim(tile_ids, my_flat * per_device, per_device)
    (outgoing,) = call(
        functools.partial(pack_kernel, capacity=capacity),
        [(tiles, capacity, width // LANES, LANES)],
        [pltpu.SMEM((tiles,), jnp.int32), pltpu.VMEM((per_device, width // LANES, LANES), jnp.float32)],
        my_tiles, mask_blocks,
    )
    outgoing, right_side, start_field = lax.optimization_barrier((outgoing, right_side, start_field))
    arrived = lax.all_to_all(outgoing, ("gx", "gy"), split_axis=0, concat_axis=0, tiled=True)
    slot_of = routes(tile_ids, block_slot, tiles, counts[2], per_device, capacity, slots)

    total, wide = rows + 8, lanes + LANES
    near, far = planes + 2 * STATE_W, planes + 2 * FINE_W
    pair_counts = [1 + (n > 2) for n in counts]
    groups = [(start_field, START_W), (right_side, FINE_W)]
    first_x = halo_x(groups)
    first_y = swap("gy", lambda up, n: flat([cut(v, 2, START_W, up) for v, _ in groups]))
    first_z = swap("lvl", lambda up, n: flat([cut(v, 3, LANES, up) for v, _ in groups]))
    first_y, first_z, slot_of = lax.optimization_barrier((first_y, first_z, slot_of))
    chi, pooled_chi = call(
        chi_kernel,
        [(1, planes, rows, lanes), (c_planes, c_rows, lanes)],
        [pltpu.VMEM(((slots + 1) * 8, LANES), jnp.float32), pltpu.VMEM((lanes // LANES, rows, LANES), jnp.float32)],
        slot_of, arrived,
    )
    group = [(chi, FINE_W)]
    chi_x = halo_x(group)
    first_x, chi_x = lax.optimization_barrier((first_x, chi_x))
    slabs = lambda v: v.reshape(-1, rows, lanes)
    far_x = len(first_x) * 4 * (START_W + FINE_W)
    chi_slabs = planes + len(chi_x) * FINE_W
    n_x, n_y, n_z = pair_counts
    y_sent = call(
        functools.partial(
            y_kernel,
            take=[planes, *[x.shape[0] for x in (*chi_x[::-1], *first_x[::-1])]],
            order=[0, *range(n_x, 0, -1), *range(2 * n_x, n_x, -1)],
            added=0,
        ),
        [(chi_slabs + far_x, CORNER, lanes)] * n_y,
        [],
        flags, slabs(chi), *chi_x[::-1], *first_x[::-1], chi_x[0][0, :1, :LANES],
    )
    far_y = swap("gy", lambda up, n: y_sent[n])
    per = rows // PAD
    edges = -(-chi_slabs // per) + -(-(8 * planes + far_x) // per)
    whole = lambda first, refs: [(first + i, 0, r.shape[0]) for i, r in enumerate(refs)]
    far_at = 1 + 2 * n_x + n_y
    plan = [
        ([(0, 0, planes), *whole(1, chi_x)], [[(far_at + n, 0, chi_slabs)] for n in range(n_y)]),
        (
            whole(1 + n_x, first_x),
            [[(1 + 2 * n_x + n, 0, 8 * planes), (far_at + n, chi_slabs, chi_slabs + far_x)] for n in range(n_y)],
        ),
    ]
    z_sent = call(
        functools.partial(z_kernel, plan=plan, count=far_at + n_y, added=0),
        [(chi_slabs + far_x + n_y * edges, rows, LANES)] * n_z,
        [],
        flags, slabs(chi), *chi_x, *first_x, *first_y, *far_y,
    )
    far_z = swap("lvl", lambda up, n: z_sent[n])
    c_slabs, s_slabs = 5 * c_planes, 4 * (rows // 8) * (lanes // LANES)
    outers = [[(c_slabs + s_slabs, 8, LANES)], [(4 * (planes + 2) // 2, PAD, LANES)], [(4 * (planes + 2) * total // 8, 8, LANES)]]
    outers = [shape * n for shape, n in zip(outers, pair_counts)]
    rhs, state, weight, *sent = call(
        functools.partial(second_kernel, nums=pair_counts),
        [(4, far, total, wide), (4, near, total, wide), (far, total, wide), *sum(outers, [])],
        [
            pltpu.VMEM((1, far, total, wide), jnp.float32),
            pltpu.VMEM((4, planes + 2 * START_W, total, wide), jnp.float32),
            pltpu.VMEM((4, far, total, wide), jnp.float32),
            pltpu.VMEM((4, lanes // LANES, rows, LANES), jnp.float32),
            pltpu.VMEM((5, c_planes, c_rows, lanes), jnp.float32),
        ],
        flags, chi, pooled_chi, right_side, start_field, *chi_x, *first_x, *first_y, *first_z, *far_y, *far_z,
    )
    (x_out, y_out, z_out), _ = split(sent, pair_counts)
    last_x = swap("gx", lambda up, n: x_out[n])
    take = [c_slabs, *[5 * COARSE_W] * n_x]
    y_sent = call(
        functools.partial(y_kernel, take=take, order=[0, *range(n_x, 0, -1)], added=n_y),
        [(sum(take) + y_out[0].shape[0], COARSE_W, c_lanes)] * n_y,
        [],
        flags, x_out[0], *last_x[::-1], *y_out, last_x[0][0, :1, :LANES],
    )
    last_y = swap("gy", lambda up, n: y_sent[n])
    plan = [([(i, 0, t) for i, t in enumerate(take)], [[(1 + n_x + n, 0, sum(take))] for n in range(n_y)])]
    z_slabs = sum(take) + n_y * -(-sum(take) // (c_rows // PAD))
    z_sent = call(
        functools.partial(z_kernel, plan=plan, count=1 + n_x + n_y, added=n_z),
        [(z_slabs + z_out[0].shape[0], c_rows, LANES)] * n_z,
        [],
        flags, x_out[0], *last_x, *last_y, *z_out,
    )
    last_z = swap("lvl", lambda up, n: z_sent[n])
    c_ext = (c_planes + 2 * COARSE_W, c_rows + 8, c_lanes + LANES)
    (out,) = call(
        functools.partial(last_kernel, nums=pair_counts),
        [right_side.shape],
        [
            pltpu.VMEM((5, *c_ext), jnp.float32),
            pltpu.VMEM((4, *c_ext), jnp.float32),
            pltpu.VMEM((4, *c_ext), jnp.float32),
            pltpu.VMEM((4, near, total, wide), jnp.float32),
            pltpu.VMEM((4, near, total, wide), jnp.float32),
            pltpu.VMEM((wide // LANES, total, LANES), jnp.float32),
        ],
        flags, x_out[0], state, weight, rhs, *last_x, *last_y, *last_z,
    )
    return out


def solution(mesh):
    in_specs = (
        P(None, "gx", "gy", "lvl"),
        P(None, "gx", "gy", "lvl"),
        P(("gx", "gy", "lvl"), None),
        P(),
        P(),
    )
    out_specs = P(None, "gx", "gy", "lvl")
    return jax.shard_map(body, mesh=mesh, in_specs=in_specs, out_specs=out_specs, check_vma=False)
```

```python
import functools

import jax
import jax.numpy as jnp
from jax import lax
from jax.experimental import pallas as pl
from jax.experimental.pallas import tpu as pltpu
from jax.sharding import PartitionSpec as P

COARSE_SWEEPS = 4
SHIFT = 0.05
RELAX = 0.6
KEEP = 1.0 - RELAX
LANES = 128
START_W = 3
FINE_W = 2
CORNER = 2
STATE_W = 2
COARSE_W = 4
PAD = 4
HIGHEST = lax.Precision.HIGHEST
VMEM = pl.BlockSpec(memory_space=pltpu.VMEM)
SMEM = pl.BlockSpec(memory_space=pltpu.SMEM)
PARAMS = pltpu.CompilerParams(vmem_limit_bytes=24 << 20)


def pairs(count, first):
    return [p for i in range(first, count - 1, 2) for p in ((i, i + 1), (i + 1, i))]


def cut(values, dim, width, to_next):
    size = values.shape[dim]
    if size == width:
        return values
    start = jnp.where(to_next, size - width, 0)
    return lax.dynamic_slice_in_dim(values, start, width, axis=dim)


def flat(parts):
    return jnp.concatenate([p.reshape(-1, *p.shape[-2:]) for p in parts], axis=0)


def swap(axis, message):
    count = lax.axis_size(axis)
    even = lax.axis_index(axis) % 2 == 0
    got = [lax.ppermute(message(~even, 1), axis, pairs(count, 1))] if count > 2 else []
    got.insert(0, lax.ppermute(message(even, 0), axis, pairs(count, 0)))
    return got


def halo_x(groups):
    return swap("gx", lambda up, n: flat([cut(v, 1, w, up) for v, w in groups]))


def place_halo(dst, margin, own, got, flags, width, depth, group=(0, 0), slabs=None, corner=0, base=(0, 0), early=()):
    xs, ys, zs = got
    rows, lanes = own.shape[-2:]
    fields, planes, total = dst.shape[0], dst.shape[1] - 2 * margin, dst.shape[2]
    own_slabs, x_slabs = slabs or (fields * planes, fields * width)
    pairs_y = len(ys) // 2 if corner else len(ys)
    slab_count = own_slabs + len(xs) * x_slabs
    per = rows // PAD
    even_x, even_y, even_z = flags[0] == 1, flags[1] == 1, flags[2] == 1
    near = (lax.broadcasted_iota(jnp.int32, (1, LANES), 1) < LANES // 2) == even_z

    def edge(at, row, size):
        part = slice(row, row + size)
        if early and at < own_slabs:
            return jnp.where(near, early[0][at, part], 0.0 if len(zs) == 1 else early[1][at, part])
        at = base[1] + at - (own_slabs if early else 0)
        return jnp.where(near, zs[0][at, part], 0.0 if len(zs) == 1 else zs[1][at, part])

    for f in range(fields):
        for k in range(planes + len(xs) * width):
            deep = depth
            if k < planes:
                at, plane, slab = margin + k, own[f, k] if len(own.shape) == 4 else own[f * planes + k], group[0] + f * planes + k
            else:
                which, j = divmod(k - planes, width)
                up, down = margin + planes + j, margin - width + j
                at = jnp.where(even_x, up, down) if which == 0 else jnp.where(even_x, down, up)
                plane = xs[which][group[1] + f * width + j]
                slab = own_slabs + which * x_slabs + group[1] + f * width + j
                deep = corner or depth
            dst[f, at, 0:rows, 0:lanes] = plane
            dst[f, at, 0:rows, lanes:] = edge(slab, 0, rows)
            sides = []
            for n in range(pairs_y):
                at_z = slab_count + n * (-(-slab_count // per)) + slab // per
                if corner and k >= planes:
                    y = ys[pairs_y + n][base[0] + slab - own_slabs]
                else:
                    y = ys[n][slab]
                sides.append((y, edge(at_z, slab % per * PAD, deep)))
            if len(sides) == 1:
                sides.append([jnp.zeros_like(v) for v in sides[0]])
            for to, first, second in zip((slice(0, lanes), slice(lanes, lanes + LANES)), *sides):
                dst[f, at, rows:rows + deep, to] = jnp.where(even_y, first, second)
                dst[f, at, total - deep:total, to] = jnp.where(even_y, second, first)
            gap = total - rows - 2 * deep
            if gap:
                dst[f, at, rows + deep:total - deep, :] = jnp.zeros((gap, dst.shape[3]), jnp.float32)


def place_outer(out, state, got, flags, before):
    xs, ys, zs = got
    fields, near, total, wide = state.shape
    planes, rows, lanes = near - 2 * STATE_W, total - 8, wide - LANES
    even_x, even_y, even_z = flags[0] == 1, flags[1] == 1, flags[2] == 1
    side = (lax.broadcasted_iota(jnp.int32, (1, LANES), 1) < LANES // 2) == even_z
    tiles = [(r, z) for r in range(rows // 8) for z in range(lanes // LANES)]
    for f in range(fields):
        for k in range(planes + 2):
            p, slab = STATE_W - 1 + k, f * (planes + 2) + k
            out[f, p, :, 0:lanes] = state[f, p, :, 0:lanes]
            for r in range(total // 8):
                at = before[2] + slab * (total // 8) + r
                z = jnp.where(side, zs[0][at], 0.0 if len(zs) == 1 else zs[1][at])
                out[f, p, r * 8:(r + 1) * 8, lanes:] = z
            out_by = 1 if 0 < k <= planes else 0
            for z in range(lanes // LANES):
                at, row = before[1] + slab // 2, slab % 2 * 2 + z
                first = ys[0][at, row:row + 1]
                second = ys[1][at, row:row + 1] if len(ys) > 1 else jnp.zeros_like(first)
                to = slice(z * LANES, (z + 1) * LANES)
                out[f, p, rows + out_by:rows + out_by + 1, to] = jnp.where(even_y, first, second)
                out[f, p, total - 1 - out_by:total - out_by, to] = jnp.where(even_y, second, first)
        for p in (0, near - 1):
            out[f, p] = jnp.zeros((total, wide), jnp.float32)
            is_first = even_x if p else ~even_x
            for t, (r, z) in enumerate(tiles):
                at = before[0] + f * len(tiles) + t
                first = xs[0][at]
                second = xs[1][at] if len(xs) > 1 else jnp.zeros_like(first)
                out[f, p, r * 8:(r + 1) * 8, z * LANES:(z + 1) * LANES] = jnp.where(is_first, first, second)


def send_outer(state, flags, x_out, y_out, z_out, before):
    fields, near, total, wide = state.shape
    planes, rows, lanes = near - 2 * STATE_W, total - 8, wide - LANES
    up = [[(flags[a] == 1) == (n == 0) for n in range(2)] for a in range(3)]
    tiles = [(r, z) for r in range(rows // 8) for z in range(lanes // LANES)]
    for n, ref in enumerate(x_out):
        p = jnp.where(up[0][n], STATE_W + planes - 2, STATE_W + 1)
        for f in range(fields):
            for t, (r, z) in enumerate(tiles):
                ref[before + f * len(tiles) + t] = state[f, p, r * 8:(r + 1) * 8, z * LANES:(z + 1) * LANES]
    for f in range(fields):
        for k in range(planes + 2):
            p, slab = STATE_W - 1 + k, f * (planes + 2) + k
            out_by = 1 if 0 < k <= planes else 0
            for n, ref in enumerate(y_out):
                high = state[f, p, rows - 1 - out_by:rows - out_by, 0:lanes]
                v = jnp.where(up[1][n], high, state[f, p, out_by:out_by + 1, 0:lanes])
                for z in range(lanes // LANES):
                    row = slab % 2 * 2 + z
                    ref[slab // 2, row:row + 1] = v[:, z * LANES:(z + 1) * LANES]
            for n, ref in enumerate(z_out):
                for r in range(total // 8):
                    part = slice(r * 8, (r + 1) * 8)
                    v = jnp.where(up[2][n], state[f, p, part, lanes - LANES:lanes], state[f, p, part, 0:LANES])
                    ref[slab * (total // 8) + r] = v


def inside(flags, rows, lanes, total, depth):
    row = lax.broadcasted_iota(jnp.int32, (total, lanes + LANES), 0)
    lane = lax.broadcasted_iota(jnp.int32, (total, lanes + LANES), 1)
    end = lanes + LANES
    row_ok = (row < rows) | ((row < rows + depth) & (flags[5] == 1)) | ((row >= total - depth) & (flags[6] == 1))
    lane_ok = (lane < lanes) | ((lane < lanes + depth) & (flags[7] == 1)) | ((lane >= end - depth) & (flags[8] == 1))
    return jnp.where(row_ok & lane_ok, 1.0, 0.0)


def plane_inside(flags, p, margin, planes):
    return jnp.where(p < margin, flags[4], jnp.where(p >= margin + planes, flags[3], 1)).astype(jnp.float32)


def put(ref, at, v, margin, planes, rows, lanes, reach):
    p = at[-1]
    reach = reach - max(margin - p, p - margin - planes + 1, 0)
    if reach >= 2:
        ref[at] = v
        return
    ends = v.shape
    ref[(*at, slice(0, rows), slice(0, lanes))] = v[0:rows, 0:lanes]
    for r, z in ((slice(0, rows), slice(lanes, ends[1])), (slice(rows, ends[0]), slice(0, lanes))):
        ref[(*at, r, z)] = v[r, z] if reach == 1 else jnp.zeros((r.stop - r.start, z.stop - z.start), jnp.float32)
    ref[(*at, slice(rows, ends[0]), slice(lanes, ends[1]))] = jnp.zeros((ends[0] - rows, ends[1] - lanes), jnp.float32)


def neighbours(ref, p):
    rows, lanes = ref.shape[2], ref.shape[3]
    sums, grads, spread = [], [], 0.0
    for f in range(4):
        c, xn, xp = ref[f, p], ref[f, p + 1], ref[f, p - 1]
        yn, yp = pltpu.roll(c, rows - 1, 0), pltpu.roll(c, 1, 0)
        zn, zp = pltpu.roll(c, lanes - 1, 1), pltpu.roll(c, 1, 1)
        sums.append((xn + xp) + (yn + yp) + (zn + zp))
        if f == 3:
            grads = [xn - xp, yn - yp, zn - zp]
        else:
            spread = spread + (xn - xp, yn - yp, zn - zp)[f]
    return sums, grads + [spread]


def pack_kernel(tile_ref, mask_ref, out_ref, used_ref, rows_ref, *, capacity):
    tiles = out_ref.shape[0]
    count, width = mask_ref.shape
    out_ref[...] = jnp.zeros(out_ref.shape, jnp.float32)
    for r in range(0, count, 8):
        rows_ref[r:r + 8] = mask_ref[r:r + 8].reshape(8, width // LANES, LANES)

    def clear(t, _):
        used_ref[t] = 0
        return 0

    lax.fori_loop(0, tiles, clear, 0, unroll=8)

    def row(r, _):
        t = tile_ref[r]
        n = used_ref[t]
        used_ref[t] = n + 1
        out_ref[t, jnp.minimum(n, capacity - 1)] = rows_ref[r]
        return 0

    lax.fori_loop(0, count, row, 0, unroll=32)


def split(refs, nums):
    at, got = 0, []
    for n in nums:
        got.append(refs[at:at + n])
        at += n
    return got, refs[at:]


def chi_kernel(slot_ref, rows_ref, out, coarse_out, acc, pooled):
    _, planes, rows, lanes = out.shape
    acc[...] = jnp.zeros(acc.shape, jnp.float32)
    per = rows_ref.shape[1]

    def add(s, _):
        for c in range(per):
            at = pl.ds(pl.multiple_of(slot_ref[s * per + c] * 8, 8), 8)
            acc[at, :] = acc[at, :] + rows_ref[s, c]
        return 0

    lax.fori_loop(0, rows_ref.shape[0], add, 0, unroll=4)
    z_tiles = lanes // LANES
    across = rows // 2
    for qx in range(planes // 2):
        for zt in range(z_tiles):
            total = None
            for i in range(2):
                for j in range(2):
                    v = acc[pl.ds(qx * across * 8 + (2 * i + j) * z_tiles + zt, across, stride=8), :]
                    pooled[zt, pl.ds(j, across, stride=2), :] = v
                    total = v if total is None else total + v
                out[0, 2 * qx + i, :, zt * LANES:(zt + 1) * LANES] = pooled[zt]
            coarse_out[qx, :, zt * LANES:(zt + 1) * LANES] = total


def side(up, v, dim, width):
    size = v.shape[dim]
    low = v[..., 0:width] if dim == 1 else v[0:width]
    high = v[..., size - width:] if dim == 1 else v[size - width:]
    return jnp.where(up, high, low)


def y_kernel(flags, *refs, take, order, added):
    ready, (_, *outs) = split(refs[len(take):], [added])
    for n, out in enumerate(outs):
        up = (flags[1] == 1) == (n == 0)
        at = 0
        for i in order:
            ref, count = refs[i], take[i]
            for s in range(count):
                out[at] = side(up, ref[s], 0, out.shape[1])
                at += 1
        if added:
            out[at:] = ready[0][n][...]


def z_kernel(flags, *refs, plan, count, added):
    ready, outs = split(refs[count:], [added])
    for n, out in enumerate(outs):
        up = (flags[2] == 1) == (n == 0)
        per = out.shape[1] // PAD
        at = 0
        for slabs, edges in plan:
            for i, low, high in slabs:
                for s in range(low, high):
                    out[at] = side(up, refs[i][s], 1, LANES)
                    at += 1
            for parts in edges:
                k = 0
                for i, low, high in parts:
                    for s in range(low, high):
                        depth = refs[i].shape[1]
                        row = k % per * PAD
                        out[at + k // per, row:row + depth] = side(up, refs[i][s], 1, LANES)
                        if depth < PAD:
                            out[at + k // per, row + depth:row + PAD] = jnp.zeros((PAD - depth, LANES), jnp.float32)
                        k += 1
                while k % per:
                    row = k % per * PAD
                    out[at + k // per, row:row + PAD] = jnp.zeros((PAD, LANES), jnp.float32)
                    k += 1
                at += k // per
        if added:
            out[at:] = ready[0][n][...]


def second_kernel(flags, own, pooled_chi, right_side, start_field, *refs, nums):
    n_x, n_y, n_z = nums
    (chi_x, first_x, first_y, first_z, far_y, far_z), refs = split(refs, [n_x, n_x, n_y, n_z, n_y, n_z])
    rhs, state_out, weight_out = refs[:3]
    (x_out, y_out, z_out), (chi, start, ext, tmp, pooled) = split(refs[3:], nums)
    _, planes, rows, lanes = own.shape
    total = ext.shape[2]
    chi_slabs = planes + n_x * FINE_W
    base = (chi_slabs, chi_slabs + n_y * -(-chi_slabs // (rows // PAD)))
    slabs = (8 * planes, 4 * (START_W + FINE_W))
    fields_got = (first_x, (*first_y, *far_y), far_z)
    place_halo(chi, FINE_W, own, (chi_x, far_y, far_z), flags, FINE_W, FINE_W)
    place_halo(start, START_W, start_field, fields_got, flags, START_W, START_W, (0, 0), slabs, CORNER, base, first_z)
    place_halo(rhs, FINE_W, right_side, fields_got, flags, FINE_W, START_W, (4 * planes, 4 * START_W), slabs, CORNER, base, first_z)
    mask = inside(flags, rows, lanes, total, FINE_W)
    w_p = (RELAX / (SHIFT + 6.0)) * mask

    for k in range(planes + 2 * FINE_W):
        here = plane_inside(flags, k, FINE_W, planes)
        w_u = (RELAX / (SHIFT + 6.0 + chi[0, k])) * (mask * here)
        put(weight_out, (k,), w_u, FINE_W, planes, rows, lanes, FINE_W)
        sums, grads = neighbours(start, k + START_W - FINE_W)
        for f in range(4):
            w = w_u if f < 3 else w_p * here
            v = KEEP * start[f, k + START_W - FINE_W] + w * (rhs[f, k] + sums[f] - 0.5 * grads[f])
            put(ext, (f, k), v, FINE_W, planes, rows, lanes, FINE_W)

    for p in range(1, planes + 2 * FINE_W - 1):
        here = plane_inside(flags, p, FINE_W, planes)
        sums, grads = neighbours(ext, p)
        w_u = weight_out[p]
        for f in range(4):
            w = w_u if f < 3 else w_p * here
            v = KEEP * ext[f, p] + w * (rhs[f, p] + sums[f] - 0.5 * grads[f])
            put(state_out, (f, p), v, FINE_W, planes, rows, lanes, FINE_W - 1)

    for cx in range(planes // 2):
        both = [None] * 4
        for i in range(2):
            p = FINE_W + 2 * cx + i
            sums, grads = neighbours(state_out, p)
            for f in range(4):
                diag = SHIFT + 6.0 + (chi[0, p] if f < 3 else 0.0)
                r = rhs[f, p] + sums[f] - 0.5 * grads[f] - diag * state_out[f, p]
                both[f] = r if i == 0 else both[f] + r
        for f in range(4):
            for zt in range(lanes // LANES):
                tmp[f, zt] = both[f][0:rows, zt * LANES:(zt + 1) * LANES]
                v = tmp[f, zt, pl.ds(0, rows // 2, stride=2), :] + tmp[f, zt, pl.ds(1, rows // 2, stride=2), :]
                pooled[f, cx, :, zt * LANES:(zt + 1) * LANES] = v
    pooled[4] = pooled_chi[...]
    lane = lax.broadcasted_iota(jnp.int32, (lanes, lanes // 2), 0)
    cell = lax.broadcasted_iota(jnp.int32, (lanes, lanes // 2), 1)
    gather = jnp.where(lane // 2 == cell, 0.125, 0.0)
    flat_rows = pooled[...].reshape(5 * planes // 2 * rows // 2, lanes)
    coarse = jnp.dot(flat_rows, gather, precision=HIGHEST, preferred_element_type=jnp.float32)
    coarse = coarse.reshape(5 * planes // 2, rows // 2, lanes // 2)
    for ref in x_out:
        ref[0:coarse.shape[0]] = coarse
    send_outer(state_out, flags, x_out, y_out, z_out, coarse.shape[0])


def last_kernel(flags, own, state, weight, rhs, *refs, nums):
    got, (out, ext, one, two, fine, mid, tmp) = split(refs, nums)
    planes = ext.shape[1] - 2 * COARSE_W
    rows, lanes = own.shape[1:]
    total, wide = ext.shape[2], ext.shape[3]
    own = own.at[0:5 * planes]
    place_halo(ext, COARSE_W, own, got[:3], flags, COARSE_W, COARSE_W)
    x_slabs = 5 * COARSE_W
    slabs = 5 * planes + len(got[0]) * x_slabs
    z_slabs = slabs + len(got[1]) * -(-slabs // (rows // PAD))
    place_outer(fine, state, got, flags, (x_slabs, slabs, z_slabs))
    mask = inside(flags, rows, lanes, total, COARSE_W)
    w_p = (RELAX / (SHIFT + 1.5)) * mask

    for p in range(planes + 2 * COARSE_W):
        here = plane_inside(flags, p, COARSE_W, planes)
        w_u = (RELAX / (SHIFT + 1.5 + ext[4, p])) * (mask * here)
        ext[4, p] = w_u
        for f in range(4):
            one[f, p] = (w_u if f < 3 else w_p * here) * ext[f, p]
    now, then = one, two
    for s in range(1, COARSE_SWEEPS):
        for p in range(s, planes + 2 * COARSE_W - s):
            here = plane_inside(flags, p, COARSE_W, planes)
            sums, grads = neighbours(now, p)
            for f in range(4):
                w = ext[4, p] if f < 3 else w_p * here
                v = KEEP * now[f, p] + w * (ext[f, p] + 0.25 * (sums[f] - grads[f]))
                put(then, (f, p), v, COARSE_W, planes, rows, lanes, COARSE_W + 1 - s)
        now, then = then, now

    f_total, f_wide = fine.shape[2], fine.shape[3]
    f_rows, f_lanes = 2 * rows, 2 * lanes
    cell = lax.broadcasted_iota(jnp.int32, (wide, f_wide), 0)
    lane = lax.broadcasted_iota(jnp.int32, (wide, f_wide), 1)
    from_cell = jnp.where(lane < f_lanes + LANES // 2, lane // 2, wide - 1 - (f_wide - 1 - lane) // 2)
    spread = jnp.where(cell == from_cell, 1.0, 0.0)
    c_planes = planes + 2
    flat = now[:, COARSE_W - 1:COARSE_W - 1 + c_planes].reshape(4 * c_planes * total, wide)
    grown = jnp.dot(flat, spread, precision=HIGHEST, preferred_element_type=jnp.float32)
    for f in range(4):
        for cp in range(c_planes):
            lo = (f * c_planes + cp) * total
            for zt in range(f_wide // LANES):
                v = grown[lo:lo + total, zt * LANES:(zt + 1) * LANES]
                at = f * c_planes + cp
                for j in range(2):
                    tmp[zt, pl.ds(j, rows, stride=2), :] = v[0:rows]
                    tmp[zt, pl.ds(f_rows + j, 2, stride=2), :] = v[rows:rows + 2]
                    tmp[zt, pl.ds(f_total - 4 + j, 2, stride=2), :] = v[total - 2:total]
                for i in range(2):
                    to = slice(zt * LANES, (zt + 1) * LANES)
                    fine[f, 2 * cp + i, :, to] = fine[f, 2 * cp + i, :, to] + tmp[zt]
    f_planes = 2 * planes
    f_mask = inside(flags, f_rows, f_lanes, f_total, STATE_W)
    off = FINE_W - STATE_W
    w_q = (RELAX / (SHIFT + 6.0)) * f_mask

    for p in range(1, f_planes + 3):
        here = plane_inside(flags, p, STATE_W, f_planes)
        sums, grads = neighbours(fine, p)
        for f in range(4):
            w = weight[p + off] if f < 3 else w_q * here
            v = KEEP * fine[f, p] + w * (rhs[f, p + off] + sums[f] - 0.5 * grads[f])
            put(mid, (f, p), v, STATE_W, f_planes, f_rows, f_lanes, 1)

    for k in range(f_planes):
        p = k + 2
        sums, grads = neighbours(mid, p)
        for f in range(4):
            w = weight[p + off] if f < 3 else w_q
            v = KEEP * mid[f, p] + w * (rhs[f, p + off] + sums[f] - 0.5 * grads[f])
            out[f, k] = v[0:f_rows, 0:f_lanes]


def call(kernel, shapes, scratch, *args, smem=1):
    outs = [jax.ShapeDtypeStruct(s, jnp.float32) for s in shapes]
    return pl.pallas_call(
        kernel,
        out_shape=outs,
        in_specs=[SMEM] * smem + [VMEM] * (len(args) - smem),
        out_specs=[VMEM] * len(outs),
        scratch_shapes=scratch,
        compiler_params=PARAMS,
    )(*args)


def routes(block_tile, block_slot, tiles, count_l, per_device, capacity, slots):
    my_tile = lax.axis_index("gx") * lax.axis_size("gy") + lax.axis_index("gy")
    index_l = lax.axis_index("lvl")
    their_tiles = lax.dynamic_index_in_dim(block_tile.reshape(tiles, count_l, per_device), index_l, 1, keepdims=False)
    their_slots = lax.dynamic_index_in_dim(block_slot.reshape(tiles, count_l, per_device), index_l, 1, keepdims=False)
    arriving = their_tiles == my_tile
    counter = jnp.arange(per_device, dtype=jnp.int32)
    earlier = counter[None, :, None] < counter[None, None, :]
    order = jnp.sum(jnp.where(arriving[:, :, None] & earlier, 1, 0), axis=1)
    places = jnp.arange(capacity, dtype=jnp.int32)
    hit = arriving[:, None, :] & (order[:, None, :] == places[None, :, None])
    slot = jnp.sum(jnp.where(hit, their_slots[:, None, :] - slots, 0), axis=2) + slots
    return slot.reshape(-1)


def body(right_side, start_field, mask_blocks, block_tile, block_slot):
    axes = ("gx", "gy", "lvl")
    counts = [lax.axis_size(a) for a in axes]
    index = [lax.axis_index(a) for a in axes]
    tiles = counts[0] * counts[1]
    per_device, width = mask_blocks.shape
    capacity = max(2, 2 * per_device // tiles)
    _, planes, rows, lanes = right_side.shape
    slots = planes // 2 * (rows // 2)
    c_planes, c_rows, c_lanes = planes // 2, rows // 2, lanes // 2
    flags = [i % 2 == 0 for i in index]
    for i, n in zip(index, counts):
        flags += [i < n - 1, i > 0]
    flags = jnp.stack(flags).astype(jnp.int32)

    my_flat = (index[0] * counts[1] + index[1]) * counts[2] + index[2]
    tile_ids = block_tile[:, 0]
    my_tiles = lax.dynamic_slice_in_dim(tile_ids, my_flat * per_device, per_device)
    (outgoing,) = call(
        functools.partial(pack_kernel, capacity=capacity),
        [(tiles, capacity, width // LANES, LANES)],
        [pltpu.SMEM((tiles,), jnp.int32), pltpu.VMEM((per_device, width // LANES, LANES), jnp.float32)],
        my_tiles, mask_blocks,
    )
    outgoing, right_side, start_field = lax.optimization_barrier((outgoing, right_side, start_field))
    arrived = lax.all_to_all(outgoing, ("gx", "gy"), split_axis=0, concat_axis=0, tiled=True)
    slot_of = routes(tile_ids, block_slot, tiles, counts[2], per_device, capacity, slots)

    total, wide = rows + 8, lanes + LANES
    near, far = planes + 2 * STATE_W, planes + 2 * FINE_W
    pair_counts = [1 + (n > 2) for n in counts]
    groups = [(start_field, START_W), (right_side, FINE_W)]
    first_x = halo_x(groups)
    first_y = swap("gy", lambda up, n: flat([cut(v, 2, START_W, up) for v, _ in groups]))
    first_z = swap("lvl", lambda up, n: flat([cut(v, 3, LANES, up) for v, _ in groups]))
    first_y, first_z, slot_of = lax.optimization_barrier((first_y, first_z, slot_of))
    chi, pooled_chi = call(
        chi_kernel,
        [(1, planes, rows, lanes), (c_planes, c_rows, lanes)],
        [pltpu.VMEM(((slots + 1) * 8, LANES), jnp.float32), pltpu.VMEM((lanes // LANES, rows, LANES), jnp.float32)],
        slot_of, arrived,
    )
    group = [(chi, FINE_W)]
    chi_x = halo_x(group)
    first_x, chi_x = lax.optimization_barrier((first_x, chi_x))
    slabs = lambda v: v.reshape(-1, rows, lanes)
    far_x = len(first_x) * 4 * (START_W + FINE_W)
    chi_slabs = planes + len(chi_x) * FINE_W
    n_x, n_y, n_z = pair_counts
    y_sent = call(
        functools.partial(
            y_kernel,
            take=[planes, *[x.shape[0] for x in (*chi_x[::-1], *first_x[::-1])]],
            order=[0, *range(n_x, 0, -1), *range(2 * n_x, n_x, -1)],
            added=0,
        ),
        [(chi_slabs + far_x, CORNER, lanes)] * n_y,
        [],
        flags, slabs(chi), *chi_x[::-1], *first_x[::-1], chi_x[0][0, :1, :LANES],
    )
    far_y = swap("gy", lambda up, n: y_sent[n])
    per = rows // PAD
    edges = -(-chi_slabs // per) + -(-(8 * planes + far_x) // per)
    whole = lambda first, refs: [(first + i, 0, r.shape[0]) for i, r in enumerate(refs)]
    far_at = 1 + 2 * n_x + n_y
    plan = [
        ([(0, 0, planes), *whole(1, chi_x)], [[(far_at + n, 0, chi_slabs)] for n in range(n_y)]),
        (
            whole(1 + n_x, first_x),
            [[(1 + 2 * n_x + n, 0, 8 * planes), (far_at + n, chi_slabs, chi_slabs + far_x)] for n in range(n_y)],
        ),
    ]
    z_sent = call(
        functools.partial(z_kernel, plan=plan, count=far_at + n_y, added=0),
        [(chi_slabs + far_x + n_y * edges, rows, LANES)] * n_z,
        [],
        flags, slabs(chi), *chi_x, *first_x, *first_y, *far_y,
    )
    far_z = swap("lvl", lambda up, n: z_sent[n])
    c_slabs, s_slabs = 5 * c_planes, 4 * (rows // 8) * (lanes // LANES)
    outers = [[(c_slabs + s_slabs, 8, LANES)], [(4 * (planes + 2) // 2, PAD, LANES)], [(4 * (planes + 2) * total // 8, 8, LANES)]]
    outers = [shape * n for shape, n in zip(outers, pair_counts)]
    rhs, state, weight, *sent = call(
        functools.partial(second_kernel, nums=pair_counts),
        [(4, far, total, wide), (4, near, total, wide), (far, total, wide), *sum(outers, [])],
        [
            pltpu.VMEM((1, far, total, wide), jnp.float32),
            pltpu.VMEM((4, planes + 2 * START_W, total, wide), jnp.float32),
            pltpu.VMEM((4, far, total, wide), jnp.float32),
            pltpu.VMEM((4, lanes // LANES, rows, LANES), jnp.float32),
            pltpu.VMEM((5, c_planes, c_rows, lanes), jnp.float32),
        ],
        flags, chi, pooled_chi, right_side, start_field, *chi_x, *first_x, *first_y, *first_z, *far_y, *far_z,
    )
    (x_out, y_out, z_out), _ = split(sent, pair_counts)
    last_x = swap("gx", lambda up, n: x_out[n])
    take = [c_slabs, *[5 * COARSE_W] * n_x]
    y_sent = call(
        functools.partial(y_kernel, take=take, order=[0, *range(n_x, 0, -1)], added=n_y),
        [(sum(take) + y_out[0].shape[0], COARSE_W, c_lanes)] * n_y,
        [],
        flags, x_out[0], *last_x[::-1], *y_out, last_x[0][0, :1, :LANES],
    )
    last_y = swap("gy", lambda up, n: y_sent[n])
    plan = [([(i, 0, t) for i, t in enumerate(take)], [[(1 + n_x + n, 0, sum(take))] for n in range(n_y)])]
    z_slabs = sum(take) + n_y * -(-sum(take) // (c_rows // PAD))
    z_sent = call(
        functools.partial(z_kernel, plan=plan, count=1 + n_x + n_y, added=n_z),
        [(z_slabs + z_out[0].shape[0], c_rows, LANES)] * n_z,
        [],
        flags, x_out[0], *last_x, *last_y, *z_out,
    )
    last_z = swap("lvl", lambda up, n: z_sent[n])
    c_ext = (c_planes + 2 * COARSE_W, c_rows + 8, c_lanes + LANES)
    (out,) = call(
        functools.partial(last_kernel, nums=pair_counts),
        [right_side.shape],
        [
            pltpu.VMEM((5, *c_ext), jnp.float32),
            pltpu.VMEM((4, *c_ext), jnp.float32),
            pltpu.VMEM((4, *c_ext), jnp.float32),
            pltpu.VMEM((4, near, total, wide), jnp.float32),
            pltpu.VMEM((4, near, total, wide), jnp.float32),
            pltpu.VMEM((wide // LANES, total, LANES), jnp.float32),
        ],
        flags, x_out[0], state, weight, rhs, *last_x, *last_y, *last_z,
    )
    return out


def solution(mesh):
    in_specs = (
        P(None, "gx", "gy", "lvl"),
        P(None, "gx", "gy", "lvl"),
        P(("gx", "gy", "lvl"), None),
        P(),
        P(),
    )
    out_specs = P(None, "gx", "gy", "lvl")
    return jax.shard_map(body, mesh=mesh, in_specs=in_specs, out_specs=out_specs, check_vma=False)
```
